256 devices in a mesh: seq: 8 (over z_hi, core), req: 32 (over x, z_lo, y).
Axes of the slice: x: 4, y: 4, z: 8 (z_hi: 4, z_lo: 2; z = z_hi * 2 + z_lo), core: 2. Of those that a mesh axis runs over, the one named last changes fastest.
Arguments:
- inputs: bfloat16 [32, 16, 4, 1536], P('req', 'seq'), may hold values from -6 to 6
- parents: int32 [32, 4, 16], P('req'), may hold values from 0 to 15
- block_len: int32 [32, 128], P('req', 'seq'), may hold values from 0 to 128, as said below
- prompt_key_cache: bfloat16 [32, 16384, 512], P('req', 'seq'), may hold values from -230 to 230
- prompt_value_cache: bfloat16 [32, 16384, 512], P('req', 'seq'), may hold values from -6 to 6
- generated_key_cache: bfloat16 [32, 16, 16, 512], P('req', 'seq'), may hold values from -6 to 6
- generated_value_cache: bfloat16 [32, 16, 16, 512], P('req', 'seq'), may hold values from -6 to 6
- gain_attn: float32 [1536], replicated, may hold values from 0.1 to 1.9
- gain_moe: float32 [1536], replicated, may hold values from 0.1 to 1.9
- w_query: bfloat16 [1536, 1536], P(None, 'seq'), may hold values from -0.15625 to 0.15625
- key_projection_weight: bfloat16 [1536, 512], P(None, 'seq'), may hold values from -0.15625 to 0.15625
- value_projection_weight: bfloat16 [1536, 512], P(None, 'seq'), may hold values from -0.15625 to 0.15625
- w_output: bfloat16 [1536, 1536], P('seq'), may hold values from -0.15625 to 0.15625
- w_in: bfloat16 [32, 1536, 1024], P('req'), may hold values from -0.15625 to 0.15625
- w_out: bfloat16 [32, 512, 1536], P('req'), may hold values from -0.25 to 0.25
- routes: int32 [32, 16, 4, 8], P('req', 'seq'), may hold values from 0 to 31, all different within a row; in each aligned block of 8 rows (0 to 7, 8 to 15, ..., all dimensions but the last counted through in order) at most 4 rows name the same one
- gate_weights: float32 [32, 16, 4, 8], P('req', 'seq'), may hold values from 0.05 to 1
Outputs:
- mixed: bfloat16 [32, 16, 4, 1536], P('req', 'seq')
- final_k: bfloat16 [32, 16, 20, 512], P('req', 'seq')
- final_v: bfloat16 [32, 16, 20, 512], P('req', 'seq')
The draws below stay inside these ranges and needn't reach their ends.
Inputs may be any that keep to these rules, and one draw needn't show every extreme that they name: block_len[r, j] is the number of live positions at the start of block j of request r; 0 marks an empty block; the first block of every request is full. `routes`: among the rows of one device (its 2 beams over all 4 steps, in the order beam then step) no expert is named more than 4 times.
All inputs are finite; a program needn't handle non-finite values.
Results may differ from the reference program's by a relative error of at most 0.025.
Values may be sent and summed in bfloat16 or wider, within the bound.
No kernel may reach another device: no remote copies, remote signals or barrier semaphores. Data moves between devices by JAX's collectives and lax.ppermute only.
A program may use at most 128 MiB of HBM per device.

```python
import math
import jax
import jax.numpy as jnp
import numpy as np
from jax import lax

MODEL_DIMENSION = 1536
QUERY_HEADS = 24
KEY_VALUE_HEADS = 8
HEAD_SIZE = 64
FFE = 512
TOP = 8
EXPERTS = 32
BEAMS_PER_REQUEST = 16
DECODE_STEPS = 4
BLK = 128
TAIL_TOKENS = 16
REQUEST_COUNT = 32
PROMPT_POSITIONS = 16384
NBLK = 128
BEAM_DEV = 2
MOST = 4


def draw_block_len(key, part):
    key_len = jax.random.fold_in(key, 11)
    key_gap = jax.random.fold_in(key, 12)
    lengths = jax.random.randint(key_len, (REQUEST_COUNT, NBLK), 1, BLK + 1)
    chance = jax.random.randint(key_gap, (REQUEST_COUNT, NBLK), 0, 100)
    column = jnp.arange(NBLK, dtype=jnp.int32)[None, :]
    limit = 75 * column // NBLK
    lengths = jnp.where(chance < limit, 0, lengths)
    lengths = jnp.where(column == 0, BLK, lengths)
    return lengths.astype(jnp.int32)


def draw_prompt_key_cache(key, part):
    feature_width = KEY_VALUE_HEADS * HEAD_SIZE
    base = 2.5 * jnp.clip(jax.random.normal(jax.random.fold_in(key, 21), (REQUEST_COUNT, PROMPT_POSITIONS, feature_width), jnp.float32), -6.0, 6.0)
    return base.astype(jnp.bfloat16)


def set_ends(values, own_key, smallest, largest):
    longest = values.shape.index(max(values.shape))
    spots = []
    for shift in (0, 1):
        where = [jax.random.randint(jax.random.fold_in(own_key, axis), (), 0, length) for axis, length in enumerate(values.shape)]
        where[longest] = (where[longest] + shift) % values.shape[longest]
        spots.append(tuple(where))
    return values.at[spots[0]].set(smallest).at[spots[1]].set(largest)


def level_of(own_key, extent, cuts, least, largest):
    loudness, own = 1.0, jax.random.fold_in(own_key, 6)
    for dim, shards_of in cuts:
        draws = jnp.exp(jax.random.uniform(jax.random.fold_in(own, dim), (shards_of,), jnp.float32, least / len(cuts), largest / len(cuts)))
        loudness = loudness * jnp.repeat(draws, extent[dim] // shards_of).reshape([-1 if axis == dim else 1 for axis in range(len(extent))])
    return loudness


def shared_out(rng, own, number, rows, count, top, most, skew):
    ranking = jax.random.permutation(rng, count)
    crowded, usual = load_shares(count, rows * top, most, skew, True), load_shares(count, rows * top, most, skew, False)
    places = jnp.arange(count)

    def named(sizes, rotation):
        used = int((sizes > 0).sum())
        fixed = max(1, used // 4)
        shifted = fixed + (places - fixed + rotation * (used - fixed)) % max(1, count - fixed)
        return jnp.zeros((count,), jnp.int32).at[ranking[jnp.where(places < fixed, places, shifted)]].set(jnp.asarray(sizes, jnp.int32))

    sizes = jnp.where(number % 4 == 0, named(crowded, number // 4), named(usual, number - number // 4 - 1))
    mixed = jax.random.permutation(jax.random.fold_in(own, 3), count)
    giver, receiver = mixed[0:count // 2 * 2:2], mixed[1:count // 2 * 2:2]
    room = jnp.minimum(sizes[giver] - 1, most - sizes[receiver]) // 2
    room = jnp.where((giver == ranking[0]) | (receiver == ranking[0]) | (sizes[receiver] == 0), 0, jnp.maximum(room, 0))
    shifted = jax.random.randint(jax.random.fold_in(own, 4), (count // 2,), 0, 1 << 20) % (room + 1)
    sizes = sizes.at[giver].add(-shifted).at[receiver].add(shifted)
    members = jnp.searchsorted(jnp.cumsum(sizes), jnp.arange(rows * top), side="right").astype(jnp.int32)
    table = members.reshape(top, rows).T
    table = table[jax.random.permutation(jax.random.fold_in(own, 1), rows)]
    rotation = jax.random.randint(jax.random.fold_in(own, 2), (rows, 1), 0, top)
    return jnp.take_along_axis(table, (jnp.arange(top)[None, :] + rotation) % top, axis=1)


def load_shares(number_of, total, most, skew, full):
    loads = [(1 << 20) // math.isqrt(rank ** skew) + 1 for rank in range(1, number_of + 1)]
    largest = most if full else min(most, max(-(-total // number_of), total * loads[0] // sum(loads)))
    least = 1 if total - largest >= number_of - 1 else 0
    given, rest = [largest] + [least] * (number_of - 1), total - largest - least * (number_of - 1)
    while rest > 0:
        free = [i for i in range(1, number_of) if given[i] < largest] or [i for i in range(1, number_of) if given[i] < most]
        pool, remaining = sum([loads[i] for i in free]), rest
        for i in free:
            extra = min(most - given[i], max(1, remaining * loads[i] // pool), rest)
            given[i] = given[i] + extra
            rest = rest - extra
    return np.array(given)


def scatter_about(stream_key, shape, scale, bound, shards=(), kind=jnp.bfloat16):
    result = jax.random.normal(stream_key, shape, jnp.float32) * scale
    if len(shards) > 0:
        result = level_of(stream_key, shape, shards, -0.22, 0.18) * result
    return jnp.clip(result, min=-bound, max=bound).astype(kind)


def setup_inputs(seed: int = 0) -> dict:
    splits = jax.random.split(jax.random.key(seed), 18)
    inputs = scatter_about(splits[0], (REQUEST_COUNT, BEAMS_PER_REQUEST, DECODE_STEPS, MODEL_DIMENSION), 1.0, 6.0, ((0, 32), (1, 8)))
    parents = set_ends(jax.random.randint(splits[1], (REQUEST_COUNT, DECODE_STEPS, BEAMS_PER_REQUEST), 0, BEAMS_PER_REQUEST), jax.random.fold_in(splits[1], 1), 0, BEAMS_PER_REQUEST - 1).astype(jnp.int32)
    block_len = draw_block_len(jax.random.fold_in(splits[17], 71), 0)
    prompt_key_cache = draw_prompt_key_cache(jax.random.fold_in(splits[17], 71), 0)
    prompt_value_cache = scatter_about(splits[4], (REQUEST_COUNT, PROMPT_POSITIONS, KEY_VALUE_HEADS * HEAD_SIZE), 1.0, 6.0, ((0, 32), (1, 8)))
    generated_key_cache = scatter_about(splits[5], (REQUEST_COUNT, BEAMS_PER_REQUEST, TAIL_TOKENS, KEY_VALUE_HEADS * HEAD_SIZE), 1.0, 6.0, ((0, 32), (1, 8)))
    generated_value_cache = scatter_about(splits[6], (REQUEST_COUNT, BEAMS_PER_REQUEST, TAIL_TOKENS, KEY_VALUE_HEADS * HEAD_SIZE), 1.0, 6.0, ((0, 32), (1, 8)))
    gain_attn = jnp.clip(1.0 + 0.18 * jax.random.normal(splits[7], (MODEL_DIMENSION,), jnp.float32), 0.1, 1.9)
    gain_moe = jnp.clip(1.0 + 0.18 * jax.random.normal(splits[8], (MODEL_DIMENSION,), jnp.float32), 0.1, 1.9)
    w_query = scatter_about(splits[9], (MODEL_DIMENSION, QUERY_HEADS * HEAD_SIZE), MODEL_DIMENSION ** -0.5, 0.15625, ((1, 8),))
    key_projection_weight = scatter_about(splits[10], (MODEL_DIMENSION, KEY_VALUE_HEADS * HEAD_SIZE), MODEL_DIMENSION ** -0.5, 0.15625, ((1, 8),))
    value_projection_weight = scatter_about(splits[11], (MODEL_DIMENSION, KEY_VALUE_HEADS * HEAD_SIZE), MODEL_DIMENSION ** -0.5, 0.15625, ((1, 8),))
    w_output = scatter_about(splits[12], (QUERY_HEADS * HEAD_SIZE, MODEL_DIMENSION), (QUERY_HEADS * HEAD_SIZE) ** -0.5, 0.15625, ((0, 8),))
    w_in = scatter_about(splits[13], (EXPERTS, MODEL_DIMENSION, 2 * FFE), MODEL_DIMENSION ** -0.5, 0.15625, ((0, 32),))
    w_out = scatter_about(splits[14], (EXPERTS, FFE, MODEL_DIMENSION), FFE ** -0.5, 0.25, ((0, 32),))
    routes_keys = jax.random.split(jax.random.fold_in(splits[15], 1), REQUEST_COUNT * BEAMS_PER_REQUEST * DECODE_STEPS // (BEAM_DEV * DECODE_STEPS))
    routes_turns = jax.random.permutation(jax.random.fold_in(splits[15], 3), REQUEST_COUNT * BEAMS_PER_REQUEST * DECODE_STEPS // (BEAM_DEV * DECODE_STEPS))
    routes = jax.vmap(lambda own, number: shared_out(jax.random.fold_in(splits[15], 2), own, number, BEAM_DEV * DECODE_STEPS, EXPERTS, TOP, MOST, 2))(routes_keys, routes_turns).reshape((REQUEST_COUNT, BEAMS_PER_REQUEST, DECODE_STEPS, TOP))
    gate_weights = jnp.clip(jnp.exp(math.log(1.0) - 2.9957323 * jax.random.uniform(splits[16], (REQUEST_COUNT, BEAMS_PER_REQUEST, DECODE_STEPS, TOP), jnp.float32) ** level_of(splits[16], (REQUEST_COUNT, BEAMS_PER_REQUEST, DECODE_STEPS, TOP), ((0, 32), (1, 8)), -0.2, 0.2)), 0.05, 1.0)
    return {"inputs": inputs, "parents": parents, "block_len": block_len, "prompt_key_cache": prompt_key_cache, "prompt_value_cache": prompt_value_cache, "generated_key_cache": generated_key_cache, "generated_value_cache": generated_value_cache, "gain_attn": gain_attn, "gain_moe": gain_moe, "w_query": w_query, "key_projection_weight": key_projection_weight, "value_projection_weight": value_projection_weight, "w_output": w_output, "w_in": w_in, "w_out": w_out, "routes": routes, "gate_weights": gate_weights}


EPSILON = 1e-05
ROPE_BASE = 10000.0
NEGATIVE_FILL = -1e+30
SCORE_SCALE = 0.125

def rms_scale(values, gain_vector):
    values = values.astype(jnp.float32)
    mean_sq = lax.optimization_barrier(jnp.mean(values * values, axis=-1, keepdims=True))
    return values * lax.rsqrt(mean_sq + EPSILON) * gain_vector.astype(jnp.float32)

def apply_rotary(values, token_positions, head_dim):
    lead_shape = values.shape[:-1]
    head_count = values.shape[-1] // head_dim
    shaped = values.reshape(lead_shape + (head_count, head_dim))
    half_dim = head_dim // 2
    frequency = ROPE_BASE ** (-(jnp.arange(half_dim, dtype=jnp.float32) * 2.0 / head_dim))
    angles = token_positions[:, None] * frequency[None, :]
    cosine = jnp.cos(angles)[None, :, None, :]
    sine_part = jnp.sin(angles)[None, :, None, :]
    first_half = shaped[..., :half_dim]
    second = shaped[..., half_dim:]
    turned = jnp.concatenate([first_half * cosine - second * sine_part, second * cosine + first_half * sine_part], axis=-1)
    return turned.reshape(values.shape)

def rounded(values):
    return lax.optimization_barrier(values.astype(jnp.bfloat16)).astype(jnp.float32)

def attend_request(packed, gain_attn, w_query, key_projection_weight, value_projection_weight, w_output):
    inputs, parents, block_len, prompt_key_cache, prompt_value_cache, generated_key_cache, generated_value_cache = packed
    normed = rms_scale(inputs, gain_attn).astype(jnp.bfloat16)
    flattened_rows = normed.reshape(BEAMS_PER_REQUEST * DECODE_STEPS, MODEL_DIMENSION)
    token_positions = jnp.arange(DECODE_STEPS, dtype=jnp.float32) + (PROMPT_POSITIONS + TAIL_TOKENS)
    query_rows = apply_rotary(jnp.dot(flattened_rows, w_query, preferred_element_type=jnp.float32).reshape(BEAMS_PER_REQUEST, DECODE_STEPS, QUERY_HEADS * HEAD_SIZE), token_positions, HEAD_SIZE).astype(jnp.bfloat16)
    updated_keys = apply_rotary(jnp.dot(flattened_rows, key_projection_weight, preferred_element_type=jnp.float32).reshape(BEAMS_PER_REQUEST, DECODE_STEPS, KEY_VALUE_HEADS * HEAD_SIZE), token_positions, HEAD_SIZE).astype(jnp.bfloat16)
    updated_values = jnp.dot(flattened_rows, value_projection_weight, preferred_element_type=jnp.float32).reshape(BEAMS_PER_REQUEST, DECODE_STEPS, KEY_VALUE_HEADS * HEAD_SIZE).astype(jnp.bfloat16)
    prefix_live = (jnp.arange(BLK, dtype=jnp.int32)[None, :] < block_len[:, None]).reshape(PROMPT_POSITIONS)
    prompt_key_rows = prompt_key_cache.reshape(PROMPT_POSITIONS, KEY_VALUE_HEADS, HEAD_SIZE).astype(jnp.float32)
    prompt_value_rows = prompt_value_cache.reshape(PROMPT_POSITIONS, KEY_VALUE_HEADS, HEAD_SIZE).astype(jnp.float32)
    beam_key_cache = generated_key_cache
    beam_value_cache = generated_value_cache
    newest_key = jnp.zeros((BEAMS_PER_REQUEST, DECODE_STEPS, KEY_VALUE_HEADS * HEAD_SIZE), jnp.bfloat16)
    newest_value = jnp.zeros((BEAMS_PER_REQUEST, DECODE_STEPS, KEY_VALUE_HEADS * HEAD_SIZE), jnp.bfloat16)
    outputs = []
    for decode_step_index in range(DECODE_STEPS):
        chosen = parents[decode_step_index]
        beam_key_cache = jnp.take(beam_key_cache, chosen, axis=0)
        beam_value_cache = jnp.take(beam_value_cache, chosen, axis=0)
        newest_key = jnp.take(newest_key, chosen, axis=0).at[:, decode_step_index].set(updated_keys[:, decode_step_index])
        newest_value = jnp.take(newest_value, chosen, axis=0).at[:, decode_step_index].set(updated_values[:, decode_step_index])
        decode_query_step = query_rows[:, decode_step_index].reshape(BEAMS_PER_REQUEST, KEY_VALUE_HEADS, QUERY_HEADS // KEY_VALUE_HEADS, HEAD_SIZE).astype(jnp.float32)
        prefix_scores = jnp.einsum('bgjd,kgd->bgjk', decode_query_step, prompt_key_rows) * SCORE_SCALE
        prefix_mask = prefix_live[None, None, None, :]
        prefix_scores = jnp.where(prefix_mask, prefix_scores, NEGATIVE_FILL)
        beam_key_rows = jnp.concatenate([beam_key_cache, newest_key], axis=1).reshape(BEAMS_PER_REQUEST, TAIL_TOKENS + DECODE_STEPS, KEY_VALUE_HEADS, HEAD_SIZE).astype(jnp.float32)
        beam_value_rows = jnp.concatenate([beam_value_cache, newest_value], axis=1).reshape(BEAMS_PER_REQUEST, TAIL_TOKENS + DECODE_STEPS, KEY_VALUE_HEADS, HEAD_SIZE).astype(jnp.float32)
        own_mask = (jnp.arange(TAIL_TOKENS + DECODE_STEPS, dtype=jnp.int32) <= TAIL_TOKENS + decode_step_index)[None, None, None, :]
        own_scores = jnp.einsum('bgjd,bkgd->bgjk', decode_query_step, beam_key_rows) * SCORE_SCALE
        own_scores = jnp.where(own_mask, own_scores, NEGATIVE_FILL)
        row_max = jnp.maximum(lax.optimization_barrier(jnp.max(prefix_scores, axis=-1)), lax.optimization_barrier(jnp.max(own_scores, axis=-1)))[..., None]
        prefix_weights = jnp.where(prefix_mask, jnp.exp(prefix_scores - row_max), 0.0)
        own_weights = jnp.where(own_mask, jnp.exp(own_scores - row_max), 0.0)
        denominator = lax.optimization_barrier(jnp.sum(prefix_weights, axis=-1)) + lax.optimization_barrier(jnp.sum(own_weights, axis=-1))
        numerator = jnp.einsum('bgjk,kgd->bgjd', rounded(prefix_weights), prompt_value_rows)
        numerator = numerator + jnp.einsum('bgjk,bkgd->bgjd', rounded(own_weights), beam_value_rows)
        attended_heads = (numerator / denominator[..., None]).reshape(BEAMS_PER_REQUEST, QUERY_HEADS * HEAD_SIZE).astype(jnp.bfloat16)
        projected = jnp.dot(attended_heads, w_output, preferred_element_type=jnp.float32)
        outputs.append(inputs[:, decode_step_index].astype(jnp.float32) + projected)
    hidden = jnp.stack(outputs, axis=1)
    return (hidden, jnp.concatenate([beam_key_cache, newest_key], axis=1), jnp.concatenate([beam_value_cache, newest_value], axis=1))

def reference(inputs, parents, block_len, prompt_key_cache, prompt_value_cache, generated_key_cache, generated_value_cache, gain_attn, gain_moe, w_query, key_projection_weight, value_projection_weight, w_output, w_in, w_out, routes, gate_weights):

    def per_request(packed):
        return attend_request(packed, gain_attn, w_query, key_projection_weight, value_projection_weight, w_output)
    hidden, final_k, final_v = lax.map(per_request, (inputs, parents, block_len, prompt_key_cache, prompt_value_cache, generated_key_cache, generated_value_cache))
    row_total = REQUEST_COUNT * BEAMS_PER_REQUEST * DECODE_STEPS
    flat_hidden = hidden.reshape(row_total, MODEL_DIMENSION)
    expert_in = rms_scale(flat_hidden, gain_moe).astype(jnp.bfloat16)
    chosen = routes.reshape(row_total * TOP).astype(jnp.int32)
    pair_gates = gate_weights.reshape(row_total * TOP)
    order = jnp.argsort(chosen, stable=True).astype(jnp.int32)
    expert_ids = jnp.arange(EXPERTS, dtype=jnp.int32)
    counts = lax.optimization_barrier(jnp.sum((chosen[None, :] == expert_ids[:, None]).astype(jnp.int32), axis=1)).astype(jnp.int32)
    starts = (jnp.cumsum(counts) - counts).astype(jnp.int32)
    pair_block = 256
    padded = jnp.concatenate([order, jnp.zeros((pair_block,), jnp.int32)])

    def per_expert(carried, expert_index):
        gate_up = w_in[expert_index]
        down_proj = w_out[expert_index]
        limit = counts[expert_index]
        anchor = starts[expert_index]

        def one_block(block_index, accum):
            offset = (block_index * pair_block).astype(jnp.int32)
            pair_ids = lax.dynamic_slice(padded, ((anchor + offset).astype(jnp.int32),), (pair_block,))
            live = offset + jnp.arange(pair_block, dtype=jnp.int32) < limit
            row_ids = (pair_ids // TOP).astype(jnp.int32)
            picked = jnp.take(expert_in, row_ids, axis=0)
            projected = jnp.dot(picked, gate_up, preferred_element_type=jnp.float32)
            activation = (jax.nn.silu(projected[:, :FFE]) * projected[:, FFE:]).astype(jnp.bfloat16)
            expert_out = rounded(jnp.dot(activation, down_proj, preferred_element_type=jnp.float32))
            scaled = jnp.where(live, jnp.take(pair_gates, pair_ids), 0.0)[:, None] * expert_out
            return accum.at[row_ids].add(scaled)
        trips = ((limit + pair_block - 1) // pair_block).astype(jnp.int32)
        return (lax.fori_loop(jnp.int32(0), trips, one_block, carried), None)
    summed, unused = lax.scan(per_expert, jnp.zeros((row_total, MODEL_DIMENSION), jnp.float32), expert_ids)
    mixed = (flat_hidden + summed).astype(jnp.bfloat16).reshape(REQUEST_COUNT, BEAMS_PER_REQUEST, DECODE_STEPS, MODEL_DIMENSION)
    return (mixed, final_k, final_v)
```

```python
import functools

import jax
import jax.numpy as jnp
import numpy as np
from jax import lax
from jax.experimental import pallas as pl
from jax.experimental.pallas import tpu as pltpu
from jax.sharding import PartitionSpec as P

HEAD = 64
BLK = 128
EPSILON = 1e-05
ROPE_BASE = 10000.0
FILL = -(2.0**100)
SCALE = 0.125
BF16 = jnp.bfloat16
F32 = jnp.float32


def whole():
    return pl.BlockSpec(memory_space=pltpu.VMEM)


def scalars():
    return pl.BlockSpec(memory_space=pltpu.SMEM)


def params(mib):
    return pltpu.CompilerParams(vmem_limit_bytes=mib << 20)


def dot(a, b):
    return jnp.dot(a, b, preferred_element_type=F32)


def dot_t(a, b):
    return lax.dot_general(a, b, (((1,), (1,)), ((), ())), preferred_element_type=F32)


def lanes(shape):
    return lax.broadcasted_iota(jnp.int32, shape, len(shape) - 1)


def norm(x, gain):
    mean_sq = jnp.mean(x * x, axis=-1, keepdims=True)
    return x * lax.rsqrt(mean_sq + EPSILON) * gain


def norm_kernel(x_ref, gain_ref, own_k_ref, own_v_ref, out_ref, own_ref):
    beams, steps = x_ref.shape[0], x_ref.shape[1]
    for b in range(beams):
        rows = norm(x_ref[b].astype(F32), gain_ref[...])
        out_ref[b * steps : (b + 1) * steps, :] = rows.astype(BF16)
    for d in range(own_ref.shape[0]):
        own_ref[d, 0] = own_k_ref[...]
        own_ref[d, 1] = own_v_ref[...]


def project_kernel(x_ref, wq_ref, wk_ref, wv_ref, cos_ref, sin_ref, out_ref):
    x = x_ref[...]
    rows = x.shape[0]
    q = dot(x, wq_ref[...]) * SCALE
    k = dot(x, wk_ref[...])
    v = dot(x, wv_ref[...])
    y = jnp.concatenate([q, k], axis=1)
    width = y.shape[1]
    half = HEAD // 2
    first = lanes(y.shape) % HEAD < half
    turned = jnp.where(first, pltpu.roll(y, width - half, 1), pltpu.roll(y, half, 1))
    y = (y * cos_ref[...] + turned * sin_ref[...]).astype(BF16)
    out_ref[0:rows, :] = y[:, 0:128]
    out_ref[rows : 2 * rows, :] = y[:, 128:256]
    out_ref[2 * rows : 2 * rows + rows // 2, :] = jnp.concatenate(
        [v[0 : rows // 2], v[rows // 2 :]], axis=1
    ).astype(BF16)


def lookup(parents_ref, step, cur, beams):
    found = jnp.zeros(cur.shape, jnp.int32)
    for b in range(beams):
        found = jnp.where(cur == b, parents_ref[step, b], found)
    return found


def attend_kernel(
    seq_ref,
    parents_ref,
    len_ref,
    qkv_ref,
    k_ref,
    v_ref,
    own_k_ref,
    own_v_ref,
    out_ref,
    fresh_k_ref,
    fresh_v_ref,
    s_ref,
    p_ref,
    bias_ref,
    extra_ref,
):
    steps, beams = parents_ref.shape
    rows = steps * beams
    keys = k_ref.shape[0]
    blocks = keys // BLK
    here = own_k_ref.shape[0]
    tail = own_k_ref.shape[1]
    own_keys = here * tail
    seq = seq_ref[0]
    shape = (rows, 128)
    lane = lanes(shape)
    low = lane < HEAD

    @pl.when(pl.program_id(0) == 0)
    def _():
        spot = lanes((8, BLK))
        for j in range(blocks):
            bias_ref[:, j * BLK : (j + 1) * BLK] = jnp.where(spot < len_ref[0, j], 0.0, FILL)
        row = lax.broadcasted_iota(jnp.int32, shape, 0)
        step = row % steps
        cur = row // steps
        fresh = lane - own_keys
        key_beam = fresh // steps
        key_step = fresh % steps
        live = jnp.zeros(shape, jnp.int32)
        for s in range(steps - 1, -1, -1):
            hit = (key_step == s) & (cur == key_beam) & (step >= s) & (key_beam // here == seq)
            live = live | jnp.where((fresh >= 0) & hit, 1, 0)
            cur = jnp.where(step >= s, lookup(parents_ref, s, cur, beams), cur)
        own_hit = (lane < own_keys) & (cur == seq * here + lane // tail)
        live = live | jnp.where(own_hit, 1, 0)
        extra_ref[...] = jnp.where(live > 0, 0.0, FILL)

    def swap(x):
        return pltpu.roll(x, HEAD, 1)

    parts = []
    fresh_k, fresh_v = [], []
    for c in range(2):
        t0 = qkv_ref[c, 0:rows, :].astype(F32)
        t1 = qkv_ref[c, rows : 2 * rows, :].astype(F32)
        tv = qkv_ref[c, 2 * rows : 2 * rows + rows // 2, :].astype(F32)
        keep = low if c == 0 else ~low
        for tile in (t0, swap(t0), t1) if c == 0 else (swap(t0), t0, swap(t1)):
            parts.append(jnp.where(keep, tile, 0.0).astype(BF16))
        fresh_k.append(t1)
        fresh_v.append(jnp.concatenate([tv, swap(tv)], axis=0))
    q = jnp.concatenate(parts, axis=0)
    new_k = jnp.where(low, swap(fresh_k[0]), fresh_k[1]).astype(BF16)
    new_v = jnp.where(low, fresh_v[0], swap(fresh_v[1])).astype(BF16)
    fill = jnp.zeros((128 - own_keys - rows, 128), BF16)
    extra_k = jnp.concatenate([own_k_ref[...].reshape(own_keys, 128), new_k, fill], axis=0)
    extra_v = jnp.concatenate([own_v_ref[...].reshape(own_keys, 128), new_v, fill], axis=0)

    pick_row = lax.broadcasted_iota(jnp.int32, (here * steps, rows), 0)
    pick_col = lanes((here * steps, rows))
    chosen = jnp.zeros(pick_row.shape, jnp.int32)
    for i in range(here):
        beam = seq * here + i
        for s in range(steps - 1, -1, -1):
            hit = (pick_row == i * steps + s) & (pick_col == beam * steps + s)
            chosen = chosen | jnp.where(hit, 1, 0)
            beam = parents_ref[s, beam]
    chosen = chosen.astype(F32).astype(BF16)
    fresh_k_ref[...] = dot(chosen, new_k).astype(BF16)
    fresh_v_ref[...] = dot(chosen, new_v).astype(BF16)

    s_ref[:, 0:keys] = dot_t(q, k_ref[...])
    s_ref[:, keys : keys + 128] = dot_t(q, extra_k)
    lse, total = [], []
    for i in range(6):
        span = slice(i * rows, (i + 1) * rows)
        s0 = s_ref[span, 0:keys] + bias_ref[0:1, :]
        s1 = s_ref[span, keys : keys + 128] + extra_ref[...]
        top = jnp.maximum(
            jnp.max(s0, axis=-1, keepdims=True), jnp.max(s1, axis=-1, keepdims=True)
        )
        e0 = jnp.exp(s0 - top)
        e1 = jnp.exp(s1 - top)
        p_ref[span, 0:keys] = e0.astype(BF16)
        p_ref[span, keys : keys + 128] = e1.astype(BF16)
        denominator = jnp.sum(e0, axis=-1, keepdims=True) + jnp.sum(e1, axis=-1, keepdims=True)
        total.append(denominator)
        lse.append(top + jnp.log(denominator))
    o = dot(p_ref[:, 0:keys], v_ref[...]) + dot(p_ref[:, keys : keys + 128], extra_v)
    for c in range(2):
        values = []
        stats = jnp.zeros(shape, F32)
        for j in range(3):
            i = 3 * c + j
            values.append(o[i * rows : (i + 1) * rows, :] / total[i])
            rest = lse[i]
            for piece in range(3):
                part = rest.astype(BF16).astype(F32)
                rest = rest - part
                stats = jnp.where(lane == HEAD + 3 * j + piece, part, stats)
        if c == 0:
            a = jnp.where(low, values[0], swap(values[1]))
            b = jnp.where(low, values[2], stats)
        else:
            a = jnp.where(low, swap(values[0]), values[1])
            b = jnp.where(low, swap(values[2]), stats)
        out_ref[c, :, 0:128] = a.astype(BF16)
        out_ref[c, :, 128:256] = b.astype(BF16)


def join_kernel(part_ref, w_ref, out_ref):
    sources, rows = part_ref.shape[0], part_ref.shape[1]
    shape = (rows, 128)
    low = lanes(shape) < HEAD
    b = [part_ref[s, :, 128:256].astype(F32) for s in range(sources)]
    lse = [x + pltpu.roll(x, 127, 1) + pltpu.roll(x, 126, 1) for x in b]
    top = functools.reduce(jnp.maximum, lse)
    weight = [jnp.exp(x - top) for x in lse]
    inverse = 1.0 / functools.reduce(jnp.add, weight)
    first = jnp.zeros(shape, F32)
    second = jnp.zeros(shape, F32)
    for s in range(sources):
        w = weight[s] * inverse
        w0, w1, w2 = (w[:, HEAD + 3 * j : HEAD + 3 * j + 1] for j in range(3))
        first = first + part_ref[s, :, 0:128].astype(F32) * jnp.where(low, w0, w1)
        second = second + b[s] * w2
    first = first.astype(BF16)
    second = second[:, 0:HEAD].astype(BF16)
    out = dot(first, w_ref[0:128, :]) + dot(second, w_ref[128 : 128 + HEAD, :])
    out = out.astype(BF16)
    each = rows // sources
    for s in range(sources):
        out_ref[s] = out[s * each : (s + 1) * each, :]


def dispatch_kernel(
    capacity, x_ref, sums_ref, gain_ref, route_ref, gate_ref, hidden_ref, out_ref, mix_ref
):
    beams, steps = x_ref.shape[0], x_ref.shape[1]
    rows = beams * steps
    total = sums_ref[0].astype(F32)
    for s in range(1, sums_ref.shape[0]):
        total = total + sums_ref[s].astype(F32)
    inputs = jnp.concatenate([x_ref[b].astype(F32) for b in range(beams)], axis=0)
    hidden = inputs + total
    hidden_ref[...] = hidden
    expert_in = norm(hidden, gain_ref[...]).astype(BF16)
    experts = out_ref.shape[0]
    slots = experts * capacity
    slot = lanes((rows, slots))
    routes = jnp.concatenate([route_ref[b] for b in range(beams)], axis=0)
    gates = jnp.concatenate([gate_ref[b] for b in range(beams)], axis=0)
    named = jnp.zeros((rows, slots), F32)
    gate = jnp.zeros((rows, slots), F32)
    for j in range(routes.shape[1]):
        hit = routes[:, j : j + 1] == slot // capacity
        named = jnp.where(hit, 1.0, named)
        gate = jnp.where(hit, gates[:, j : j + 1], gate)
    earlier = jnp.where(
        lanes((rows, rows)) < lax.broadcasted_iota(jnp.int32, (rows, rows), 0), 1.0, 0.0
    )
    rank = dot(earlier.astype(BF16), named.astype(BF16))
    placed = (named > 0.0) & (rank == (slot % capacity).astype(F32))
    mix_ref[...] = jnp.where(placed, gate, 0.0)
    place = jnp.where(placed, 1.0, 0.0).T.astype(BF16)
    buffer = dot(place, expert_in)
    for e in range(experts):
        out_ref[e] = buffer[e * capacity : (e + 1) * capacity, :].astype(BF16)


def expert_kernel(x_ref, w_in_ref, w_out_ref, out_ref, rows_ref):
    sources, capacity = x_ref.shape[0], x_ref.shape[1]
    for s in range(sources):
        rows_ref[s * capacity : (s + 1) * capacity, :] = x_ref[s].astype(F32)
    projected = dot(rows_ref[...].astype(BF16), w_in_ref[0])
    half = projected.shape[1] // 2
    g, u = projected[:, 0:half], projected[:, half:]
    act = (g * jax.nn.sigmoid(g) * u).astype(BF16)
    out = dot(act, w_out_ref[0])
    for s in range(sources):
        out_ref[s] = out[s * capacity : (s + 1) * capacity, :].astype(BF16)


def mix_kernel(hidden_ref, mix_ref, back_ref, out_ref, rows_ref):
    experts, capacity = back_ref.shape[0], back_ref.shape[1]
    for e in range(experts):
        rows_ref[e * capacity : (e + 1) * capacity, :] = back_ref[e].astype(F32)
    returned = rows_ref[...].astype(BF16)
    rest = mix_ref[...]
    total = hidden_ref[...]
    for _ in range(3):
        part = rest.astype(BF16)
        rest = rest - part.astype(F32)
        total = total + dot(part, returned)
    steps = out_ref.shape[1]
    for b in range(out_ref.shape[0]):
        out_ref[b] = total[b * steps : (b + 1) * steps, :].astype(BF16)


def final_kernel(seq_ref, parents_ref, own_ref, fresh_k_ref, fresh_v_ref, k_ref, v_ref):
    steps = parents_ref.shape[0]
    here, tail = own_ref.shape[2], own_ref.shape[3]
    for i in range(here):
        beam = seq_ref[0] * here + i
        for s in range(steps - 1, -1, -1):
            beam = parents_ref[s, beam]
        k_ref[i, 0:tail, :] = own_ref[beam // here, 0, beam % here]
        v_ref[i, 0:tail, :] = own_ref[beam // here, 1, beam % here]
        k_ref[i, tail:, :] = fresh_k_ref[i * steps : (i + 1) * steps, :]
        v_ref[i, tail:, :] = fresh_v_ref[i * steps : (i + 1) * steps, :]


def rotary_tables(rows, steps, start):
    half = HEAD // 2
    frequency = ROPE_BASE ** (-(np.arange(half, dtype=np.float64) * 2.0 / HEAD))
    angles = (np.arange(rows) % steps + start)[:, None] * frequency[None, :]
    cosine = np.tile(np.cos(angles), (1, 8)).astype(np.float32)
    sine = np.sin(angles)
    sine = np.tile(np.concatenate([-sine, sine], axis=1), (1, 4)).astype(np.float32)
    return cosine, sine


def call(kernel, outs, *args, ins=None, scratch=(), mib=48, flops=0, moved=0):
    return pl.pallas_call(
        kernel,
        out_shape=outs,
        in_specs=ins or [whole()] * len(args),
        out_specs=jax.tree.map(lambda _: whole(), outs),
        scratch_shapes=list(scratch),
        compiler_params=params(mib),
        cost_estimate=pl.CostEstimate(
            flops=flops or 1 << 20, bytes_accessed=moved or 1 << 20, transcendentals=0
        ),
    )(*args)


def shaped(shape, dtype=BF16):
    return jax.ShapeDtypeStruct(shape, dtype)


def local(
    inputs,
    parents,
    block_len,
    prompt_key_cache,
    prompt_value_cache,
    generated_key_cache,
    generated_value_cache,
    gain_attn,
    gain_moe,
    w_query,
    key_projection_weight,
    value_projection_weight,
    w_output,
    w_in,
    w_out,
    routes,
    gate_weights,
):
    n_seq = lax.axis_size("seq")
    n_req = lax.axis_size("req")
    seq = lax.axis_index("seq").astype(jnp.int32).reshape(1)
    here, steps, width = inputs.shape[1:]
    local_rows = here * steps
    rows = local_rows * n_seq
    keys, kv_width = prompt_key_cache.shape[1:]
    tail = generated_key_cache.shape[2]
    top = routes.shape[3]
    capacity = 4
    x = inputs[0]
    own_shape = (here, tail, kv_width)

    normed, own = call(
        norm_kernel,
        (shaped((local_rows, width)), shaped((n_seq, 2) + own_shape)),
        x,
        gain_attn.reshape(1, width),
        generated_key_cache[0],
        generated_value_cache[0],
    )
    normed_all = lax.all_gather(normed, "seq", axis=0, tiled=True)
    cosine, sine = rotary_tables(rows, steps, keys * n_seq + tail)
    packed_rows = 2 * rows + rows // 2
    qkv = call(
        project_kernel,
        shaped((packed_rows, 128)),
        normed_all,
        w_query,
        key_projection_weight,
        value_projection_weight,
        cosine,
        sine,
    )
    qkv_all = lax.all_gather(qkv, "seq", axis=0, tiled=False)
    own_all = lax.all_to_all(own, "seq", split_axis=0, concat_axis=0, tiled=True)

    pairs = kv_width // 128
    partial, fresh_k, fresh_v = pl.pallas_call(
        attend_kernel,
        grid=(pairs,),
        out_shape=(
            shaped((n_seq, rows, 256)),
            shaped((local_rows, kv_width)),
            shaped((local_rows, kv_width)),
        ),
        in_specs=[
            scalars(),
            scalars(),
            scalars(),
            pl.BlockSpec((2, packed_rows, 128), lambda p: (p, 0, 0)),
            pl.BlockSpec((keys, 128), lambda p: (0, p)),
            pl.BlockSpec((keys, 128), lambda p: (0, p)),
            pl.BlockSpec((here, tail, 128), lambda p: (0, 0, p)),
            pl.BlockSpec((here, tail, 128), lambda p: (0, 0, p)),
        ],
        out_specs=(
            pl.BlockSpec((2, rows, 256), lambda p: (p, 0, 0)),
            pl.BlockSpec((local_rows, 128), lambda p: (0, p)),
            pl.BlockSpec((local_rows, 128), lambda p: (0, p)),
        ),
        scratch_shapes=[
            pltpu.VMEM((6 * rows, keys + 128), F32),
            pltpu.VMEM((6 * rows, keys + 128), BF16),
            pltpu.VMEM((8, keys), F32),
            pltpu.VMEM((rows, 128), F32),
        ],
        compiler_params=params(48),
        cost_estimate=pl.CostEstimate(
            flops=4 * 24 * rows * keys * HEAD,
            bytes_accessed=4 * keys * kv_width,
            transcendentals=24 * rows * keys,
        ),
    )(
        seq,
        parents[0],
        block_len,
        qkv_all,
        prompt_key_cache[0],
        prompt_value_cache[0],
        generated_key_cache[0],
        generated_value_cache[0],
    )
    parts = lax.all_to_all(partial, "seq", split_axis=0, concat_axis=0, tiled=True)
    sums = call(join_kernel, shaped((n_seq, local_rows, width)), parts, w_output)
    sums = lax.all_to_all(sums, "seq", split_axis=0, concat_axis=0, tiled=True)
    hidden, buffer, mix = call(
        functools.partial(dispatch_kernel, capacity),
        (
            shaped((local_rows, width), F32),
            shaped((n_req, capacity, width)),
            shaped((local_rows, n_req * capacity), F32),
        ),
        x,
        sums,
        gain_moe.reshape(1, width),
        routes[0],
        gate_weights[0],
    )
    buffer = lax.all_to_all(buffer, "req", split_axis=0, concat_axis=0, tiled=True)
    back = call(
        expert_kernel,
        shaped(buffer.shape),
        buffer,
        w_in,
        w_out,
        scratch=[pltpu.VMEM((n_req * capacity, width), F32)],
    )
    back = lax.all_to_all(back, "req", split_axis=0, concat_axis=0, tiled=True)
    mixed = call(
        mix_kernel,
        shaped((here, steps, width)),
        hidden,
        mix,
        back,
        scratch=[pltpu.VMEM((n_req * capacity, width), F32)],
    )
    final_k, final_v = call(
        final_kernel,
        (shaped((here, tail + steps, kv_width)),) * 2,
        seq,
        parents[0],
        own_all,
        fresh_k,
        fresh_v,
        ins=[scalars(), scalars(), whole(), whole(), whole()],
    )
    return (mixed[None], final_k[None], final_v[None])


def solution(mesh):
    placed = (
        P("req", "seq", None, None),
        P("req", None, None),
        P("req", "seq"),
        P("req", "seq", None),
        P("req", "seq", None),
        P("req", "seq", None, None),
        P("req", "seq", None, None),
        P(),
        P(),
        P(None, "seq"),
        P(None, "seq"),
        P(None, "seq"),
        P("seq", None),
        P("req", None, None),
        P("req", None, None),
        P("req", "seq", None, None),
        P("req", "seq", None, None),
    )
    return jax.shard_map(
        local,
        mesh=mesh,
        in_specs=placed,
        out_specs=(P("req", "seq", None, None),) * 3,
        check_vma=False,
    )
```

```python
import functools

import jax
import jax.numpy as jnp
import numpy as np
from jax import lax
from jax.experimental import pallas as pl
from jax.experimental.pallas import tpu as pltpu
from jax.sharding import PartitionSpec as P

HEAD = 64
BLK = 128
EPSILON = 1e-05
ROPE_BASE = 10000.0
FILL = -(2.0**100)
SCALE = 0.125
BF16 = jnp.bfloat16
F32 = jnp.float32


def whole():
    return pl.BlockSpec(memory_space=pltpu.VMEM)


def scalars():
    return pl.BlockSpec(memory_space=pltpu.SMEM)


def params(mib):
    return pltpu.CompilerParams(vmem_limit_bytes=mib << 20)


def dot(a, b):
    return jnp.dot(a, b, preferred_element_type=F32)


def dot_t(a, b):
    return lax.dot_general(a, b, (((1,), (1,)), ((), ())), preferred_element_type=F32)


def lanes(shape):
    return lax.broadcasted_iota(jnp.int32, shape, len(shape) - 1)


def norm(x, gain):
    mean_sq = jnp.mean(x * x, axis=-1, keepdims=True)
    return x * lax.rsqrt(mean_sq + EPSILON) * gain


def norm_kernel(x_ref, gain_ref, out_ref):
    beams, steps = x_ref.shape[0], x_ref.shape[1]
    gain = gain_ref[...].reshape(1, -1)
    rows = [norm(x_ref[b].astype(F32), gain) for b in range(beams)]
    rows = jnp.concatenate(rows, axis=0).astype(BF16)
    for d in range(out_ref.shape[0]):
        out_ref[d] = rows


def pack_kernel(order_ref, own_k_ref, own_v_ref, out_ref):
    out_ref[0] = own_k_ref[...]
    out_ref[1] = own_v_ref[...]


def project_kernel(x_ref, wq_ref, wk_ref, wv_ref, cos_ref, sin_ref, out_ref):
    rows = x_ref.shape[0] * x_ref.shape[1]
    x = x_ref[...].reshape(rows, x_ref.shape[2])
    q = dot_t(x, wq_ref[...]) * SCALE
    k = dot_t(x, wk_ref[...])
    v = dot_t(x, wv_ref[...])
    y = jnp.concatenate([q, k], axis=1)
    width = y.shape[1]
    half = HEAD // 2
    first = lanes(y.shape) % HEAD < half
    turned = jnp.where(first, pltpu.roll(y, width - half, 1), pltpu.roll(y, half, 1))
    y = (y * cos_ref[...] + turned * sin_ref[...]).astype(BF16)
    v = jnp.concatenate([v[0 : rows // 2], v[rows // 2 :]], axis=1).astype(BF16)
    for d in range(out_ref.shape[0]):
        out_ref[d, 0:rows, :] = y[:, 0:128]
        out_ref[d, rows : 2 * rows, :] = y[:, 128:256]
        out_ref[d, 2 * rows : 2 * rows + rows // 2, :] = v


def lookup(parents_ref, step, cur, beams):
    found = jnp.zeros(cur.shape, jnp.int32)
    for b in range(beams):
        found = jnp.where(cur == b, parents_ref[step, b], found)
    return found


def mask_kernel(tail, here, order_ref, seq_ref, parents_ref, len_ref, bias_ref, extra_ref):
    steps, beams = parents_ref.shape
    own_keys = here * tail
    seq = seq_ref[0]
    shape = extra_ref.shape
    lane = lanes(shape)
    spot = lanes((bias_ref.shape[0], BLK))
    for j in range(bias_ref.shape[1] // BLK):
        bias_ref[:, j * BLK : (j + 1) * BLK] = jnp.where(spot < len_ref[0, j], 0.0, FILL)
    row = lax.broadcasted_iota(jnp.int32, shape, 0)
    step = row % steps
    cur = row // steps
    fresh = lane - own_keys
    key_beam = fresh // steps
    key_step = fresh % steps
    live = jnp.zeros(shape, jnp.int32)
    for s in range(steps - 1, -1, -1):
        hit = (key_step == s) & (cur == key_beam) & (step >= s) & (key_beam // here == seq)
        live = live | jnp.where((fresh >= 0) & hit, 1, 0)
        cur = jnp.where(step >= s, lookup(parents_ref, s, cur, beams), cur)
    own_hit = (lane < own_keys) & (cur == seq * here + lane // tail)
    live = live | jnp.where(own_hit, 1, 0)
    extra_ref[...] = jnp.where(live > 0, 0.0, FILL)


def attend_kernel(
    seq_ref,
    parents_ref,
    bias_ref,
    extra_ref,
    qkv_ref,
    k_ref,
    v_ref,
    own_k_ref,
    own_v_ref,
    out_ref,
    fresh_k_ref,
    fresh_v_ref,
    s_ref,
    p_ref,
):
    steps, beams = parents_ref.shape
    rows = steps * beams
    keys = k_ref.shape[0]
    here = own_k_ref.shape[0]
    tail = own_k_ref.shape[1]
    own_keys = here * tail
    seq = seq_ref[0]
    shape = (rows, 128)
    lane = lanes(shape)
    low = lane < HEAD

    def swap(x):
        return pltpu.roll(x, HEAD, 1)

    parts = []
    fresh_k, fresh_v = [], []
    for c in range(2):
        t0 = qkv_ref[c, 0:rows, :].astype(F32)
        t1 = qkv_ref[c, rows : 2 * rows, :].astype(F32)
        tv = qkv_ref[c, 2 * rows : 2 * rows + rows // 2, :].astype(F32)
        keep = low if c == 0 else ~low
        for tile in (t0, swap(t0), t1) if c == 0 else (swap(t0), t0, swap(t1)):
            parts.append(jnp.where(keep, tile, 0.0).astype(BF16))
        fresh_k.append(t1)
        fresh_v.append(jnp.concatenate([tv, swap(tv)], axis=0))
    q = jnp.concatenate(parts, axis=0)
    new_k = jnp.where(low, swap(fresh_k[0]), fresh_k[1]).astype(BF16)
    new_v = jnp.where(low, fresh_v[0], swap(fresh_v[1])).astype(BF16)
    fill = jnp.zeros((128 - own_keys - rows, 128), BF16)
    extra_k = jnp.concatenate([own_k_ref[...].reshape(own_keys, 128), new_k, fill], axis=0)
    extra_v = jnp.concatenate([own_v_ref[...].reshape(own_keys, 128), new_v, fill], axis=0)

    pick_row = lax.broadcasted_iota(jnp.int32, (here * steps, rows), 0)
    pick_col = lanes((here * steps, rows))
    chosen = jnp.zeros(pick_row.shape, jnp.int32)
    for i in range(here):
        beam = seq * here + i
        for s in range(steps - 1, -1, -1):
            hit = (pick_row == i * steps + s) & (pick_col == beam * steps + s)
            chosen = chosen | jnp.where(hit, 1, 0)
            beam = parents_ref[s, beam]
    chosen = chosen.astype(F32).astype(BF16)
    fresh_k_ref[...] = dot(chosen, new_k).astype(BF16)
    fresh_v_ref[...] = dot(chosen, new_v).astype(BF16)

    s_ref[:, 0:keys] = dot_t(q, k_ref[...])
    s_ref[:, keys : keys + 128] = dot_t(q, extra_k)
    lse, total = [], []
    for i in range(6):
        span = slice(i * rows, (i + 1) * rows)
        s0 = s_ref[span, 0:keys] + bias_ref[0:1, :]
        s1 = s_ref[span, keys : keys + 128] + extra_ref[...]
        top = jnp.maximum(
            jnp.max(s0, axis=-1, keepdims=True), jnp.max(s1, axis=-1, keepdims=True)
        )
        e0 = jnp.exp(s0 - top)
        e1 = jnp.exp(s1 - top)
        p_ref[span, 0:keys] = e0.astype(BF16)
        p_ref[span, keys : keys + 128] = e1.astype(BF16)
        denominator = jnp.sum(e0, axis=-1, keepdims=True) + jnp.sum(e1, axis=-1, keepdims=True)
        total.append(denominator)
        lse.append(top + jnp.log(denominator))
    o = dot(p_ref[:, 0:keys], v_ref[...]) + dot(p_ref[:, keys : keys + 128], extra_v)
    for c in range(2):
        values = []
        stats = jnp.zeros(shape, F32)
        for j in range(3):
            i = 3 * c + j
            values.append(o[i * rows : (i + 1) * rows, :] / total[i])
            rest = lse[i]
            for piece in range(3):
                part = rest.astype(BF16).astype(F32)
                rest = rest - part
                stats = jnp.where(lane == HEAD + 3 * j + piece, part, stats)
        if c == 0:
            a = jnp.where(low, values[0], swap(values[1]))
            b = jnp.where(low, values[2], stats)
        else:
            a = jnp.where(low, swap(values[0]), values[1])
            b = jnp.where(low, swap(values[2]), stats)
        out_ref[c, :, 0:128] = a.astype(BF16)
        out_ref[c, :, 128:256] = b.astype(BF16)


def join_kernel(part_ref, w_ref, out_ref):
    sources, rows = part_ref.shape[0], part_ref.shape[1]
    shape = (rows, 128)
    low = lanes(shape) < HEAD
    b = [part_ref[s, :, 128:256].astype(F32) for s in range(sources)]
    lse = [x + pltpu.roll(x, 127, 1) + pltpu.roll(x, 126, 1) for x in b]
    top = functools.reduce(jnp.maximum, lse)
    weight = [jnp.exp(x - top) for x in lse]
    inverse = 1.0 / functools.reduce(jnp.add, weight)
    first = jnp.zeros(shape, F32)
    second = jnp.zeros(shape, F32)
    for s in range(sources):
        w = weight[s] * inverse
        w0, w1, w2 = (w[:, HEAD + 3 * j : HEAD + 3 * j + 1] for j in range(3))
        first = first + part_ref[s, :, 0:128].astype(F32) * jnp.where(low, w0, w1)
        second = second + b[s] * w2
    first = first.astype(BF16)
    second = second[:, 0:HEAD].astype(BF16)
    out = dot(first, w_ref[0:128, :]) + dot(second, w_ref[128 : 128 + HEAD, :])
    out = out.astype(BF16)
    each = rows // sources
    for s in range(sources):
        out_ref[s] = out[s * each : (s + 1) * each, :]


def route_kernel(capacity, order_ref, route_ref, gate_ref, place_ref, mix_ref):
    beams, steps = route_ref.shape[0], route_ref.shape[1]
    rows = beams * steps
    slots = place_ref.shape[0]
    slot = lanes((rows, slots))
    routes = jnp.concatenate([route_ref[b] for b in range(beams)], axis=0)
    gates = jnp.concatenate([gate_ref[b] for b in range(beams)], axis=0)
    named = jnp.zeros((rows, slots), F32)
    gate = jnp.zeros((rows, slots), F32)
    for j in range(routes.shape[1]):
        hit = routes[:, j : j + 1] == slot // capacity
        named = jnp.where(hit, 1.0, named)
        gate = jnp.where(hit, gates[:, j : j + 1], gate)
    earlier = jnp.where(
        lanes((rows, rows)) < lax.broadcasted_iota(jnp.int32, (rows, rows), 0), 1.0, 0.0
    )
    rank = dot(earlier.astype(BF16), named.astype(BF16))
    placed = (named > 0.0) & (rank == (slot % capacity).astype(F32))
    mix_ref[...] = jnp.where(placed, gate, 0.0)
    place_ref[...] = jnp.where(placed, 1.0, 0.0).T.astype(BF16)


def dispatch_kernel(x_ref, sums_ref, gain_ref, place_ref, hidden_ref, out_ref):
    beams = x_ref.shape[0]
    total = sums_ref[0].astype(F32)
    for s in range(1, sums_ref.shape[0]):
        total = total + sums_ref[s].astype(F32)
    inputs = jnp.concatenate([x_ref[b].astype(F32) for b in range(beams)], axis=0)
    hidden = inputs + total
    hidden_ref[...] = hidden
    expert_in = norm(hidden, gain_ref[...].reshape(1, -1)).astype(BF16)
    buffer = dot(place_ref[...], expert_in)
    experts, capacity = out_ref.shape[0], out_ref.shape[1]
    for e in range(experts):
        out_ref[e] = buffer[e * capacity : (e + 1) * capacity, :].astype(BF16)


def expert_kernel(x_ref, w_in_ref, w_out_ref, out_ref, rows_ref):
    sources, capacity = x_ref.shape[0], x_ref.shape[1]
    for s in range(sources):
        rows_ref[s * capacity : (s + 1) * capacity, :] = x_ref[s].astype(F32)
    projected = dot(rows_ref[...].astype(BF16), w_in_ref[0])
    half = projected.shape[1] // 2
    g, u = projected[:, 0:half], projected[:, half:]
    act = (g * jax.nn.sigmoid(g) * u).astype(BF16)
    out = dot(act, w_out_ref[0])
    for s in range(sources):
        out_ref[s] = out[s * capacity : (s + 1) * capacity, :].astype(BF16)


def mix_kernel(hidden_ref, mix_ref, back_ref, out_ref, rows_ref):
    experts, capacity = back_ref.shape[0], back_ref.shape[1]
    for e in range(experts):
        rows_ref[e * capacity : (e + 1) * capacity, :] = back_ref[e].astype(F32)
    returned = rows_ref[...].astype(BF16)
    rest = mix_ref[...]
    total = hidden_ref[...]
    for _ in range(3):
        part = rest.astype(BF16)
        rest = rest - part.astype(F32)
        total = total + dot(part, returned)
    steps = out_ref.shape[1]
    for b in range(out_ref.shape[0]):
        out_ref[b] = total[b * steps : (b + 1) * steps, :].astype(BF16)


def final_kernel(seq_ref, parents_ref, fresh_k_ref, fresh_v_ref, *refs):
    own_refs, (k_ref, v_ref) = refs[:-2], refs[-2:]
    steps = parents_ref.shape[0]
    here, tail = own_refs[0].shape[1], own_refs[0].shape[2]
    seq = seq_ref[0]
    for i in range(here):
        beam = seq * here + i
        for s in range(steps - 1, -1, -1):
            beam = parents_ref[s, beam]
        apart = lax.bitwise_xor(beam // here, seq)
        for j, own_ref in enumerate(own_refs):

            @pl.when(apart == j)
            def _():
                k_ref[0:tail, i, :] = own_ref[0, beam % here]
                v_ref[0:tail, i, :] = own_ref[1, beam % here]

        k_ref[tail:, i, :] = fresh_k_ref[i * steps : (i + 1) * steps, :]
        v_ref[tail:, i, :] = fresh_v_ref[i * steps : (i + 1) * steps, :]


def rotary_tables(rows, steps, start):
    half = HEAD // 2
    frequency = ROPE_BASE ** (-(np.arange(half, dtype=np.float64) * 2.0 / HEAD))
    angles = (np.arange(rows) % steps + start)[:, None] * frequency[None, :]
    cosine = np.tile(np.cos(angles), (1, 8)).astype(np.float32)
    sine = np.sin(angles)
    sine = np.tile(np.concatenate([-sine, sine], axis=1), (1, 4)).astype(np.float32)
    return cosine, sine


def call(kernel, outs, *args, ins=None, scratch=(), mib=48, flops=0, moved=0, grid=()):
    return pl.pallas_call(
        kernel,
        grid=grid,
        out_shape=outs,
        in_specs=ins or [whole()] * len(args),
        out_specs=jax.tree.map(lambda _: whole(), outs),
        scratch_shapes=list(scratch),
        compiler_params=params(mib),
        cost_estimate=pl.CostEstimate(
            flops=flops or 1 << 20, bytes_accessed=moved or 1 << 20, transcendentals=0
        ),
    )(*args)


def shaped(shape, dtype=BF16):
    return jax.ShapeDtypeStruct(shape, dtype)


def local(
    inputs,
    parents,
    block_len,
    prompt_key_cache,
    prompt_value_cache,
    generated_key_cache,
    generated_value_cache,
    gain_attn,
    gain_moe,
    w_query,
    key_projection_weight,
    value_projection_weight,
    w_output,
    w_in,
    w_out,
    routes,
    gate_weights,
):
    n_seq = lax.axis_size("seq")
    n_req = lax.axis_size("req")
    seq = lax.axis_index("seq").astype(jnp.int32).reshape(1)
    here, steps, width = inputs.shape[1:]
    local_rows = here * steps
    rows = local_rows * n_seq
    keys, kv_width = prompt_key_cache.shape[1:]
    tail = generated_key_cache.shape[2]
    top = routes.shape[3]
    capacity = 4
    x = inputs[0]
    anywhere = pl.BlockSpec(memory_space=pl.ANY)

    def exchange(a, axis):
        return lax.all_to_all(a, axis, split_axis=0, concat_axis=0, tiled=True)

    def apart(a, distance):
        return lax.ppermute(a, "seq", [(i, i ^ distance) for i in range(n_seq)])

    normed = call(
        norm_kernel,
        shaped((n_seq, local_rows, width)),
        x,
        gain_attn,
        grid=(1,),
        ins=[
            pl.BlockSpec((here, steps, width), lambda i: (0, 0, 0)),
            pl.BlockSpec((width,), lambda i: (0,)),
        ],
        mib=60,
    )
    normed_all = exchange(normed, "seq")
    bias, extra = call(
        functools.partial(mask_kernel, tail, here),
        (shaped((8, keys), F32), shaped((rows, 128), F32)),
        normed,
        seq,
        parents[0],
        block_len,
        ins=[anywhere, scalars(), scalars(), scalars()],
        mib=8,
    )
    cosine, sine = rotary_tables(rows, steps, keys * n_seq + tail)
    packed_rows = 2 * rows + rows // 2
    qkv = call(
        project_kernel,
        shaped((n_seq, packed_rows, 128)),
        normed_all,
        w_query.T,
        key_projection_weight.T,
        value_projection_weight.T,
        cosine,
        sine,
        mib=16,
    )
    qkv_all = exchange(qkv, "seq")

    pairs = kv_width // 128
    partial, fresh_k, fresh_v = pl.pallas_call(
        attend_kernel,
        grid=(pairs,),
        out_shape=(
            shaped((n_seq, rows, 256)),
            shaped((local_rows, kv_width)),
            shaped((local_rows, kv_width)),
        ),
        in_specs=[
            scalars(),
            scalars(),
            whole(),
            whole(),
            pl.BlockSpec((2, packed_rows, 128), lambda p: (p, 0, 0)),
            pl.BlockSpec((keys, 128), lambda p: (0, p)),
            pl.BlockSpec((keys, 128), lambda p: (0, p)),
            pl.BlockSpec((here, tail, 128), lambda p: (0, 0, p)),
            pl.BlockSpec((here, tail, 128), lambda p: (0, 0, p)),
        ],
        out_specs=(
            pl.BlockSpec((2, rows, 256), lambda p: (p, 0, 0)),
            pl.BlockSpec((local_rows, 128), lambda p: (0, p)),
            pl.BlockSpec((local_rows, 128), lambda p: (0, p)),
        ),
        scratch_shapes=[
            pltpu.VMEM((6 * rows, keys + 128), F32),
            pltpu.VMEM((6 * rows, keys + 128), BF16),
        ],
        compiler_params=params(60),
        cost_estimate=pl.CostEstimate(
            flops=4 * 24 * rows * keys * HEAD,
            bytes_accessed=4 * keys * kv_width,
            transcendentals=24 * rows * keys,
        ),
    )(
        seq,
        parents[0],
        bias,
        extra,
        qkv_all,
        prompt_key_cache[0],
        prompt_value_cache[0],
        generated_key_cache[0],
        generated_value_cache[0],
    )
    parts = exchange(partial, "seq")
    sums = call(join_kernel, shaped((n_seq, local_rows, width)), parts, w_output, mib=16)
    slots = n_req * capacity
    place, mix = call(
        functools.partial(route_kernel, capacity),
        (shaped((slots, local_rows)), shaped((local_rows, slots), F32)),
        sums,
        routes[0],
        gate_weights[0],
        ins=[anywhere, whole(), whole()],
        mib=8,
    )
    sums = exchange(sums, "seq")
    hidden, buffer = call(
        dispatch_kernel,
        (shaped((local_rows, width), F32), shaped((n_req, capacity, width))),
        x,
        sums,
        gain_moe,
        place,
        mib=16,
    )
    own = call(
        pack_kernel,
        shaped((2, here, tail, kv_width)),
        buffer,
        generated_key_cache[0],
        generated_value_cache[0],
        ins=[anywhere, whole(), whole()],
        mib=8,
    )
    even = [own] + [apart(own, k) for k in range(2, n_seq, 2)]
    odd = [apart(a, 1) for a in even]
    owns = [a for pair in zip(even, odd) for a in pair]
    buffer = exchange(buffer, "req")
    back = call(
        expert_kernel,
        shaped(buffer.shape),
        buffer,
        w_in,
        w_out,
        scratch=[pltpu.VMEM((slots, width), F32)],
        mib=16,
    )
    back = exchange(back, "req")
    mixed = call(
        mix_kernel,
        shaped((here, steps, width)),
        hidden,
        mix,
        back,
        scratch=[pltpu.VMEM((slots, width), F32)],
        mib=16,
    )
    final_k, final_v = call(
        final_kernel,
        (shaped((tail + steps, here, kv_width)),) * 2,
        seq,
        parents[0],
        fresh_k,
        fresh_v,
        *owns,
        ins=[scalars(), scalars()] + [whole()] * (2 + n_seq),
        mib=16,
    )
    return (
        mixed[None],
        final_k.transpose(1, 0, 2)[None],
        final_v.transpose(1, 0, 2)[None],
    )


def solution(mesh):
    placed = (
        P("req", "seq", None, None),
        P("req", None, None),
        P("req", "seq"),
        P("req", "seq", None),
        P("req", "seq", None),
        P("req", "seq", None, None),
        P("req", "seq", None, None),
        P(),
        P(),
        P(None, "seq"),
        P(None, "seq"),
        P(None, "seq"),
        P("seq", None),
        P("req", None, None),
        P("req", None, None),
        P("req", "seq", None, None),
        P("req", "seq", None, None),
    )
    return jax.shard_map(
        local,
        mesh=mesh,
        in_specs=placed,
        out_specs=(P("req", "seq", None, None),) * 3,
        check_vma=False,
    )
```

```python
import functools

import jax
import jax.numpy as jnp
import numpy as np
from jax import lax
from jax.experimental import pallas as pl
from jax.experimental.pallas import tpu as pltpu
from jax.sharding import PartitionSpec as P

HEAD = 64
BLK = 128
EPSILON = 1e-05
ROPE_BASE = 10000.0
FILL = -(2.0**100)
SCALE = 0.125
BF16 = jnp.bfloat16
F32 = jnp.float32


def scalars():
    return pl.BlockSpec(memory_space=pltpu.SMEM)


def params(mib):
    return pltpu.CompilerParams(vmem_limit_bytes=mib << 20)


def dot(a, b):
    return jnp.dot(a, b, preferred_element_type=F32)


def dot_t(a, b):
    return lax.dot_general(a, b, (((1,), (1,)), ((), ())), preferred_element_type=F32)


def lanes(shape):
    return lax.broadcasted_iota(jnp.int32, shape, len(shape) - 1)


def norm(x, gain):
    mean_sq = jnp.mean(x * x, axis=-1, keepdims=True)
    return x * lax.rsqrt(mean_sq + EPSILON) * gain


def norm_kernel(x_ref, gain_ref, out_ref):
    beams, steps = x_ref.shape[0], x_ref.shape[1]
    gain = gain_ref[...].reshape(1, -1)
    rows = [norm(x_ref[b].astype(F32), gain) for b in range(beams)]
    rows = jnp.concatenate(rows, axis=0).astype(BF16)
    for d in range(out_ref.shape[0]):
        out_ref[d] = rows


def pack_kernel(order_ref, own_k_ref, own_v_ref, out_ref):
    out_ref[0] = own_k_ref[...]
    out_ref[1] = own_v_ref[...]


def project_kernel(x_ref, wq_ref, wk_ref, wv_ref, cos_ref, sin_ref, out_ref):
    rows = x_ref.shape[0] * x_ref.shape[1]
    x = x_ref[...].reshape(rows, x_ref.shape[2])
    q = dot_t(x, wq_ref[...]) * SCALE
    k = dot_t(x, wk_ref[...])
    v = dot_t(x, wv_ref[...])
    y = jnp.concatenate([q, k], axis=1)
    width = y.shape[1]
    half = HEAD // 2
    first = lanes(y.shape) % HEAD < half
    turned = jnp.where(first, pltpu.roll(y, width - half, 1), pltpu.roll(y, half, 1))
    y = (y * cos_ref[...] + turned * sin_ref[...]).astype(BF16)
    v = jnp.concatenate([v[0 : rows // 2], v[rows // 2 :]], axis=1).astype(BF16)
    for d in range(out_ref.shape[0]):
        out_ref[d, 0:rows, :] = y[:, 0:128]
        out_ref[d, rows : 2 * rows, :] = y[:, 128:256]
        out_ref[d, 2 * rows : 2 * rows + rows // 2, :] = v


def lookup(parents_ref, step, cur, beams):
    found = jnp.zeros(cur.shape, jnp.int32)
    for b in range(beams):
        found = jnp.where(cur == b, parents_ref[step, b], found)
    return found


def mask_kernel(tail, here, order_ref, seq_ref, parents_ref, len_ref, bias_ref, extra_ref):
    steps, beams = parents_ref.shape
    own_keys = here * tail
    seq = seq_ref[0]
    shape = extra_ref.shape
    lane = lanes(shape)
    spot = lanes((bias_ref.shape[0], BLK))
    for j in range(bias_ref.shape[1] // BLK):
        bias_ref[:, j * BLK : (j + 1) * BLK] = jnp.where(spot < len_ref[0, j], 0.0, FILL)
    row = lax.broadcasted_iota(jnp.int32, shape, 0)
    step = row % steps
    cur = row // steps
    fresh = lane - own_keys
    key_beam = fresh // steps
    key_step = fresh % steps
    live = jnp.zeros(shape, jnp.int32)
    for s in range(steps - 1, -1, -1):
        hit = (key_step == s) & (cur == key_beam) & (step >= s) & (key_beam // here == seq)
        live = live | jnp.where((fresh >= 0) & hit, 1, 0)
        cur = jnp.where(step >= s, lookup(parents_ref, s, cur, beams), cur)
    own_hit = (lane < own_keys) & (cur == seq * here + lane // tail)
    live = live | jnp.where(own_hit, 1, 0)
    extra_ref[...] = jnp.where(live > 0, 0.0, FILL)


def attend_kernel(
    seq_ref,
    parents_ref,
    bias_ref,
    extra_ref,
    qkv_ref,
    k_ref,
    v_ref,
    own_k_ref,
    own_v_ref,
    out_ref,
    fresh_k_ref,
    fresh_v_ref,
    s_ref,
    p_ref,
):
    steps, beams = parents_ref.shape
    rows = steps * beams
    keys = k_ref.shape[0]
    here = own_k_ref.shape[0]
    tail = own_k_ref.shape[1]
    own_keys = here * tail
    seq = seq_ref[0]
    shape = (rows, 128)
    lane = lanes(shape)
    low = lane < HEAD

    def swap(x):
        return pltpu.roll(x, HEAD, 1)

    parts = []
    fresh_k, fresh_v = [], []
    for c in range(2):
        t0 = qkv_ref[c, 0:rows, :].astype(F32)
        t1 = qkv_ref[c, rows : 2 * rows, :].astype(F32)
        tv = qkv_ref[c, 2 * rows : 2 * rows + rows // 2, :].astype(F32)
        keep = low if c == 0 else ~low
        for tile in (t0, swap(t0), t1) if c == 0 else (swap(t0), t0, swap(t1)):
            parts.append(jnp.where(keep, tile, 0.0).astype(BF16))
        fresh_k.append(t1)
        fresh_v.append(jnp.concatenate([tv, swap(tv)], axis=0))
    q = jnp.concatenate(parts, axis=0)
    new_k = jnp.where(low, swap(fresh_k[0]), fresh_k[1]).astype(BF16)
    new_v = jnp.where(low, fresh_v[0], swap(fresh_v[1])).astype(BF16)
    fill = jnp.zeros((128 - own_keys - rows, 128), BF16)
    extra_k = jnp.concatenate([own_k_ref[...].reshape(own_keys, 128), new_k, fill], axis=0)
    extra_v = jnp.concatenate([own_v_ref[...].reshape(own_keys, 128), new_v, fill], axis=0)

    pick_row = lax.broadcasted_iota(jnp.int32, (here * steps, rows), 0)
    pick_col = lanes((here * steps, rows))
    chosen = jnp.zeros(pick_row.shape, jnp.int32)
    for i in range(here):
        beam = seq * here + i
        for s in range(steps - 1, -1, -1):
            hit = (pick_row == i * steps + s) & (pick_col == beam * steps + s)
            chosen = chosen | jnp.where(hit, 1, 0)
            beam = parents_ref[s, beam]
    chosen = chosen.astype(F32).astype(BF16)
    fresh_k_ref[...] = dot(chosen, new_k).astype(BF16)
    fresh_v_ref[...] = dot(chosen, new_v).astype(BF16)

    s_ref[:, 0:keys] = dot_t(q, k_ref[...])
    s_ref[:, keys : keys + 128] = dot_t(q, extra_k)
    lse, total = [], []
    for i in range(6):
        span = slice(i * rows, (i + 1) * rows)
        s0 = s_ref[span, 0:keys] + bias_ref[0:1, :]
        s1 = s_ref[span, keys : keys + 128] + extra_ref[...]
        top = jnp.maximum(
            jnp.max(s0, axis=-1, keepdims=True), jnp.max(s1, axis=-1, keepdims=True)
        )
        e0 = jnp.exp(s0 - top)
        e1 = jnp.exp(s1 - top)
        p_ref[span, 0:keys] = e0.astype(BF16)
        p_ref[span, keys : keys + 128] = e1.astype(BF16)
        denominator = jnp.sum(e0, axis=-1, keepdims=True) + jnp.sum(e1, axis=-1, keepdims=True)
        total.append(denominator)
        lse.append(top + jnp.log(denominator))
    o = dot(p_ref[:, 0:keys], v_ref[...]) + dot(p_ref[:, keys : keys + 128], extra_v)
    for c in range(2):
        values = []
        stats = jnp.zeros(shape, F32)
        for j in range(3):
            i = 3 * c + j
            values.append(o[i * rows : (i + 1) * rows, :] / total[i])
            rest = lse[i]
            for piece in range(3):
                part = rest.astype(BF16).astype(F32)
                rest = rest - part
                stats = jnp.where(lane == HEAD + 3 * j + piece, part, stats)
        if c == 0:
            a = jnp.where(low, values[0], swap(values[1]))
            b = jnp.where(low, values[2], stats)
        else:
            a = jnp.where(low, swap(values[0]), values[1])
            b = jnp.where(low, swap(values[2]), stats)
        out_ref[c, :, 0:128] = a.astype(BF16)
        out_ref[c, :, 128:256] = b.astype(BF16)


def join_kernel(part_ref, w_ref, out_ref):
    sources, rows = part_ref.shape[0], part_ref.shape[1]
    shape = (rows, 128)
    low = lanes(shape) < HEAD
    b = [part_ref[s, :, 128:256].astype(F32) for s in range(sources)]
    lse = [x + pltpu.roll(x, 127, 1) + pltpu.roll(x, 126, 1) for x in b]
    top = functools.reduce(jnp.maximum, lse)
    weight = [jnp.exp(x - top) for x in lse]
    inverse = 1.0 / functools.reduce(jnp.add, weight)
    first = jnp.zeros(shape, F32)
    second = jnp.zeros(shape, F32)
    for s in range(sources):
        w = weight[s] * inverse
        w0, w1, w2 = (w[:, HEAD + 3 * j : HEAD + 3 * j + 1] for j in range(3))
        first = first + part_ref[s, :, 0:128].astype(F32) * jnp.where(low, w0, w1)
        second = second + b[s] * w2
    first = first.astype(BF16)
    second = second[:, 0:HEAD].astype(BF16)
    out = dot(first, w_ref[0:128, :]) + dot(second, w_ref[128 : 128 + HEAD, :])
    out = out.astype(BF16)
    each = rows // sources
    for s in range(sources):
        out_ref[s] = out[s * each : (s + 1) * each, :]


def route_kernel(capacity, order_ref, route_ref, gate_ref, place_ref, mix_ref):
    beams, steps = route_ref.shape[0], route_ref.shape[1]
    rows = beams * steps
    slots = place_ref.shape[0]
    slot = lanes((rows, slots))
    routes = jnp.concatenate([route_ref[b] for b in range(beams)], axis=0)
    gates = jnp.concatenate([gate_ref[b] for b in range(beams)], axis=0)
    named = jnp.zeros((rows, slots), F32)
    gate = jnp.zeros((rows, slots), F32)
    for j in range(routes.shape[1]):
        hit = routes[:, j : j + 1] == slot // capacity
        named = jnp.where(hit, 1.0, named)
        gate = jnp.where(hit, gates[:, j : j + 1], gate)
    earlier = jnp.where(
        lanes((rows, rows)) < lax.broadcasted_iota(jnp.int32, (rows, rows), 0), 1.0, 0.0
    )
    rank = dot(earlier.astype(BF16), named.astype(BF16))
    placed = (named > 0.0) & (rank == (slot % capacity).astype(F32))
    mix_ref[...] = jnp.where(placed, gate, 0.0)
    place_ref[...] = jnp.where(placed, 1.0, 0.0).T.astype(BF16)


def dispatch_kernel(x_ref, sums_ref, gain_ref, place_ref, hidden_ref, out_ref):
    beams = x_ref.shape[0]
    total = sums_ref[0].astype(F32)
    for s in range(1, sums_ref.shape[0]):
        total = total + sums_ref[s].astype(F32)
    inputs = jnp.concatenate([x_ref[b].astype(F32) for b in range(beams)], axis=0)
    hidden = inputs + total
    hidden_ref[...] = hidden
    expert_in = norm(hidden, gain_ref[...].reshape(1, -1)).astype(BF16)
    buffer = dot(place_ref[...], expert_in)
    experts, capacity = out_ref.shape[0], out_ref.shape[1]
    for e in range(experts):
        out_ref[e] = buffer[e * capacity : (e + 1) * capacity, :].astype(BF16)


def expert_kernel(x_ref, w_in_ref, w_out_ref, out_ref, rows_ref):
    sources, capacity = x_ref.shape[0], x_ref.shape[1]
    for s in range(sources):
        rows_ref[s * capacity : (s + 1) * capacity, :] = x_ref[s].astype(F32)
    projected = dot(rows_ref[...].astype(BF16), w_in_ref[0])
    half = projected.shape[1] // 2
    g, u = projected[:, 0:half], projected[:, half:]
    act = (g * jax.nn.sigmoid(g) * u).astype(BF16)
    out = dot(act, w_out_ref[0])
    for s in range(sources):
        out_ref[s] = out[s * capacity : (s + 1) * capacity, :].astype(BF16)


def mix_kernel(hidden_ref, mix_ref, back_ref, out_ref, rows_ref):
    experts, capacity = back_ref.shape[0], back_ref.shape[1]
    for e in range(experts):
        rows_ref[e * capacity : (e + 1) * capacity, :] = back_ref[e].astype(F32)
    returned = rows_ref[...].astype(BF16)
    rest = mix_ref[...]
    total = hidden_ref[...]
    for _ in range(3):
        part = rest.astype(BF16)
        rest = rest - part.astype(F32)
        total = total + dot(part, returned)
    steps = out_ref.shape[1]
    for b in range(out_ref.shape[0]):
        out_ref[b] = total[b * steps : (b + 1) * steps, :].astype(BF16)


def final_kernel(seq_ref, parents_ref, fresh_k_ref, fresh_v_ref, *refs):
    own_refs, (k_ref, v_ref) = refs[:-2], refs[-2:]
    steps = parents_ref.shape[0]
    here, tail = own_refs[0].shape[1], own_refs[0].shape[2]
    seq = seq_ref[0]
    for i in range(here):
        beam = seq * here + i
        for s in range(steps - 1, -1, -1):
            beam = parents_ref[s, beam]
        apart = lax.bitwise_xor(beam // here, seq)
        for j, own_ref in enumerate(own_refs):

            @pl.when(apart == j)
            def _():
                k_ref[0:tail, i, :] = own_ref[0, beam % here]
                v_ref[0:tail, i, :] = own_ref[1, beam % here]

        k_ref[tail:, i, :] = fresh_k_ref[i * steps : (i + 1) * steps, :]
        v_ref[tail:, i, :] = fresh_v_ref[i * steps : (i + 1) * steps, :]


def rotary_tables(rows, steps, start):
    half = HEAD // 2
    frequency = ROPE_BASE ** (-(np.arange(half, dtype=np.float64) * 2.0 / HEAD))
    angles = (np.arange(rows) % steps + start)[:, None] * frequency[None, :]
    cosine = np.tile(np.cos(angles), (1, 8)).astype(np.float32)
    sine = np.sin(angles)
    sine = np.tile(np.concatenate([-sine, sine], axis=1), (1, 4)).astype(np.float32)
    return cosine, sine


def block(shape):
    return pl.BlockSpec(shape, lambda i: (0,) * len(shape))


def call(kernel, outs, *args, ins=(), scratch=(), mib=48):
    specs = list(ins) + [block(a.shape) for a in args[len(ins) :]]
    return pl.pallas_call(
        kernel,
        grid=(1,),
        out_shape=outs,
        in_specs=specs,
        out_specs=jax.tree.map(lambda o: block(o.shape), outs),
        scratch_shapes=list(scratch),
        compiler_params=params(mib),
        cost_estimate=pl.CostEstimate(
            flops=1 << 20, bytes_accessed=1 << 20, transcendentals=0
        ),
    )(*args)


def shaped(shape, dtype=BF16):
    return jax.ShapeDtypeStruct(shape, dtype)


def local(
    inputs,
    parents,
    block_len,
    prompt_key_cache,
    prompt_value_cache,
    generated_key_cache,
    generated_value_cache,
    gain_attn,
    gain_moe,
    w_query,
    key_projection_weight,
    value_projection_weight,
    w_output,
    w_in,
    w_out,
    routes,
    gate_weights,
):
    def stay(a):
        return pltpu.with_memory_space_constraint(a, pltpu.MemorySpace.HBM)

    n_seq = lax.axis_size("seq")
    n_req = lax.axis_size("req")
    seq = lax.axis_index("seq").astype(jnp.int32).reshape(1)
    here, steps, width = inputs.shape[1:]
    local_rows = here * steps
    rows = local_rows * n_seq
    keys, kv_width = prompt_key_cache.shape[1:]
    tail = generated_key_cache.shape[2]
    top = routes.shape[3]
    capacity = 4
    x = stay(inputs[0])
    anywhere = pl.BlockSpec(memory_space=pl.ANY)

    def exchange(a, axis):
        return lax.all_to_all(a, axis, split_axis=0, concat_axis=0, tiled=True)

    def apart(a, distance):
        return lax.ppermute(a, "seq", [(i, i ^ distance) for i in range(n_seq)])

    normed = call(
        norm_kernel,
        shaped((n_seq, local_rows, width)),
        x,
        stay(gain_attn),
    )
    normed_all = exchange(normed, "seq")
    bias, extra = call(
        functools.partial(mask_kernel, tail, here),
        (shaped((8, keys), F32), shaped((rows, 128), F32)),
        normed,
        seq,
        parents[0],
        block_len,
        ins=[anywhere, scalars(), scalars(), scalars()],
    )
    cosine, sine = map(jnp.asarray, rotary_tables(rows, steps, keys * n_seq + tail))
    packed_rows = 2 * rows + rows // 2
    qkv = call(
        project_kernel,
        shaped((n_seq, packed_rows, 128)),
        normed_all,
        stay(w_query.T),
        stay(key_projection_weight.T),
        stay(value_projection_weight.T),
        stay(cosine),
        stay(sine),
    )
    qkv_all = exchange(qkv, "seq")

    pairs = kv_width // 128
    partial, fresh_k, fresh_v = pl.pallas_call(
        attend_kernel,
        grid=(pairs,),
        out_shape=(
            shaped((n_seq, rows, 256)),
            shaped((local_rows, kv_width)),
            shaped((local_rows, kv_width)),
        ),
        in_specs=[
            scalars(),
            scalars(),
            pl.BlockSpec((8, keys), lambda p: (0, 0)),
            pl.BlockSpec((rows, 128), lambda p: (0, 0)),
            pl.BlockSpec((2, packed_rows, 128), lambda p: (p, 0, 0)),
            pl.BlockSpec((keys, 128), lambda p: (0, p)),
            pl.BlockSpec((keys, 128), lambda p: (0, p)),
            pl.BlockSpec((here, tail, 128), lambda p: (0, 0, p)),
            pl.BlockSpec((here, tail, 128), lambda p: (0, 0, p)),
        ],
        out_specs=(
            pl.BlockSpec((2, rows, 256), lambda p: (p, 0, 0)),
            pl.BlockSpec((local_rows, 128), lambda p: (0, p)),
            pl.BlockSpec((local_rows, 128), lambda p: (0, p)),
        ),
        scratch_shapes=[
            pltpu.VMEM((6 * rows, keys + 128), F32),
            pltpu.VMEM((6 * rows, keys + 128), BF16),
        ],
        compiler_params=params(48),
        cost_estimate=pl.CostEstimate(
            flops=4 * 24 * rows * keys * HEAD,
            bytes_accessed=4 * keys * kv_width,
            transcendentals=24 * rows * keys,
        ),
    )(
        seq,
        parents[0],
        bias,
        extra,
        qkv_all,
        stay(prompt_key_cache[0]),
        stay(prompt_value_cache[0]),
        stay(generated_key_cache[0]),
        stay(generated_value_cache[0]),
    )
    parts = exchange(partial, "seq")
    sums = call(join_kernel, shaped((n_seq, local_rows, width)), parts, stay(w_output))
    slots = n_req * capacity
    place, mix = call(
        functools.partial(route_kernel, capacity),
        (shaped((slots, local_rows)), shaped((local_rows, slots), F32)),
        sums,
        stay(routes[0]),
        stay(gate_weights[0]),
        ins=[anywhere],
    )
    sums = exchange(sums, "seq")
    hidden, buffer = call(
        dispatch_kernel,
        (shaped((local_rows, width), F32), shaped((n_req, capacity, width))),
        x,
        sums,
        stay(gain_moe),
        place,
    )
    own = call(
        pack_kernel,
        shaped((2, here, tail, kv_width)),
        buffer,
        stay(generated_key_cache[0]),
        stay(generated_value_cache[0]),
        ins=[anywhere],
    )
    even = [own] + [apart(own, k) for k in range(2, n_seq, 2)]
    odd = [apart(a, 1) for a in even]
    owns = [a for pair in zip(even, odd) for a in pair]
    buffer = exchange(buffer, "req")
    back = call(
        expert_kernel,
        shaped(buffer.shape),
        buffer,
        w_in,
        stay(w_out),
        scratch=[pltpu.VMEM((slots, width), F32)],
    )
    back = exchange(back, "req")
    mixed = call(
        mix_kernel,
        shaped((here, steps, width)),
        hidden,
        mix,
        back,
        scratch=[pltpu.VMEM((slots, width), F32)],
    )
    final_k, final_v = call(
        final_kernel,
        (shaped((tail + steps, here, kv_width)),) * 2,
        seq,
        parents[0],
        fresh_k,
        fresh_v,
        *owns,
        ins=[scalars(), scalars()],
    )
    return (
        mixed[None],
        final_k.transpose(1, 0, 2)[None],
        final_v.transpose(1, 0, 2)[None],
    )


def solution(mesh):
    placed = (
        P("req", "seq", None, None),
        P("req", None, None),
        P("req", "seq"),
        P("req", "seq", None),
        P("req", "seq", None),
        P("req", "seq", None, None),
        P("req", "seq", None, None),
        P(),
        P(),
        P(None, "seq"),
        P(None, "seq"),
        P(None, "seq"),
        P("seq", None),
        P("req", None, None),
        P("req", None, None),
        P("req", "seq", None, None),
        P("req", "seq", None, None),
    )
    return jax.shard_map(
        local,
        mesh=mesh,
        in_specs=placed,
        out_specs=(P("req", "seq", None, None),) * 3,
        check_vma=False,
    )
```

```python
import functools

import jax
import jax.numpy as jnp
import numpy as np
from jax import lax
from jax.experimental import pallas as pl
from jax.experimental.pallas import tpu as pltpu
from jax.sharding import PartitionSpec as P

HEAD = 64
BLK = 128
EPSILON = 1e-05
ROPE_BASE = 10000.0
FILL = -(2.0**100)
SCALE = 0.125
BF16 = jnp.bfloat16
F32 = jnp.float32


def scalars():
    return pl.BlockSpec(memory_space=pltpu.SMEM)


def params(mib):
    return pltpu.CompilerParams(vmem_limit_bytes=mib << 20)


def dot(a, b):
    return jnp.dot(a, b, preferred_element_type=F32)


def dot_t(a, b):
    return lax.dot_general(a, b, (((1,), (1,)), ((), ())), preferred_element_type=F32)


def lanes(shape):
    return lax.broadcasted_iota(jnp.int32, shape, len(shape) - 1)


def norm(x, gain):
    mean_sq = jnp.mean(x * x, axis=-1, keepdims=True)
    return x * lax.rsqrt(mean_sq + EPSILON) * gain


def norm_kernel(x_ref, gain_ref, out_ref):
    beams, steps = x_ref.shape[0], x_ref.shape[1]
    gain = gain_ref[...].reshape(1, -1)
    rows = [norm(x_ref[b].astype(F32), gain) for b in range(beams)]
    rows = jnp.concatenate(rows, axis=0).astype(BF16)
    for d in range(out_ref.shape[0]):
        out_ref[d] = rows


def pack_kernel(order_ref, own_k_ref, own_v_ref, out_ref):
    out_ref[0] = own_k_ref[...]
    out_ref[1] = own_v_ref[...]


def swap(x):
    return pltpu.roll(x, HEAD, 1)


def even_odd(own, other, core):
    return jnp.where(core == 0, own, other), jnp.where(core == 0, other, own)


def project_kernel(
    x_ref,
    seq_ref,
    wq_ref,
    wk_ref,
    wv_ref,
    other_wq_ref,
    other_wk_ref,
    other_wv_ref,
    cos_ref,
    sin_ref,
    q_ref,
    kv_ref,
):
    core = seq_ref[0] % 2
    rows = x_ref.shape[0] * x_ref.shape[1]
    x = x_ref[...].reshape(rows, x_ref.shape[2])
    half = HEAD // 2

    def turned(wq, wk):
        y = jnp.concatenate([dot_t(x, wq) * SCALE, dot_t(x, wk)], axis=1)
        first = lanes(y.shape) % HEAD < half
        width = y.shape[1]
        turn = jnp.where(first, pltpu.roll(y, width - half, 1), pltpu.roll(y, half, 1))
        return y * cos_ref[...] + turn * sin_ref[...]

    y = turned(wq_ref[...], wk_ref[...])
    z = turned(other_wq_ref[...], other_wk_ref[...])
    even, odd = even_odd(y, z, core)
    v_even, v_odd = even_odd(dot_t(x, wv_ref[...]), dot_t(x, other_wv_ref[...]), core)
    low = lanes((rows, 128)) < HEAD
    e0, e1, o0, o1 = even[:, 0:128], even[:, 128:256], odd[:, 0:128], odd[:, 128:256]
    tiles = [
        jnp.where(low, e0, swap(o0)),
        jnp.where(low, swap(e0), o0),
        jnp.where(low, e1, swap(o1)),
    ]
    q = jnp.concatenate(tiles, axis=0).astype(BF16)
    for d in range(q_ref.shape[0]):
        q_ref[d] = q
    kv_ref[0] = jnp.where(low, swap(e1), o1).astype(BF16)
    kv_ref[1] = jnp.concatenate([v_even, v_odd], axis=1).astype(BF16)


def lookup(parents_ref, step, cur, beams):
    found = jnp.zeros(cur.shape, jnp.int32)
    for b in range(beams):
        found = jnp.where(cur == b, parents_ref[step, b], found)
    return found


def mask_kernel(
    tail,
    here,
    order_ref,
    seq_ref,
    parents_ref,
    len_ref,
    other_len_ref,
    bias_ref,
    extra_ref,
    fresh_ref,
    final_ref,
):
    steps, beams = parents_ref.shape
    seq = seq_ref[0]
    core = seq % 2
    other = seq + 1 - 2 * core
    shape = extra_ref.shape
    rows = shape[0]
    lane = lanes(shape)
    spot = lanes((bias_ref.shape[0], BLK))
    half = bias_ref.shape[1] // 2
    for source, start in ((len_ref, 0), (other_len_ref, half)):
        for j in range(half // BLK):
            at = start + j * BLK
            bias_ref[:, at : at + BLK] = jnp.where(spot < source[0, j], 0.0, FILL)
    row = lax.broadcasted_iota(jnp.int32, shape, 0)

    def beam_of(place, parity):
        return (place // (here * steps)) * 2 * here + parity * here + place // steps % here

    step = row % steps
    key = lane % rows
    key_beam = beam_of(key, jnp.where(lane < rows, core, 1 - core))
    key_step = key % steps
    real = lane < 2 * rows
    cur = beam_of(row, core)
    end = cur
    live = jnp.zeros(shape, jnp.int32)
    chosen = jnp.zeros(shape, jnp.int32)
    for s in range(steps - 1, -1, -1):
        here_now = real & (key_step == s)
        live = live | jnp.where(here_now & (cur == key_beam) & (step >= s), 1, 0)
        chosen = chosen | jnp.where(here_now & (end == key_beam) & (step == s), 1, 0)
        cur = jnp.where(step >= s, lookup(parents_ref, s, cur, beams), cur)
        end = jnp.where(step < s, lookup(parents_ref, s, end, beams), end)
    fresh_ref[...] = jnp.where(live > 0, 0.0, FILL)
    final_ref[...] = jnp.where(chosen > 0, 1.0, 0.0).astype(BF16)
    own_keys = here * tail
    holder = jnp.where(lane < own_keys, seq, other)
    own_beam = holder * here + lane % own_keys // tail
    extra_ref[...] = jnp.where((lane < 2 * own_keys) & (cur == own_beam), 0.0, FILL)


def split_heads(q_ref, rows):
    low = lanes((3 * rows, 128)) < HEAD
    q = q_ref[...].reshape(3 * rows, 128).astype(F32)
    both = [jnp.where(low, q, 0.0), jnp.where(low, 0.0, q)]
    return jnp.concatenate(both, axis=0).astype(BF16)


def pack_partial(o, total, lse, rows, store):
    lane = lanes((rows, 128))
    low = lane < HEAD
    stats = jnp.zeros((rows, 128), F32)
    for i in range(6):
        rest = lse[i]
        for piece in range(3):
            part = rest.astype(BF16).astype(F32)
            rest = rest - part
            stats = jnp.where(lane == 3 * i + piece, part, stats)
    for j in range(3):
        even = o[j * rows : (j + 1) * rows, :] / total[j]
        odd = o[(3 + j) * rows : (4 + j) * rows, :] / total[3 + j]
        store(j, jnp.where(low, even, odd).astype(BF16))
    store(3, stats.astype(BF16))


def fresh_kernel(q_ref, kv_ref, other_ref, bias_ref, final_ref, out_ref, pick_ref):
    rows = kv_ref.shape[1]
    q = split_heads(q_ref.at[0], rows)
    fill = jnp.zeros((128 - 2 * rows, 128), BF16)
    k = jnp.concatenate([kv_ref[0], other_ref[0], fill], axis=0)
    v = jnp.concatenate([kv_ref[1], other_ref[1], fill], axis=0)
    s = dot_t(q, k)
    probs, total, lse = [], [], []
    for i in range(6):
        piece = s[i * rows : (i + 1) * rows, :] + bias_ref[...]
        top = jnp.max(piece, axis=-1, keepdims=True)
        e = jnp.exp(piece - top)
        total.append(jnp.sum(e, axis=-1, keepdims=True))
        lse.append(top + jnp.log(total[i]))
        probs.append(e.astype(BF16))
    o = dot(jnp.concatenate(probs, axis=0), v)

    def store(j, tile):
        out_ref[:, j * 128 : (j + 1) * 128] = tile

    pack_partial(o, total, lse, rows, store)
    pick_k = dot(final_ref[...], k).astype(BF16)
    pick_v = dot(final_ref[...], v).astype(BF16)
    each = pick_ref.shape[1]
    for d in range(pick_ref.shape[0]):
        pick_ref[d, :, 0:128] = pick_k[d * each : (d + 1) * each, :]
        pick_ref[d, :, 128:256] = pick_v[d * each : (d + 1) * each, :]
        pick_ref[d, :, 256:512] = jnp.zeros((each, 256), BF16)


def attend_kernel(
    bias_ref,
    extra_ref,
    q_ref,
    k_ref,
    v_ref,
    other_k_ref,
    other_v_ref,
    own_ref,
    other_own_ref,
    pick_ref,
    out_ref,
    s_ref,
    p_ref,
):
    rows = extra_ref.shape[0]
    half = k_ref.shape[0]
    keys = 2 * half
    own_keys = own_ref.shape[1] * own_ref.shape[2]
    q = split_heads(q_ref.at[0], rows)
    fill = jnp.zeros((128 - 2 * own_keys, 128), BF16)
    extra = [
        jnp.concatenate(
            [
                own_ref[i].reshape(own_keys, 128),
                other_own_ref[i].reshape(own_keys, 128),
                fill,
            ],
            axis=0,
        )
        for i in range(2)
    ]
    s_ref[:, 0:half] = dot_t(q, k_ref[...])
    s_ref[:, half:keys] = dot_t(q, other_k_ref[...])
    s_ref[:, keys : keys + 128] = dot_t(q, extra[0])
    lse, total = [], []
    for i in range(6):
        span = slice(i * rows, (i + 1) * rows)
        s0 = s_ref[span, 0:keys] + bias_ref[0:1, :]
        s1 = s_ref[span, keys : keys + 128] + extra_ref[...]
        top = jnp.maximum(
            jnp.max(s0, axis=-1, keepdims=True), jnp.max(s1, axis=-1, keepdims=True)
        )
        e0 = jnp.exp(s0 - top)
        e1 = jnp.exp(s1 - top)
        p_ref[span, 0:keys] = e0.astype(BF16)
        p_ref[span, keys : keys + 128] = e1.astype(BF16)
        denominator = jnp.sum(e0, axis=-1, keepdims=True) + jnp.sum(e1, axis=-1, keepdims=True)
        total.append(denominator)
        lse.append(top + jnp.log(denominator))
    o = dot(p_ref[:, 0:half], v_ref[...]) + dot(p_ref[:, half:keys], other_v_ref[...])
    o = o + dot(p_ref[:, keys : keys + 128], extra[1])

    def store(j, tile):
        out_ref[0, 0:rows, j * 128 : (j + 1) * 128] = tile

    pack_partial(o, total, lse, rows, store)
    out_ref[0, rows:, :] = pick_ref[0]


def join_kernel(part_ref, fresh_ref, seq_ref, w_ref, other_w_ref, out_ref):
    sources, rows = part_ref.shape[0], fresh_ref.shape[0]
    core = seq_ref[0] % 2
    low = lanes((rows, 128)) < HEAD

    def tile(s, j):
        span = slice(j * 128, (j + 1) * 128)
        source = fresh_ref[:, span] if s == sources else part_ref[s, 0:rows, span]
        return source.astype(F32)

    stats = [tile(s, 3) for s in range(sources + 1)]
    lse = [x + pltpu.roll(x, 127, 1) + pltpu.roll(x, 126, 1) for x in stats]
    top = functools.reduce(jnp.maximum, lse)
    weight = [jnp.exp(x - top) for x in lse]
    inverse = 1.0 / functools.reduce(jnp.add, weight)
    out = jnp.zeros((rows, w_ref.shape[1]), F32)
    for j in range(3):
        total = jnp.zeros((rows, 128), F32)
        for s in range(sources + 1):
            w = weight[s] * inverse
            even, odd = w[:, 3 * j : 3 * j + 1], w[:, 9 + 3 * j : 10 + 3 * j]
            total = total + tile(s, j) * jnp.where(low, even, odd)
        total = jnp.where(core == 0, total, swap(total)).astype(BF16)
        span = slice(j * HEAD, (j + 1) * HEAD)
        out = out + dot(total, jnp.concatenate([w_ref[span, :], other_w_ref[span, :]], axis=0))
    out = out.astype(BF16)
    each = rows // sources
    for s in range(sources):
        out_ref[s] = out[s * each : (s + 1) * each, :]


def route_kernel(capacity, order_ref, route_ref, gate_ref, place_ref, mix_ref):
    beams, steps = route_ref.shape[0], route_ref.shape[1]
    rows = beams * steps
    slots = place_ref.shape[0]
    slot = lanes((rows, slots))
    routes = jnp.concatenate([route_ref[b] for b in range(beams)], axis=0)
    gates = jnp.concatenate([gate_ref[b] for b in range(beams)], axis=0)
    named = jnp.zeros((rows, slots), F32)
    gate = jnp.zeros((rows, slots), F32)
    for j in range(routes.shape[1]):
        hit = routes[:, j : j + 1] == slot // capacity
        named = jnp.where(hit, 1.0, named)
        gate = jnp.where(hit, gates[:, j : j + 1], gate)
    earlier = jnp.where(
        lanes((rows, rows)) < lax.broadcasted_iota(jnp.int32, (rows, rows), 0), 1.0, 0.0
    )
    rank = dot(earlier.astype(BF16), named.astype(BF16))
    placed = (named > 0.0) & (rank == (slot % capacity).astype(F32))
    mix_ref[...] = jnp.where(placed, gate, 0.0)
    place_ref[...] = jnp.where(placed, 1.0, 0.0).T.astype(BF16)


def dispatch_kernel(x_ref, sums_ref, gain_ref, place_ref, hidden_ref, out_ref):
    beams = x_ref.shape[0]
    total = sums_ref[0].astype(F32)
    for s in range(1, sums_ref.shape[0]):
        total = total + sums_ref[s].astype(F32)
    inputs = jnp.concatenate([x_ref[b].astype(F32) for b in range(beams)], axis=0)
    hidden = inputs + total
    hidden_ref[...] = hidden
    expert_in = norm(hidden, gain_ref[...].reshape(1, -1)).astype(BF16)
    buffer = dot(place_ref[...], expert_in)
    experts, capacity = out_ref.shape[0], out_ref.shape[1]
    for e in range(experts):
        out_ref[e] = buffer[e * capacity : (e + 1) * capacity, :].astype(BF16)


def expert_kernel(x_ref, w_in_ref, w_out_ref, out_ref, rows_ref):
    sources, capacity = x_ref.shape[0], x_ref.shape[1]
    for s in range(sources):
        rows_ref[s * capacity : (s + 1) * capacity, :] = x_ref[s].astype(F32)
    projected = dot(rows_ref[...].astype(BF16), w_in_ref[0])
    half = projected.shape[1] // 2
    g, u = projected[:, 0:half], projected[:, half:]
    act = (g * jax.nn.sigmoid(g) * u).astype(BF16)
    out = dot(act, w_out_ref[0])
    for s in range(sources):
        out_ref[s] = out[s * capacity : (s + 1) * capacity, :].astype(BF16)


def mix_kernel(hidden_ref, mix_ref, back_ref, out_ref, rows_ref):
    experts, capacity = back_ref.shape[0], back_ref.shape[1]
    for e in range(experts):
        rows_ref[e * capacity : (e + 1) * capacity, :] = back_ref[e].astype(F32)
    returned = rows_ref[...].astype(BF16)
    rest = mix_ref[...]
    total = hidden_ref[...]
    for _ in range(3):
        part = rest.astype(BF16)
        rest = rest - part.astype(F32)
        total = total + dot(part, returned)
    steps = out_ref.shape[1]
    for b in range(out_ref.shape[0]):
        out_ref[b] = total[b * steps : (b + 1) * steps, :].astype(BF16)


def final_kernel(seq_ref, parents_ref, part_ref, *refs):
    own_refs, (k_ref, v_ref) = refs[:-2], refs[-2:]
    steps = parents_ref.shape[0]
    here, tail = own_refs[0].shape[1], own_refs[0].shape[2]
    start = part_ref.shape[1] - here * steps
    seq = seq_ref[0]
    for i in range(here):
        beam = seq * here + i
        for s in range(steps - 1, -1, -1):
            beam = parents_ref[s, beam]
        apart = lax.bitwise_xor(beam // here, seq)
        for j, own_ref in enumerate(own_refs):

            @pl.when(apart == j)
            def _():
                k_ref[0:tail, i, :] = own_ref[0, beam % here]
                v_ref[0:tail, i, :] = own_ref[1, beam % here]

        span = slice(start + i * steps, start + (i + 1) * steps)
        for p in range(part_ref.shape[0]):
            k_ref[tail:, i, p * 128 : (p + 1) * 128] = part_ref[p, span, 0:128]
            v_ref[tail:, i, p * 128 : (p + 1) * 128] = part_ref[p, span, 128:256]


def rotary_tables(rows, steps, start):
    half = HEAD // 2
    frequency = ROPE_BASE ** (-(np.arange(half, dtype=np.float64) * 2.0 / HEAD))
    angles = (np.arange(rows) % steps + start)[:, None] * frequency[None, :]
    cosine = np.tile(np.cos(angles), (1, 8)).astype(np.float32)
    sine = np.sin(angles)
    sine = np.tile(np.concatenate([-sine, sine], axis=1), (1, 4)).astype(np.float32)
    return cosine, sine


def block(shape):
    return pl.BlockSpec(shape, lambda i: (0,) * len(shape))


def call(kernel, outs, *args, ins=(), scratch=(), mib=48):
    specs = list(ins) + [block(a.shape) for a in args[len(ins) :]]
    return pl.pallas_call(
        kernel,
        grid=(1,),
        out_shape=outs,
        in_specs=specs,
        out_specs=jax.tree.map(lambda o: block(o.shape), outs),
        scratch_shapes=list(scratch),
        compiler_params=params(mib),
        cost_estimate=pl.CostEstimate(
            flops=1 << 20, bytes_accessed=1 << 20, transcendentals=0
        ),
    )(*args)


def shaped(shape, dtype=BF16):
    return jax.ShapeDtypeStruct(shape, dtype)


def local(
    inputs,
    parents,
    block_len,
    prompt_key_cache,
    prompt_value_cache,
    generated_key_cache,
    generated_value_cache,
    gain_attn,
    gain_moe,
    w_query,
    key_projection_weight,
    value_projection_weight,
    w_output,
    w_in,
    w_out,
    routes,
    gate_weights,
):
    def stay(a):
        return pltpu.with_memory_space_constraint(a, pltpu.MemorySpace.HBM)

    n_seq = lax.axis_size("seq")
    n_req = lax.axis_size("req")
    n_chips = n_seq // 2
    seq = lax.axis_index("seq").astype(jnp.int32).reshape(1)
    here, steps, width = inputs.shape[1:]
    local_rows = here * steps
    rows = local_rows * n_chips
    keys, kv_width = prompt_key_cache.shape[1:]
    tail = generated_key_cache.shape[2]
    capacity = 4
    x = stay(inputs[0])
    anywhere = pl.BlockSpec(memory_space=pl.ANY)
    same_core = [[2 * z + core for z in range(n_chips)] for core in range(2)]

    def exchange(a, axis):
        return lax.all_to_all(a, axis, split_axis=0, concat_axis=0, tiled=True)

    def exchange_chips(a):
        return lax.all_to_all(
            a, "seq", split_axis=0, concat_axis=0, tiled=True, axis_index_groups=same_core
        )

    def apart(a, distance):
        return lax.ppermute(a, "seq", [(i, i ^ distance) for i in range(n_seq)])

    def of_other_core(a):
        return apart(a, 1)

    normed = call(norm_kernel, shaped((n_chips, local_rows, width)), x, stay(gain_attn))
    normed_all = exchange_chips(normed)
    weights = [w_query.T, key_projection_weight.T, value_projection_weight.T]
    other_weights = [of_other_core(w) for w in weights]
    prompt = [prompt_key_cache[0], prompt_value_cache[0]]
    other_prompt = [of_other_core(a) for a in prompt]
    other_w_output = of_other_core(w_output)
    own = call(
        pack_kernel,
        shaped((2, here, tail, kv_width)),
        normed,
        stay(generated_key_cache[0]),
        stay(generated_value_cache[0]),
        ins=[anywhere],
    )
    other_own = apart(own, 1)
    bias, extra, fresh_bias, final = call(
        functools.partial(mask_kernel, tail, here),
        (
            shaped((8, 2 * keys), F32),
            shaped((rows, 128), F32),
            shaped((rows, 128), F32),
            shaped((rows, 128)),
        ),
        normed,
        seq,
        parents[0],
        block_len,
        apart(block_len, 1),
        ins=[anywhere, scalars(), scalars(), scalars(), scalars()],
    )
    cosine, sine = map(jnp.asarray, rotary_tables(rows, steps, keys * n_seq + tail))
    q, kv = call(
        project_kernel,
        (shaped((n_chips, 3 * rows, 128)), shaped((2, rows, 128))),
        normed_all,
        seq,
        *[stay(w) for w in weights],
        *other_weights,
        stay(cosine),
        stay(sine),
        ins=[block(normed_all.shape), scalars()],
    )
    q_all = exchange_chips(q)
    fresh, pick = call(
        fresh_kernel,
        (shaped((rows, 512)), shaped((n_chips, local_rows, 512))),
        q,
        kv,
        apart(kv, 1),
        fresh_bias,
        final,
    )

    held = pl.BlockSpec((keys, 128), lambda p: (0, p))
    held_own = pl.BlockSpec((2, here, tail, 128), lambda p: (0, 0, 0, p))
    partial = pl.pallas_call(
        attend_kernel,
        grid=(kv_width // 128,),
        out_shape=shaped((n_chips, rows + local_rows, 512)),
        in_specs=[
            pl.BlockSpec((8, 2 * keys), lambda p: (0, 0)),
            pl.BlockSpec((rows, 128), lambda p: (0, 0)),
            pl.BlockSpec((1, 3 * rows, 128), lambda p: (p, 0, 0)),
            held,
            held,
            held,
            held,
            held_own,
            held_own,
            pl.BlockSpec((1, local_rows, 512), lambda p: (p, 0, 0)),
        ],
        out_specs=pl.BlockSpec((1, rows + local_rows, 512), lambda p: (p, 0, 0)),
        scratch_shapes=[
            pltpu.VMEM((6 * rows, 2 * keys + 128), F32),
            pltpu.VMEM((6 * rows, 2 * keys + 128), BF16),
        ],
        compiler_params=params(48),
        cost_estimate=pl.CostEstimate(
            flops=4 * 24 * rows * 2 * keys * HEAD,
            bytes_accessed=8 * keys * kv_width,
            transcendentals=24 * rows * 2 * keys,
        ),
    )(bias, extra, q_all, *map(stay, prompt), *other_prompt, own, other_own, pick)
    parts = exchange_chips(partial)
    sums = call(
        join_kernel,
        shaped((n_chips, local_rows, width)),
        parts,
        fresh,
        seq,
        stay(w_output),
        other_w_output,
        ins=[block(parts.shape), block(fresh.shape), scalars()],
    )
    slots = n_req * capacity
    place, mix = call(
        functools.partial(route_kernel, capacity),
        (shaped((slots, local_rows)), shaped((local_rows, slots), F32)),
        sums,
        stay(routes[0]),
        stay(gate_weights[0]),
        ins=[anywhere],
    )
    sums = exchange_chips(sums)
    hidden, buffer = call(
        dispatch_kernel,
        (shaped((local_rows, width), F32), shaped((n_req, capacity, width))),
        x,
        sums,
        stay(gain_moe),
        place,
    )
    own, buffer = lax.optimization_barrier((own, buffer))
    even = [own] + [apart(own, k) for k in range(2, n_seq, 2)]
    buffer = exchange(buffer, "req")
    back = call(
        expert_kernel,
        shaped(buffer.shape),
        buffer,
        stay(w_in),
        stay(w_out),
        scratch=[pltpu.VMEM((slots, width), F32)],
    )
    back, *even = lax.optimization_barrier((back, *even))
    odd = [other_own] + [apart(a, 1) for a in even[1:]]
    owns = [a for pair in zip(even, odd) for a in pair]
    back = exchange(back, "req")
    mixed = call(
        mix_kernel,
        shaped((here, steps, width)),
        hidden,
        mix,
        back,
        scratch=[pltpu.VMEM((slots, width), F32)],
    )
    final_k, final_v = call(
        final_kernel,
        (shaped((tail + steps, here, kv_width)),) * 2,
        seq,
        parents[0],
        parts,
        *owns,
        ins=[scalars(), scalars()],
    )
    return (
        mixed[None],
        final_k.transpose(1, 0, 2)[None],
        final_v.transpose(1, 0, 2)[None],
    )


def solution(mesh):
    placed = (
        P("req", "seq", None, None),
        P("req", None, None),
        P("req", "seq"),
        P("req", "seq", None),
        P("req", "seq", None),
        P("req", "seq", None, None),
        P("req", "seq", None, None),
        P(),
        P(),
        P(None, "seq"),
        P(None, "seq"),
        P(None, "seq"),
        P("seq", None),
        P("req", None, None),
        P("req", None, None),
        P("req", "seq", None, None),
        P("req", "seq", None, None),
    )
    return jax.shard_map(
        local,
        mesh=mesh,
        in_specs=placed,
        out_specs=(P("req", "seq", None, None),) * 3,
        check_vma=False,
    )
```

```python
import functools

import jax
import jax.numpy as jnp
import numpy as np
from jax import lax
from jax.experimental import pallas as pl
from jax.experimental.pallas import tpu as pltpu
from jax.sharding import PartitionSpec as P

HEAD = 64
BLK = 128
EPSILON = 1e-05
ROPE_BASE = 10000.0
FILL = -(2.0**100)
SCALE = 0.125
BF16 = jnp.bfloat16
F32 = jnp.float32


def scalars():
    return pl.BlockSpec(memory_space=pltpu.SMEM)


def params(mib):
    return pltpu.CompilerParams(vmem_limit_bytes=mib << 20)


def dot(a, b):
    return jnp.dot(a, b, preferred_element_type=F32)


def dot_t(a, b):
    return lax.dot_general(a, b, (((1,), (1,)), ((), ())), preferred_element_type=F32)


def lanes(shape):
    return lax.broadcasted_iota(jnp.int32, shape, len(shape) - 1)


def norm(x, gain):
    mean_sq = jnp.mean(x * x, axis=-1, keepdims=True)
    return x * lax.rsqrt(mean_sq + EPSILON) * gain


def norm_kernel(x_ref, gain_ref, out_ref):
    beams, steps = x_ref.shape[0], x_ref.shape[1]
    gain = gain_ref[...].reshape(1, -1)
    rows = [norm(x_ref[b].astype(F32), gain) for b in range(beams)]
    rows = jnp.concatenate(rows, axis=0).astype(BF16)
    for d in range(out_ref.shape[0]):
        out_ref[d] = rows


def pack_kernel(order_ref, own_k_ref, own_v_ref, out_ref):
    out_ref[0] = own_k_ref[...]
    out_ref[1] = own_v_ref[...]


def swap(x):
    return pltpu.roll(x, HEAD, 1)


def even_odd(own, other, core):
    return jnp.where(core == 0, own, other), jnp.where(core == 0, other, own)


def project_kernel(
    x_ref,
    seq_ref,
    wq_ref,
    wk_ref,
    wv_ref,
    other_wq_ref,
    other_wk_ref,
    other_wv_ref,
    cos_ref,
    sin_ref,
    q_ref,
    kv_ref,
):
    core = seq_ref[0] % 2
    rows = x_ref.shape[0] * x_ref.shape[1]
    x = x_ref[...].reshape(rows, x_ref.shape[2])
    half = HEAD // 2

    def turned(wq, wk):
        y = jnp.concatenate([dot_t(x, wq) * SCALE, dot_t(x, wk)], axis=1)
        first = lanes(y.shape) % HEAD < half
        width = y.shape[1]
        turn = jnp.where(first, pltpu.roll(y, width - half, 1), pltpu.roll(y, half, 1))
        return y * cos_ref[...] + turn * sin_ref[...]

    y = turned(wq_ref[...], wk_ref[...])
    z = turned(other_wq_ref[...], other_wk_ref[...])
    even, odd = even_odd(y, z, core)
    v_even, v_odd = even_odd(dot_t(x, wv_ref[...]), dot_t(x, other_wv_ref[...]), core)
    low = lanes((rows, 128)) < HEAD
    e0, e1, o0, o1 = even[:, 0:128], even[:, 128:256], odd[:, 0:128], odd[:, 128:256]
    tiles = [
        jnp.where(low, e0, swap(o0)),
        jnp.where(low, swap(e0), o0),
        jnp.where(low, e1, swap(o1)),
    ]
    q = jnp.concatenate(tiles, axis=0).astype(BF16)
    for d in range(q_ref.shape[0]):
        q_ref[d] = q
    kv_ref[0] = jnp.where(low, swap(e1), o1).astype(BF16)
    kv_ref[1] = jnp.concatenate([v_even, v_odd], axis=1).astype(BF16)


def lookup(parents_ref, step, cur, beams):
    found = jnp.zeros(cur.shape, jnp.int32)
    for b in range(beams):
        found = jnp.where(cur == b, parents_ref[step, b], found)
    return found


def mask_kernel(
    tail,
    here,
    order_ref,
    seq_ref,
    parents_ref,
    len_ref,
    other_len_ref,
    bias_ref,
    extra_ref,
    fresh_ref,
    final_ref,
):
    steps, beams = parents_ref.shape
    seq = seq_ref[0]
    core = seq % 2
    other = seq + 1 - 2 * core
    shape = extra_ref.shape
    rows = shape[0]
    lane = lanes(shape)
    spot = lanes((bias_ref.shape[0], BLK))
    half = bias_ref.shape[1] // 2
    for source, start in ((len_ref, 0), (other_len_ref, half)):
        for j in range(half // BLK):
            at = start + j * BLK
            bias_ref[:, at : at + BLK] = jnp.where(spot < source[0, j], 0.0, FILL)
    row = lax.broadcasted_iota(jnp.int32, shape, 0)

    def beam_of(place, parity):
        return (place // (here * steps)) * 2 * here + parity * here + place // steps % here

    step = row % steps
    key = lane % rows
    key_beam = beam_of(key, jnp.where(lane < rows, core, 1 - core))
    key_step = key % steps
    real = lane < 2 * rows
    cur = beam_of(row, core)
    end = cur
    live = jnp.zeros(shape, jnp.int32)
    chosen = jnp.zeros(shape, jnp.int32)
    for s in range(steps - 1, -1, -1):
        here_now = real & (key_step == s)
        live = live | jnp.where(here_now & (cur == key_beam) & (step >= s), 1, 0)
        chosen = chosen | jnp.where(here_now & (end == key_beam) & (step == s), 1, 0)
        cur = jnp.where(step >= s, lookup(parents_ref, s, cur, beams), cur)
        end = jnp.where(step < s, lookup(parents_ref, s, end, beams), end)
    fresh_ref[...] = jnp.where(live > 0, 0.0, FILL)
    final_ref[...] = jnp.where(chosen > 0, 1.0, 0.0).astype(BF16)
    own_keys = here * tail
    holder = jnp.where(lane < own_keys, seq, other)
    own_beam = holder * here + lane % own_keys // tail
    extra_ref[...] = jnp.where((lane < 2 * own_keys) & (cur == own_beam), 0.0, FILL)


def split_heads(q_ref, rows):
    low = lanes((3 * rows, 128)) < HEAD
    q = q_ref[...].reshape(3 * rows, 128).astype(F32)
    both = [jnp.where(low, q, 0.0), jnp.where(low, 0.0, q)]
    return jnp.concatenate(both, axis=0).astype(BF16)


def pack_partial(o, total, lse, rows, store):
    lane = lanes((rows, 128))
    low = lane < HEAD
    stats = jnp.zeros((rows, 128), F32)
    for i in range(6):
        rest = lse[i]
        for piece in range(3):
            part = rest.astype(BF16).astype(F32)
            rest = rest - part
            stats = jnp.where(lane == 3 * i + piece, part, stats)
    for j in range(3):
        even = o[j * rows : (j + 1) * rows, :] / total[j]
        odd = o[(3 + j) * rows : (4 + j) * rows, :] / total[3 + j]
        store(j, jnp.where(low, even, odd).astype(BF16))
    store(3, stats.astype(BF16))


def fresh_kernel(q_ref, kv_ref, other_ref, bias_ref, final_ref, out_ref, pick_ref):
    rows = kv_ref.shape[1]
    q = split_heads(q_ref.at[0], rows)
    fill = jnp.zeros((128 - 2 * rows, 128), BF16)
    k = jnp.concatenate([kv_ref[0], other_ref[0], fill], axis=0)
    v = jnp.concatenate([kv_ref[1], other_ref[1], fill], axis=0)
    s = dot_t(q, k)
    probs, total, lse = [], [], []
    for i in range(6):
        piece = s[i * rows : (i + 1) * rows, :] + bias_ref[...]
        top = jnp.max(piece, axis=-1, keepdims=True)
        e = jnp.exp(piece - top)
        total.append(jnp.sum(e, axis=-1, keepdims=True))
        lse.append(top + jnp.log(total[i]))
        probs.append(e.astype(BF16))
    o = dot(jnp.concatenate(probs, axis=0), v)

    def store(j, tile):
        out_ref[:, j * 128 : (j + 1) * 128] = tile

    pack_partial(o, total, lse, rows, store)
    pick_k = dot(final_ref[...], k).astype(BF16)
    pick_v = dot(final_ref[...], v).astype(BF16)
    each = pick_ref.shape[1]
    for d in range(pick_ref.shape[0]):
        pick_ref[d, :, 0:128] = pick_k[d * each : (d + 1) * each, :]
        pick_ref[d, :, 128:256] = pick_v[d * each : (d + 1) * each, :]
        pick_ref[d, :, 256:512] = jnp.zeros((each, 256), BF16)


def attend_kernel(
    bias_ref,
    extra_ref,
    q_ref,
    own_ref,
    other_own_ref,
    pick_ref,
    *refs,
):
    sources, out_ref, held = refs[0:4], refs[4], refs[5:9]
    score_refs, prob_refs, top_ref, sem = refs[9:11], refs[11:13], refs[13], refs[14]
    k_ref, v_ref, other_k_ref, other_v_ref = held
    rows = extra_ref.shape[0]
    half = k_ref.shape[0]
    keys = 2 * half
    own_keys = own_ref.shape[1] * own_ref.shape[2]
    pairs = q_ref.shape[0]
    chunk = 512
    chunks = keys // chunk
    fill = jnp.zeros((128 - 2 * own_keys, 128), BF16)

    def lane_span(pair):
        return slice(pair * 128, (pair + 1) * 128)

    copies = {}
    for pair in range(pairs):
        for i in (0, 2, 1, 3):
            copies[pair, i] = pltpu.make_async_copy(
                sources[i].at[:, lane_span(pair)], held[i].at[:, lane_span(pair)], sem.at[pair, i]
            )
            copies[pair, i].start()

    def extra(pair, i):
        both = [r[i, :, :, lane_span(pair)].reshape(own_keys, 128) for r in (own_ref, other_own_ref)]
        return jnp.concatenate([*both, fill], axis=0)

    def fold(x):
        tiles = [x[:, at : at + 128] for at in range(0, x.shape[1], 128)]
        return functools.reduce(jnp.maximum, tiles)

    queries = {}

    def score(pair, i):
        s_ref = score_refs[pair % 2]
        if i == 0:
            copies[pair, 0].wait()
            queries[pair] = split_heads(q_ref.at[pair], rows)
            s = dot_t(queries[pair], extra(pair, 0))
            s = s + jnp.concatenate([extra_ref[...]] * 6, axis=0)
            s_ref[:, keys:] = s
            top = s
        else:
            top = top_ref[...]
        at = i * chunk
        source, start = (k_ref, at) if at < half else (other_k_ref, at - half)
        if at == half:
            copies[pair, 2].wait()
        s = dot_t(queries[pair], source[start : start + chunk, lane_span(pair)])
        s = s + bias_ref[0:1, at : at + chunk]
        s_ref[:, at : at + chunk] = s
        top_ref[...] = jnp.maximum(top, fold(s))

    tops, totals = {}, {}

    def soften(pair, i):
        s_ref, p_ref = score_refs[pair % 2], prob_refs[pair % 2]
        span = slice(i * rows, (i + 1) * rows)
        top = tops[pair][span, :]
        total = jnp.zeros((rows, 128), F32)
        for at in range(0, keys + 128, 128):
            e = jnp.exp(s_ref[span, at : at + 128] - top)
            total = total + e
            p_ref[span, at : at + 128] = e.astype(BF16)
        totals[pair, i] = jnp.sum(total, axis=-1, keepdims=True)

    summed = {}

    def weigh(pair, part):
        p_ref = prob_refs[pair % 2]
        copies[pair, 1 + 2 * part].wait()
        if part == 0:
            summed[pair] = dot(p_ref[:, 0:half], v_ref[:, lane_span(pair)])
            return
        o = summed[pair] + dot(p_ref[:, half:keys], other_v_ref[:, lane_span(pair)])
        o = o + dot(p_ref[:, keys:], extra(pair, 1))
        total = [totals[pair, i] for i in range(6)]
        lse = [tops[pair][i * rows : (i + 1) * rows, :] + jnp.log(total[i]) for i in range(6)]

        def store(j, tile):
            out_ref[pair, 0:rows, lane_span(j)] = tile

        pack_partial(o, total, lse, rows, store)
        out_ref[pair, rows:, :] = pick_ref[pair]

    for turn in range(pairs + 2):
        for i in range(chunks):
            if turn < pairs:
                score(turn, i)
            if 0 <= turn - 1 < pairs and i < 6:
                soften(turn - 1, i)
            if turn >= 2 and i in (3, 6):
                weigh(turn - 2, 0 if i == 3 else 1)
        if turn < pairs:
            tops[turn] = jnp.max(top_ref[...], axis=-1, keepdims=True)


def join_kernel(part_ref, fresh_ref, seq_ref, w_ref, other_w_ref, out_ref):
    sources, rows = part_ref.shape[0], fresh_ref.shape[0]
    core = seq_ref[0] % 2
    low = lanes((rows, 128)) < HEAD

    def tile(s, j):
        span = slice(j * 128, (j + 1) * 128)
        source = fresh_ref[:, span] if s == sources else part_ref[s, 0:rows, span]
        return source.astype(F32)

    stats = [tile(s, 3) for s in range(sources + 1)]
    lse = [x + pltpu.roll(x, 127, 1) + pltpu.roll(x, 126, 1) for x in stats]
    top = functools.reduce(jnp.maximum, lse)
    weight = [jnp.exp(x - top) for x in lse]
    inverse = 1.0 / functools.reduce(jnp.add, weight)
    out = jnp.zeros((rows, w_ref.shape[1]), F32)
    for j in range(3):
        total = jnp.zeros((rows, 128), F32)
        for s in range(sources + 1):
            w = weight[s] * inverse
            even, odd = w[:, 3 * j : 3 * j + 1], w[:, 9 + 3 * j : 10 + 3 * j]
            total = total + tile(s, j) * jnp.where(low, even, odd)
        total = jnp.where(core == 0, total, swap(total)).astype(BF16)
        span = slice(j * HEAD, (j + 1) * HEAD)
        out = out + dot(total, jnp.concatenate([w_ref[span, :], other_w_ref[span, :]], axis=0))
    out = out.astype(BF16)
    each = rows // sources
    for s in range(sources):
        out_ref[s] = out[s * each : (s + 1) * each, :]


def route_kernel(capacity, order_ref, route_ref, gate_ref, place_ref, mix_ref):
    beams, steps = route_ref.shape[0], route_ref.shape[1]
    rows = beams * steps
    slots = place_ref.shape[0]
    slot = lanes((rows, slots))
    routes = jnp.concatenate([route_ref[b] for b in range(beams)], axis=0)
    gates = jnp.concatenate([gate_ref[b] for b in range(beams)], axis=0)
    named = jnp.zeros((rows, slots), F32)
    gate = jnp.zeros((rows, slots), F32)
    for j in range(routes.shape[1]):
        hit = routes[:, j : j + 1] == slot // capacity
        named = jnp.where(hit, 1.0, named)
        gate = jnp.where(hit, gates[:, j : j + 1], gate)
    earlier = jnp.where(
        lanes((rows, rows)) < lax.broadcasted_iota(jnp.int32, (rows, rows), 0), 1.0, 0.0
    )
    rank = dot(earlier.astype(BF16), named.astype(BF16))
    placed = (named > 0.0) & (rank == (slot % capacity).astype(F32))
    mix_ref[...] = jnp.where(placed, gate, 0.0)
    place_ref[...] = jnp.where(placed, 1.0, 0.0).T.astype(BF16)


def dispatch_kernel(x_ref, sums_ref, gain_ref, place_ref, hidden_ref, out_ref):
    beams = x_ref.shape[0]
    total = sums_ref[0].astype(F32)
    for s in range(1, sums_ref.shape[0]):
        total = total + sums_ref[s].astype(F32)
    inputs = jnp.concatenate([x_ref[b].astype(F32) for b in range(beams)], axis=0)
    hidden = inputs + total
    hidden_ref[...] = hidden
    expert_in = norm(hidden, gain_ref[...].reshape(1, -1)).astype(BF16)
    buffer = dot(place_ref[...], expert_in)
    experts, capacity = out_ref.shape[0], out_ref.shape[1]
    for e in range(experts):
        out_ref[e] = buffer[e * capacity : (e + 1) * capacity, :].astype(BF16)


def expert_kernel(x_hbm, w_in_hbm, w_out_hbm, out_ref, x_ref, w_in_ref, w_out_ref, rows_ref, sem):
    pairs = ((x_hbm, x_ref), (w_in_hbm, w_in_ref), (w_out_hbm, w_out_ref))
    copies = [pltpu.make_async_copy(a, b, sem.at[i]) for i, (a, b) in enumerate(pairs)]
    for copy in copies:
        copy.start()
    sources, capacity = x_ref.shape[0], x_ref.shape[1]
    copies[0].wait()
    for s in range(sources):
        rows_ref[s * capacity : (s + 1) * capacity, :] = x_ref[s].astype(F32)
    x = rows_ref[...].astype(BF16)
    copies[1].wait()
    projected = dot(x, w_in_ref[0])
    half = projected.shape[1] // 2
    g, u = projected[:, 0:half], projected[:, half:]
    act = (g * jax.nn.sigmoid(g) * u).astype(BF16)
    copies[2].wait()
    out = dot(act, w_out_ref[0])
    for s in range(sources):
        out_ref[s] = out[s * capacity : (s + 1) * capacity, :].astype(BF16)


def mix_kernel(hidden_ref, mix_ref, back_ref, out_ref, rows_ref):
    experts, capacity = back_ref.shape[0], back_ref.shape[1]
    for e in range(experts):
        rows_ref[e * capacity : (e + 1) * capacity, :] = back_ref[e].astype(F32)
    returned = rows_ref[...].astype(BF16)
    rest = mix_ref[...]
    total = hidden_ref[...]
    for _ in range(3):
        part = rest.astype(BF16)
        rest = rest - part.astype(F32)
        total = total + dot(part, returned)
    steps = out_ref.shape[1]
    for b in range(out_ref.shape[0]):
        out_ref[b] = total[b * steps : (b + 1) * steps, :].astype(BF16)


def final_kernel(seq_ref, parents_ref, part_ref, *refs):
    own_refs, (k_ref, v_ref) = refs[:-2], refs[-2:]
    steps = parents_ref.shape[0]
    here, tail = own_refs[0].shape[1], own_refs[0].shape[2]
    start = part_ref.shape[1] - here * steps
    seq = seq_ref[0]
    for i in range(here):
        beam = seq * here + i
        for s in range(steps - 1, -1, -1):
            beam = parents_ref[s, beam]
        apart = lax.bitwise_xor(beam // here, seq)
        for j, own_ref in enumerate(own_refs):

            @pl.when(apart == j)
            def _():
                k_ref[0:tail, i, :] = own_ref[0, beam % here]
                v_ref[0:tail, i, :] = own_ref[1, beam % here]

        span = slice(start + i * steps, start + (i + 1) * steps)
        for p in range(part_ref.shape[0]):
            k_ref[tail:, i, p * 128 : (p + 1) * 128] = part_ref[p, span, 0:128]
            v_ref[tail:, i, p * 128 : (p + 1) * 128] = part_ref[p, span, 128:256]


def rotary_tables(rows, steps, start):
    half = HEAD // 2
    frequency = ROPE_BASE ** (-(np.arange(half, dtype=np.float64) * 2.0 / HEAD))
    angles = (np.arange(rows) % steps + start)[:, None] * frequency[None, :]
    cosine = np.tile(np.cos(angles), (1, 8)).astype(np.float32)
    sine = np.sin(angles)
    sine = np.tile(np.concatenate([-sine, sine], axis=1), (1, 4)).astype(np.float32)
    return cosine, sine


def block(shape):
    return pl.BlockSpec(shape, lambda i: (0,) * len(shape))


def call(kernel, outs, *args, ins=(), scratch=(), mib=32):
    specs = list(ins) + [block(a.shape) for a in args[len(ins) :]]
    return pl.pallas_call(
        kernel,
        grid=(1,),
        out_shape=outs,
        in_specs=specs,
        out_specs=jax.tree.map(lambda o: block(o.shape), outs),
        scratch_shapes=list(scratch),
        compiler_params=params(mib),
        cost_estimate=pl.CostEstimate(
            flops=1 << 20, bytes_accessed=1 << 20, transcendentals=0
        ),
    )(*args)


def shaped(shape, dtype=BF16):
    return jax.ShapeDtypeStruct(shape, dtype)


def local(
    inputs,
    parents,
    block_len,
    prompt_key_cache,
    prompt_value_cache,
    generated_key_cache,
    generated_value_cache,
    gain_attn,
    gain_moe,
    w_query,
    key_projection_weight,
    value_projection_weight,
    w_output,
    w_in,
    w_out,
    routes,
    gate_weights,
):
    def stay(a):
        return pltpu.with_memory_space_constraint(a, pltpu.MemorySpace.HBM)

    n_seq = lax.axis_size("seq")
    n_req = lax.axis_size("req")
    n_chips = n_seq // 2
    seq = lax.axis_index("seq").astype(jnp.int32).reshape(1)
    here, steps, width = inputs.shape[1:]
    local_rows = here * steps
    rows = local_rows * n_chips
    keys, kv_width = prompt_key_cache.shape[1:]
    tail = generated_key_cache.shape[2]
    capacity = 4
    x = stay(inputs[0])
    anywhere = pl.BlockSpec(memory_space=pl.ANY)
    same_core = [[2 * z + core for z in range(n_chips)] for core in range(2)]

    def exchange(a, axis):
        return lax.all_to_all(a, axis, split_axis=0, concat_axis=0, tiled=True)

    def exchange_chips(a):
        return lax.all_to_all(
            a, "seq", split_axis=0, concat_axis=0, tiled=True, axis_index_groups=same_core
        )

    def apart(a, distance):
        return lax.ppermute(a, "seq", [(i, i ^ distance) for i in range(n_seq)])

    def of_other_core(a):
        return apart(a, 1)

    normed = call(norm_kernel, shaped((n_chips, local_rows, width)), x, stay(gain_attn))
    weights = [w_query.T, key_projection_weight.T, value_projection_weight.T]
    prompt = [prompt_key_cache[0], prompt_value_cache[0]]
    normed, *traded = lax.optimization_barrier((normed, *weights, *prompt, w_output))
    normed_all = exchange_chips(normed)
    traded = [of_other_core(a) for a in traded]
    other_weights, other_prompt, other_w_output = traded[:3], traded[3:5], traded[5]
    own = call(
        pack_kernel,
        shaped((2, here, tail, kv_width)),
        normed,
        stay(generated_key_cache[0]),
        stay(generated_value_cache[0]),
        ins=[anywhere],
    )
    other_own = apart(own, 1)
    bias, extra, fresh_bias, final = call(
        functools.partial(mask_kernel, tail, here),
        (
            shaped((8, 2 * keys), F32),
            shaped((rows, 128), F32),
            shaped((rows, 128), F32),
            shaped((rows, 128)),
        ),
        normed,
        seq,
        parents[0],
        block_len,
        apart(block_len, 1),
        ins=[anywhere, scalars(), scalars(), scalars(), scalars()],
    )
    cosine, sine = map(jnp.asarray, rotary_tables(rows, steps, keys * n_seq + tail))
    q, kv = call(
        project_kernel,
        (shaped((n_chips, 3 * rows, 128)), shaped((2, rows, 128))),
        normed_all,
        seq,
        *[stay(w) for w in weights],
        *other_weights,
        stay(cosine),
        stay(sine),
        ins=[block(normed_all.shape), scalars()],
    )
    q_all = exchange_chips(q)
    fresh, pick = call(
        fresh_kernel,
        (shaped((rows, 512)), shaped((n_chips, local_rows, 512))),
        q,
        kv,
        apart(kv, 1),
        fresh_bias,
        final,
    )

    resident = pl.BlockSpec(memory_space=pltpu.VMEM)
    operands = (bias, extra, q_all, own, other_own, pick)
    partial_shape = shaped((n_chips, rows + local_rows, 512))
    partial = pl.pallas_call(
        attend_kernel,
        grid=(1,),
        out_shape=partial_shape,
        in_specs=[resident] * len(operands) + [anywhere] * 4,
        out_specs=block(partial_shape.shape),
        scratch_shapes=[pltpu.VMEM((keys, kv_width), BF16)] * 4
        + [
            pltpu.VMEM((6 * rows, 2 * keys + 128), F32),
            pltpu.VMEM((6 * rows, 2 * keys + 128), F32),
            pltpu.VMEM((6 * rows, 2 * keys + 128), BF16),
            pltpu.VMEM((6 * rows, 2 * keys + 128), BF16),
            pltpu.VMEM((6 * rows, 128), F32),
            pltpu.SemaphoreType.DMA((kv_width // 128, 4)),
        ],
        compiler_params=params(32),
        cost_estimate=pl.CostEstimate(
            flops=4 * 24 * rows * 2 * keys * HEAD,
            bytes_accessed=8 * keys * kv_width,
            transcendentals=24 * rows * 2 * keys,
        ),
    )(*operands, *map(stay, prompt), *other_prompt)
    parts = exchange_chips(partial)
    sums = call(
        join_kernel,
        shaped((n_chips, local_rows, width)),
        parts,
        fresh,
        seq,
        stay(w_output),
        other_w_output,
        ins=[block(parts.shape), block(fresh.shape), scalars()],
    )
    slots = n_req * capacity
    place, mix = call(
        functools.partial(route_kernel, capacity),
        (shaped((slots, local_rows)), shaped((local_rows, slots), F32)),
        sums,
        stay(routes[0]),
        stay(gate_weights[0]),
        ins=[anywhere],
    )
    sums = exchange_chips(sums)
    hidden, buffer = call(
        dispatch_kernel,
        (shaped((local_rows, width), F32), shaped((n_req, capacity, width))),
        x,
        sums,
        stay(gain_moe),
        place,
    )
    own, buffer = lax.optimization_barrier((own, buffer))
    even = [own] + [apart(own, k) for k in range(2, n_seq, 2)]
    buffer = exchange(buffer, "req")
    back = call(
        expert_kernel,
        shaped(buffer.shape),
        buffer,
        stay(w_in),
        stay(w_out),
        ins=[anywhere] * 3,
        scratch=[
            pltpu.VMEM(buffer.shape, BF16),
            pltpu.VMEM(w_in.shape, BF16),
            pltpu.VMEM(w_out.shape, BF16),
            pltpu.VMEM((slots, width), F32),
            pltpu.SemaphoreType.DMA((3,)),
        ],
    )
    back, *even = lax.optimization_barrier((back, *even))
    odd = [other_own] + [apart(a, 1) for a in even[1:]]
    owns = [a for pair in zip(even, odd) for a in pair]
    back = exchange(back, "req")
    mixed = call(
        mix_kernel,
        shaped((here, steps, width)),
        hidden,
        mix,
        back,
        scratch=[pltpu.VMEM((slots, width), F32)],
    )
    final_k, final_v = call(
        final_kernel,
        (shaped((tail + steps, here, kv_width)),) * 2,
        seq,
        parents[0],
        parts,
        *owns,
        ins=[scalars(), scalars()],
    )
    return (
        mixed[None],
        final_k.transpose(1, 0, 2)[None],
        final_v.transpose(1, 0, 2)[None],
    )


def solution(mesh):
    placed = (
        P("req", "seq", None, None),
        P("req", None, None),
        P("req", "seq"),
        P("req", "seq", None),
        P("req", "seq", None),
        P("req", "seq", None, None),
        P("req", "seq", None, None),
        P(),
        P(),
        P(None, "seq"),
        P(None, "seq"),
        P(None, "seq"),
        P("seq", None),
        P("req", None, None),
        P("req", None, None),
        P("req", "seq", None, None),
        P("req", "seq", None, None),
    )
    return jax.shard_map(
        local,
        mesh=mesh,
        in_specs=placed,
        out_specs=(P("req", "seq", None, None),) * 3,
        check_vma=False,
    )
```

```python
import functools

import jax
import jax.numpy as jnp
import numpy as np
from jax import lax
from jax.experimental import pallas as pl
from jax.experimental.pallas import tpu as pltpu
from jax.sharding import PartitionSpec as P

HEAD = 64
BLK = 128
EPSILON = 1e-05
ROPE_BASE = 10000.0
FILL = -(2.0**100)
SCALE = 0.125
BF16 = jnp.bfloat16
F32 = jnp.float32


def scalars():
    return pl.BlockSpec(memory_space=pltpu.SMEM)


def params(mib):
    return pltpu.CompilerParams(vmem_limit_bytes=mib << 20)


def dot(a, b):
    return jnp.dot(a, b, preferred_element_type=F32)


def dot_t(a, b):
    return lax.dot_general(a, b, (((1,), (1,)), ((), ())), preferred_element_type=F32)


def lanes(shape):
    return lax.broadcasted_iota(jnp.int32, shape, len(shape) - 1)


def norm(x, gain):
    mean_sq = jnp.mean(x * x, axis=-1, keepdims=True)
    return x * lax.rsqrt(mean_sq + EPSILON) * gain


def norm_kernel(x_ref, gain_ref, out_ref):
    beams, steps = x_ref.shape[0], x_ref.shape[1]
    gain = gain_ref[...].reshape(1, -1)
    rows = [norm(x_ref[b].astype(F32), gain) for b in range(beams)]
    rows = jnp.concatenate(rows, axis=0).astype(BF16)
    for d in range(out_ref.shape[0]):
        out_ref[d] = rows


def pack_kernel(order_ref, own_k_ref, own_v_ref, out_ref):
    out_ref[0] = own_k_ref[...]
    out_ref[1] = own_v_ref[...]


def swap(x):
    return pltpu.roll(x, HEAD, 1)


def even_odd(own, other, core):
    return jnp.where(core == 0, own, other), jnp.where(core == 0, other, own)


def project_kernel(
    x_ref,
    seq_ref,
    wq_ref,
    wk_ref,
    wv_ref,
    other_wq_ref,
    other_wk_ref,
    other_wv_ref,
    cos_ref,
    sin_ref,
    q_ref,
    kv_ref,
):
    core = seq_ref[0] % 2
    rows = x_ref.shape[0] * x_ref.shape[1]
    x = x_ref[...].reshape(rows, x_ref.shape[2])
    half = HEAD // 2

    def turned(wq, wk):
        y = jnp.concatenate([dot_t(x, wq) * SCALE, dot_t(x, wk)], axis=1)
        first = lanes(y.shape) % HEAD < half
        width = y.shape[1]
        turn = jnp.where(first, pltpu.roll(y, width - half, 1), pltpu.roll(y, half, 1))
        return y * cos_ref[...] + turn * sin_ref[...]

    y = turned(wq_ref[...], wk_ref[...])
    z = turned(other_wq_ref[...], other_wk_ref[...])
    even, odd = even_odd(y, z, core)
    v_even, v_odd = even_odd(dot_t(x, wv_ref[...]), dot_t(x, other_wv_ref[...]), core)
    low = lanes((rows, 128)) < HEAD
    e0, e1, o0, o1 = even[:, 0:128], even[:, 128:256], odd[:, 0:128], odd[:, 128:256]
    tiles = [
        jnp.where(low, e0, swap(o0)),
        jnp.where(low, swap(e0), o0),
        jnp.where(low, e1, swap(o1)),
    ]
    q = jnp.concatenate(tiles, axis=0).astype(BF16)
    for d in range(q_ref.shape[0]):
        q_ref[d] = q
    kv_ref[0] = jnp.where(low, swap(e1), o1).astype(BF16)
    kv_ref[1] = jnp.concatenate([v_even, v_odd], axis=1).astype(BF16)


def lookup(parents_ref, step, cur, beams):
    found = jnp.zeros(cur.shape, jnp.int32)
    for b in range(beams):
        found = jnp.where(cur == b, parents_ref[step, b], found)
    return found


def mask_kernel(
    tail,
    here,
    order_ref,
    seq_ref,
    parents_ref,
    len_ref,
    other_len_ref,
    bias_ref,
    extra_ref,
    fresh_ref,
    final_ref,
):
    steps, beams = parents_ref.shape
    seq = seq_ref[0]
    core = seq % 2
    other = seq + 1 - 2 * core
    shape = extra_ref.shape
    rows = shape[0]
    lane = lanes(shape)
    spot = lanes((bias_ref.shape[0], BLK))
    half = bias_ref.shape[1] // 2
    for source, start in ((len_ref, 0), (other_len_ref, half)):
        for j in range(half // BLK):
            at = start + j * BLK
            bias_ref[:, at : at + BLK] = jnp.where(spot < source[0, j], 0.0, FILL)
    row = lax.broadcasted_iota(jnp.int32, shape, 0)

    def beam_of(place, parity):
        return (place // (here * steps)) * 2 * here + parity * here + place // steps % here

    step = row % steps
    key = lane % rows
    key_beam = beam_of(key, jnp.where(lane < rows, core, 1 - core))
    key_step = key % steps
    real = lane < 2 * rows
    cur = beam_of(row, core)
    end = cur
    live = jnp.zeros(shape, jnp.int32)
    chosen = jnp.zeros(shape, jnp.int32)
    for s in range(steps - 1, -1, -1):
        here_now = real & (key_step == s)
        live = live | jnp.where(here_now & (cur == key_beam) & (step >= s), 1, 0)
        chosen = chosen | jnp.where(here_now & (end == key_beam) & (step == s), 1, 0)
        cur = jnp.where(step >= s, lookup(parents_ref, s, cur, beams), cur)
        end = jnp.where(step < s, lookup(parents_ref, s, end, beams), end)
    fresh_ref[...] = jnp.where(live > 0, 0.0, FILL)
    final_ref[...] = jnp.where(chosen > 0, 1.0, 0.0).astype(BF16)
    own_keys = here * tail
    holder = jnp.where(lane < own_keys, seq, other)
    own_beam = holder * here + lane % own_keys // tail
    extra_ref[...] = jnp.where((lane < 2 * own_keys) & (cur == own_beam), 0.0, FILL)


def split_heads(q_ref, rows):
    low = lanes((3 * rows, 128)) < HEAD
    q = q_ref[...].reshape(3 * rows, 128).astype(F32)
    both = [jnp.where(low, q, 0.0), jnp.where(low, 0.0, q)]
    return jnp.concatenate(both, axis=0).astype(BF16)


def pack_partial(o, total, lse, rows, store):
    lane = lanes((rows, 128))
    low = lane < HEAD
    stats = jnp.zeros((rows, 128), F32)
    for i in range(6):
        rest = lse[i]
        for piece in range(3):
            part = rest.astype(BF16).astype(F32)
            rest = rest - part
            stats = jnp.where(lane == 3 * i + piece, part, stats)
    for j in range(3):
        even = o[j * rows : (j + 1) * rows, :] / total[j]
        odd = o[(3 + j) * rows : (4 + j) * rows, :] / total[3 + j]
        store(j, jnp.where(low, even, odd).astype(BF16))
    store(3, stats.astype(BF16))


def fresh_kernel(q_ref, kv_ref, other_ref, bias_ref, final_ref, out_ref, pick_ref):
    rows = kv_ref.shape[1]
    q = split_heads(q_ref.at[0], rows)
    fill = jnp.zeros((128 - 2 * rows, 128), BF16)
    k = jnp.concatenate([kv_ref[0], other_ref[0], fill], axis=0)
    v = jnp.concatenate([kv_ref[1], other_ref[1], fill], axis=0)
    s = dot_t(q, k)
    probs, total, lse = [], [], []
    for i in range(6):
        piece = s[i * rows : (i + 1) * rows, :] + bias_ref[...]
        top = jnp.max(piece, axis=-1, keepdims=True)
        e = jnp.exp(piece - top)
        total.append(jnp.sum(e, axis=-1, keepdims=True))
        lse.append(top + jnp.log(total[i]))
        probs.append(e.astype(BF16))
    o = dot(jnp.concatenate(probs, axis=0), v)

    def store(j, tile):
        out_ref[:, j * 128 : (j + 1) * 128] = tile

    pack_partial(o, total, lse, rows, store)
    pick_k = dot(final_ref[...], k).astype(BF16)
    pick_v = dot(final_ref[...], v).astype(BF16)
    each = pick_ref.shape[1]
    for d in range(pick_ref.shape[0]):
        pick_ref[d, :, 0:128] = pick_k[d * each : (d + 1) * each, :]
        pick_ref[d, :, 128:256] = pick_v[d * each : (d + 1) * each, :]
        pick_ref[d, :, 256:512] = jnp.zeros((each, 256), BF16)


def attend_kernel(
    bias_ref,
    extra_ref,
    q_ref,
    own_ref,
    other_own_ref,
    pick_ref,
    *refs,
):
    other_k_ref, sources, out_ref, held = refs[0], refs[1:4], refs[4], refs[5:8]
    score_refs, prob_refs, top_ref, sem = refs[8:10], refs[10:12], refs[12], refs[13]
    k_ref, v_ref, other_v_ref = held
    rows = extra_ref.shape[0]
    half = k_ref.shape[0]
    keys = 2 * half
    own_keys = own_ref.shape[1] * own_ref.shape[2]
    pairs = q_ref.shape[0]
    chunk = 512
    chunks = keys // chunk
    fill = jnp.zeros((128 - 2 * own_keys, 128), BF16)

    def lane_span(pair):
        return slice(pair * 128, (pair + 1) * 128)

    copies = {}
    for pair in range(pairs):
        for i in range(3):
            copies[pair, i] = pltpu.make_async_copy(
                sources[i].at[:, lane_span(pair)], held[i].at[:, lane_span(pair)], sem.at[pair, i]
            )

    def needed(turn):
        keys_of = [copies[turn, 0]] if turn < pairs else []
        return keys_of + [copies[turn - 1, i] for i in (1, 2) if 1 <= turn <= pairs]

    for copy in needed(0) + needed(1):
        copy.start()

    def extra(pair, i):
        both = [r[i, :, :, lane_span(pair)].reshape(own_keys, 128) for r in (own_ref, other_own_ref)]
        return jnp.concatenate([*both, fill], axis=0)

    def fold(x):
        tiles = [x[:, at : at + 128] for at in range(0, x.shape[1], 128)]
        return functools.reduce(jnp.maximum, tiles)

    queries = {}

    def score(pair, i):
        s_ref = score_refs[pair % 2]
        if i == 0:
            queries[pair] = split_heads(q_ref.at[pair], rows)
            s = dot_t(queries[pair], extra(pair, 0))
            s = s + jnp.concatenate([extra_ref[...]] * 6, axis=0)
            s_ref[:, keys:] = s
            top = s
        else:
            top = top_ref[...]
        at = i * chunk
        source, start = (k_ref, at) if at < half else (other_k_ref, at - half)
        s = dot_t(queries[pair], source[start : start + chunk, lane_span(pair)])
        s = s + bias_ref[0:1, at : at + chunk]
        s_ref[:, at : at + chunk] = s
        top_ref[...] = jnp.maximum(top, fold(s))

    tops, totals = {}, {}

    def soften(pair, i):
        s_ref, p_ref = score_refs[pair % 2], prob_refs[pair % 2]
        span = slice(i * rows, (i + 1) * rows)
        top = tops[pair][span, :]
        total = jnp.zeros((rows, 128), F32)
        for at in range(0, keys + 128, 128):
            e = jnp.exp(s_ref[span, at : at + 128] - top)
            total = total + e
            p_ref[span, at : at + 128] = e.astype(BF16)
        totals[pair, i] = jnp.sum(total, axis=-1, keepdims=True)

    summed = {}

    def weigh(pair, part):
        p_ref = prob_refs[pair % 2]
        if part == 0:
            summed[pair] = dot(p_ref[:, 0:half], v_ref[:, lane_span(pair)])
            return
        o = summed[pair] + dot(p_ref[:, half:keys], other_v_ref[:, lane_span(pair)])
        o = o + dot(p_ref[:, keys:], extra(pair, 1))
        total = [totals[pair, i] for i in range(6)]
        lse = [tops[pair][i * rows : (i + 1) * rows, :] + jnp.log(total[i]) for i in range(6)]

        def store(j, tile):
            out_ref[pair, 0:rows, lane_span(j)] = tile

        pack_partial(o, total, lse, rows, store)
        out_ref[pair, rows:, :] = pick_ref[pair]

    for turn in range(pairs + 2):
        for copy in needed(turn):
            copy.wait()
        for copy in needed(turn + 2):
            copy.start()
        for i in range(chunks):
            if turn < pairs:
                score(turn, i)
            if 0 <= turn - 1 < pairs and i < 6:
                soften(turn - 1, i)
            if turn >= 2 and i in (3, 6):
                weigh(turn - 2, 0 if i == 3 else 1)
        if turn < pairs:
            tops[turn] = jnp.max(top_ref[...], axis=-1, keepdims=True)


def join_kernel(part_ref, fresh_ref, seq_ref, w_ref, other_w_ref, out_ref):
    sources, rows = part_ref.shape[0], fresh_ref.shape[0]
    core = seq_ref[0] % 2
    low = lanes((rows, 128)) < HEAD

    def tile(s, j):
        span = slice(j * 128, (j + 1) * 128)
        source = fresh_ref[:, span] if s == sources else part_ref[s, 0:rows, span]
        return source.astype(F32)

    stats = [tile(s, 3) for s in range(sources + 1)]
    lse = [x + pltpu.roll(x, 127, 1) + pltpu.roll(x, 126, 1) for x in stats]
    top = functools.reduce(jnp.maximum, lse)
    weight = [jnp.exp(x - top) for x in lse]
    inverse = 1.0 / functools.reduce(jnp.add, weight)
    out = jnp.zeros((rows, w_ref.shape[1]), F32)
    for j in range(3):
        total = jnp.zeros((rows, 128), F32)
        for s in range(sources + 1):
            w = weight[s] * inverse
            even, odd = w[:, 3 * j : 3 * j + 1], w[:, 9 + 3 * j : 10 + 3 * j]
            total = total + tile(s, j) * jnp.where(low, even, odd)
        total = jnp.where(core == 0, total, swap(total)).astype(BF16)
        span = slice(j * HEAD, (j + 1) * HEAD)
        out = out + dot(total, jnp.concatenate([w_ref[span, :], other_w_ref[span, :]], axis=0))
    out = out.astype(BF16)
    each = rows // sources
    for s in range(sources):
        out_ref[s] = out[s * each : (s + 1) * each, :]


def route_kernel(capacity, order_ref, route_ref, gate_ref, place_ref, mix_ref):
    beams, steps = route_ref.shape[0], route_ref.shape[1]
    rows = beams * steps
    slots = place_ref.shape[0]
    slot = lanes((rows, slots))
    routes = jnp.concatenate([route_ref[b] for b in range(beams)], axis=0)
    gates = jnp.concatenate([gate_ref[b] for b in range(beams)], axis=0)
    named = jnp.zeros((rows, slots), F32)
    gate = jnp.zeros((rows, slots), F32)
    for j in range(routes.shape[1]):
        hit = routes[:, j : j + 1] == slot // capacity
        named = jnp.where(hit, 1.0, named)
        gate = jnp.where(hit, gates[:, j : j + 1], gate)
    earlier = jnp.where(
        lanes((rows, rows)) < lax.broadcasted_iota(jnp.int32, (rows, rows), 0), 1.0, 0.0
    )
    rank = dot(earlier.astype(BF16), named.astype(BF16))
    placed = (named > 0.0) & (rank == (slot % capacity).astype(F32))
    mix_ref[...] = jnp.where(placed, gate, 0.0)
    place_ref[...] = jnp.where(placed, 1.0, 0.0).T.astype(BF16)


def dispatch_kernel(x_ref, sums_ref, gain_ref, place_ref, hidden_ref, out_ref):
    beams = x_ref.shape[0]
    total = sums_ref[0].astype(F32)
    for s in range(1, sums_ref.shape[0]):
        total = total + sums_ref[s].astype(F32)
    inputs = jnp.concatenate([x_ref[b].astype(F32) for b in range(beams)], axis=0)
    hidden = inputs + total
    hidden_ref[...] = hidden
    expert_in = norm(hidden, gain_ref[...].reshape(1, -1)).astype(BF16)
    buffer = dot(place_ref[...], expert_in)
    experts, capacity = out_ref.shape[0], out_ref.shape[1]
    for e in range(experts):
        out_ref[e] = buffer[e * capacity : (e + 1) * capacity, :].astype(BF16)


def expert_kernel(x_ref, w_in_hbm, w_out_ref, out_ref, w_in_ref, rows_ref, sem):
    depth = w_in_ref.shape[1] // 3
    spans = [slice(i * depth, (i + 1) * depth) for i in range(3)]
    copies = [
        pltpu.make_async_copy(w_in_hbm.at[:, span], w_in_ref.at[:, span], sem.at[i])
        for i, span in enumerate(spans)
    ]
    for copy in copies:
        copy.start()
    sources, capacity = x_ref.shape[0], x_ref.shape[1]
    for s in range(sources):
        rows_ref[s * capacity : (s + 1) * capacity, :] = x_ref[s].astype(F32)
    x = rows_ref[...].astype(BF16)
    projected = jnp.zeros((sources * capacity, w_in_ref.shape[2]), F32)
    for copy, span in zip(copies, spans):
        copy.wait()
        projected = projected + dot(x[:, span], w_in_ref[0, span, :])
    half = projected.shape[1] // 2
    g, u = projected[:, 0:half], projected[:, half:]
    act = (g * jax.nn.sigmoid(g) * u).astype(BF16)
    out = dot(act, w_out_ref[0])
    for s in range(sources):
        out_ref[s] = out[s * capacity : (s + 1) * capacity, :].astype(BF16)


def mix_kernel(hidden_ref, mix_ref, back_ref, out_ref, rows_ref):
    experts, capacity = back_ref.shape[0], back_ref.shape[1]
    for e in range(experts):
        rows_ref[e * capacity : (e + 1) * capacity, :] = back_ref[e].astype(F32)
    returned = rows_ref[...].astype(BF16)
    rest = mix_ref[...]
    total = hidden_ref[...]
    for _ in range(3):
        part = rest.astype(BF16)
        rest = rest - part.astype(F32)
        total = total + dot(part, returned)
    steps = out_ref.shape[1]
    for b in range(out_ref.shape[0]):
        out_ref[b] = total[b * steps : (b + 1) * steps, :].astype(BF16)


def final_kernel(seq_ref, parents_ref, part_ref, *refs):
    own_refs, (k_ref, v_ref) = refs[:-2], refs[-2:]
    steps = parents_ref.shape[0]
    here, tail = own_refs[0].shape[1], own_refs[0].shape[2]
    start = part_ref.shape[1] - here * steps
    seq = seq_ref[0]
    for i in range(here):
        beam = seq * here + i
        for s in range(steps - 1, -1, -1):
            beam = parents_ref[s, beam]
        apart = lax.bitwise_xor(beam // here, seq)
        for j, own_ref in enumerate(own_refs):

            @pl.when(apart == j)
            def _():
                k_ref[0:tail, i, :] = own_ref[0, beam % here]
                v_ref[0:tail, i, :] = own_ref[1, beam % here]

        span = slice(start + i * steps, start + (i + 1) * steps)
        for p in range(part_ref.shape[0]):
            k_ref[tail:, i, p * 128 : (p + 1) * 128] = part_ref[p, span, 0:128]
            v_ref[tail:, i, p * 128 : (p + 1) * 128] = part_ref[p, span, 128:256]


def rotary_tables(rows, steps, start):
    half = HEAD // 2
    frequency = ROPE_BASE ** (-(np.arange(half, dtype=np.float64) * 2.0 / HEAD))
    angles = (np.arange(rows) % steps + start)[:, None] * frequency[None, :]
    cosine = np.tile(np.cos(angles), (1, 8)).astype(np.float32)
    sine = np.sin(angles)
    sine = np.tile(np.concatenate([-sine, sine], axis=1), (1, 4)).astype(np.float32)
    return cosine, sine


def block(shape):
    return pl.BlockSpec(shape, lambda i: (0,) * len(shape))


def call(kernel, outs, *args, ins=(), scratch=(), mib=32):
    specs = list(ins) + [block(a.shape) for a in args[len(ins) :]]
    return pl.pallas_call(
        kernel,
        grid=(1,),
        out_shape=outs,
        in_specs=specs,
        out_specs=jax.tree.map(lambda o: block(o.shape), outs),
        scratch_shapes=list(scratch),
        compiler_params=params(mib),
        cost_estimate=pl.CostEstimate(
            flops=1 << 20, bytes_accessed=1 << 20, transcendentals=0
        ),
    )(*args)


def shaped(shape, dtype=BF16):
    return jax.ShapeDtypeStruct(shape, dtype)


def local(
    inputs,
    parents,
    block_len,
    prompt_key_cache,
    prompt_value_cache,
    generated_key_cache,
    generated_value_cache,
    gain_attn,
    gain_moe,
    w_query,
    key_projection_weight,
    value_projection_weight,
    w_output,
    w_in,
    w_out,
    routes,
    gate_weights,
):
    def stay(a):
        return pltpu.with_memory_space_constraint(a, pltpu.MemorySpace.HBM)

    n_seq = lax.axis_size("seq")
    n_req = lax.axis_size("req")
    n_chips = n_seq // 2
    seq = lax.axis_index("seq").astype(jnp.int32).reshape(1)
    here, steps, width = inputs.shape[1:]
    local_rows = here * steps
    rows = local_rows * n_chips
    keys, kv_width = prompt_key_cache.shape[1:]
    tail = generated_key_cache.shape[2]
    capacity = 4
    x = stay(inputs[0])
    anywhere = pl.BlockSpec(memory_space=pl.ANY)
    same_core = [[2 * z + core for z in range(n_chips)] for core in range(2)]

    def exchange(a, axis):
        return lax.all_to_all(a, axis, split_axis=0, concat_axis=0, tiled=True)

    def exchange_chips(a):
        return lax.all_to_all(
            a, "seq", split_axis=0, concat_axis=0, tiled=True, axis_index_groups=same_core
        )

    def apart(a, distance):
        return lax.ppermute(a, "seq", [(i, i ^ distance) for i in range(n_seq)])

    def of_other_core(a):
        return apart(a, 1)

    normed = call(norm_kernel, shaped((n_chips, local_rows, width)), x, stay(gain_attn))
    weights = [w_query.T, key_projection_weight.T, value_projection_weight.T]
    prompt = [prompt_key_cache[0], prompt_value_cache[0]]
    normed, *traded = lax.optimization_barrier((normed, *weights, *prompt, w_output))
    normed_all = exchange_chips(normed)
    traded = [of_other_core(a) for a in traded]
    other_weights, other_prompt, other_w_output = traded[:3], traded[3:5], traded[5]
    own = call(
        pack_kernel,
        shaped((2, here, tail, kv_width)),
        normed,
        stay(generated_key_cache[0]),
        stay(generated_value_cache[0]),
        ins=[anywhere],
    )
    other_own = apart(own, 1)
    bias, extra, fresh_bias, final = call(
        functools.partial(mask_kernel, tail, here),
        (
            shaped((8, 2 * keys), F32),
            shaped((rows, 128), F32),
            shaped((rows, 128), F32),
            shaped((rows, 128)),
        ),
        normed,
        seq,
        parents[0],
        block_len,
        apart(block_len, 1),
        ins=[anywhere, scalars(), scalars(), scalars(), scalars()],
    )
    cosine, sine = map(jnp.asarray, rotary_tables(rows, steps, keys * n_seq + tail))
    q, kv = call(
        project_kernel,
        (shaped((n_chips, 3 * rows, 128)), shaped((2, rows, 128))),
        normed_all,
        seq,
        *[stay(w) for w in weights],
        *other_weights,
        stay(cosine),
        stay(sine),
        ins=[block(normed_all.shape), scalars()],
    )
    q_all = exchange_chips(q)
    fresh, pick = call(
        fresh_kernel,
        (shaped((rows, 512)), shaped((n_chips, local_rows, 512))),
        q,
        kv,
        apart(kv, 1),
        fresh_bias,
        final,
    )

    resident = pl.BlockSpec(memory_space=pltpu.VMEM)
    operands = (bias, extra, q_all, own, other_own, pick, other_prompt[0])
    partial_shape = shaped((n_chips, rows + local_rows, 512))
    partial = pl.pallas_call(
        attend_kernel,
        grid=(1,),
        out_shape=partial_shape,
        in_specs=[resident] * len(operands) + [anywhere] * 3,
        out_specs=block(partial_shape.shape),
        scratch_shapes=[pltpu.VMEM((keys, kv_width), BF16)] * 3
        + [
            pltpu.VMEM((6 * rows, 2 * keys + 128), F32),
            pltpu.VMEM((6 * rows, 2 * keys + 128), F32),
            pltpu.VMEM((6 * rows, 2 * keys + 128), BF16),
            pltpu.VMEM((6 * rows, 2 * keys + 128), BF16),
            pltpu.VMEM((6 * rows, 128), F32),
            pltpu.SemaphoreType.DMA((kv_width // 128, 3)),
        ],
        compiler_params=params(32),
        cost_estimate=pl.CostEstimate(
            flops=4 * 24 * rows * 2 * keys * HEAD,
            bytes_accessed=8 * keys * kv_width,
            transcendentals=24 * rows * 2 * keys,
        ),
    )(*operands, *map(stay, prompt), other_prompt[1])
    parts = exchange_chips(partial)
    sums = call(
        join_kernel,
        shaped((n_chips, local_rows, width)),
        parts,
        fresh,
        seq,
        stay(w_output),
        other_w_output,
        ins=[block(parts.shape), block(fresh.shape), scalars()],
    )
    slots = n_req * capacity
    place, mix = call(
        functools.partial(route_kernel, capacity),
        (shaped((slots, local_rows)), shaped((local_rows, slots), F32)),
        sums,
        stay(routes[0]),
        stay(gate_weights[0]),
        ins=[anywhere],
    )
    sums = exchange_chips(sums)
    hidden, buffer = call(
        dispatch_kernel,
        (shaped((local_rows, width), F32), shaped((n_req, capacity, width))),
        x,
        sums,
        stay(gain_moe),
        place,
    )
    own, buffer = lax.optimization_barrier((own, buffer))
    even = [own] + [apart(own, k) for k in range(2, n_seq, 2)]
    buffer = exchange(buffer, "req")
    back = call(
        expert_kernel,
        shaped(buffer.shape),
        buffer,
        stay(w_in),
        w_out,
        ins=[resident, anywhere, resident],
        scratch=[
            pltpu.VMEM(w_in.shape, BF16),
            pltpu.VMEM((slots, width), F32),
            pltpu.SemaphoreType.DMA((3,)),
        ],
    )
    back, *even = lax.optimization_barrier((back, *even))
    odd = [other_own] + [apart(a, 1) for a in even[1:]]
    owns = [a for pair in zip(even, odd) for a in pair]
    back = exchange(back, "req")
    mixed = call(
        mix_kernel,
        shaped((here, steps, width)),
        hidden,
        mix,
        back,
        scratch=[pltpu.VMEM((slots, width), F32)],
    )
    final_k, final_v = call(
        final_kernel,
        (shaped((tail + steps, here, kv_width)),) * 2,
        seq,
        parents[0],
        parts,
        *owns,
        ins=[scalars(), scalars()],
    )
    return (
        mixed[None],
        final_k.transpose(1, 0, 2)[None],
        final_v.transpose(1, 0, 2)[None],
    )


def solution(mesh):
    placed = (
        P("req", "seq", None, None),
        P("req", None, None),
        P("req", "seq"),
        P("req", "seq", None),
        P("req", "seq", None),
        P("req", "seq", None, None),
        P("req", "seq", None, None),
        P(),
        P(),
        P(None, "seq"),
        P(None, "seq"),
        P(None, "seq"),
        P("seq", None),
        P("req", None, None),
        P("req", None, None),
        P("req", "seq", None, None),
        P("req", "seq", None, None),
    )
    return jax.shard_map(
        local,
        mesh=mesh,
        in_specs=placed,
        out_specs=(P("req", "seq", None, None),) * 3,
        check_vma=False,
    )
```

```python
import functools

import jax
import jax.numpy as jnp
import numpy as np
from jax import lax
from jax.experimental import pallas as pl
from jax.experimental.pallas import tpu as pltpu
from jax.sharding import PartitionSpec as P

HEAD = 64
BLK = 128
EPSILON = 1e-05
ROPE_BASE = 10000.0
FILL = -(2.0**100)
SCALE = 0.125
BF16 = jnp.bfloat16
F32 = jnp.float32


def scalars():
    return pl.BlockSpec(memory_space=pltpu.SMEM)


def params(mib):
    return pltpu.CompilerParams(vmem_limit_bytes=mib << 20)


def dot(a, b):
    return jnp.dot(a, b, preferred_element_type=F32)


def dot_t(a, b):
    return lax.dot_general(a, b, (((1,), (1,)), ((), ())), preferred_element_type=F32)


def lanes(shape):
    return lax.broadcasted_iota(jnp.int32, shape, len(shape) - 1)


def norm(x, gain):
    mean_sq = jnp.mean(x * x, axis=-1, keepdims=True)
    return x * lax.rsqrt(mean_sq + EPSILON) * gain


def norm_kernel(x_ref, gain_ref, out_ref):
    beams, steps = x_ref.shape[0], x_ref.shape[1]
    gain = gain_ref[...].reshape(1, -1)
    rows = [norm(x_ref[b].astype(F32), gain) for b in range(beams)]
    rows = jnp.concatenate(rows, axis=0).astype(BF16)
    for d in range(out_ref.shape[0]):
        out_ref[d] = rows


def pack_kernel(order_ref, own_k_ref, own_v_ref, out_ref):
    out_ref[0] = own_k_ref[...]
    out_ref[1] = own_v_ref[...]


def swap(x):
    return pltpu.roll(x, HEAD, 1)


def even_odd(own, other, core):
    return jnp.where(core == 0, own, other), jnp.where(core == 0, other, own)


def project_kernel(
    x_ref,
    seq_ref,
    wq_ref,
    wk_ref,
    wv_ref,
    other_wq_ref,
    other_wk_ref,
    other_wv_ref,
    cos_ref,
    sin_ref,
    q_ref,
    kv_ref,
):
    core = seq_ref[0] % 2
    rows = x_ref.shape[0] * x_ref.shape[1]
    x = x_ref[...].reshape(rows, x_ref.shape[2])
    half = HEAD // 2

    def turned(wq, wk):
        y = jnp.concatenate([dot_t(x, wq) * SCALE, dot_t(x, wk)], axis=1)
        first = lanes(y.shape) % HEAD < half
        width = y.shape[1]
        turn = jnp.where(first, pltpu.roll(y, width - half, 1), pltpu.roll(y, half, 1))
        return y * cos_ref[...] + turn * sin_ref[...]

    y = turned(wq_ref[...], wk_ref[...])
    z = turned(other_wq_ref[...], other_wk_ref[...])
    even, odd = even_odd(y, z, core)
    v_even, v_odd = even_odd(dot_t(x, wv_ref[...]), dot_t(x, other_wv_ref[...]), core)
    low = lanes((rows, 128)) < HEAD
    e0, e1, o0, o1 = even[:, 0:128], even[:, 128:256], odd[:, 0:128], odd[:, 128:256]
    tiles = [
        jnp.where(low, e0, swap(o0)),
        jnp.where(low, swap(e0), o0),
        jnp.where(low, e1, swap(o1)),
    ]
    q = jnp.concatenate(tiles, axis=0).astype(BF16)
    for d in range(q_ref.shape[0]):
        q_ref[d] = q
    kv_ref[0] = jnp.where(low, swap(e1), o1).astype(BF16)
    kv_ref[1] = jnp.concatenate([v_even, v_odd], axis=1).astype(BF16)


def lookup(parents_ref, step, cur, beams):
    found = jnp.zeros(cur.shape, jnp.int32)
    for b in range(beams):
        found = jnp.where(cur == b, parents_ref[step, b], found)
    return found


def mask_kernel(
    tail,
    here,
    order_ref,
    seq_ref,
    parents_ref,
    len_ref,
    other_len_ref,
    bias_ref,
    extra_ref,
    fresh_ref,
    final_ref,
):
    steps, beams = parents_ref.shape
    seq = seq_ref[0]
    core = seq % 2
    other = seq + 1 - 2 * core
    shape = extra_ref.shape
    rows = shape[0]
    lane = lanes(shape)
    spot = lanes((bias_ref.shape[0], BLK))
    half = bias_ref.shape[1] // 2
    for source, start in ((len_ref, 0), (other_len_ref, half)):
        for j in range(half // BLK):
            at = start + j * BLK
            bias_ref[:, at : at + BLK] = jnp.where(spot < source[0, j], 0.0, FILL)
    row = lax.broadcasted_iota(jnp.int32, shape, 0)

    def beam_of(place, parity):
        return (place // (here * steps)) * 2 * here + parity * here + place // steps % here

    step = row % steps
    key = lane % rows
    key_beam = beam_of(key, jnp.where(lane < rows, core, 1 - core))
    key_step = key % steps
    real = lane < 2 * rows
    cur = beam_of(row, core)
    end = cur
    live = jnp.zeros(shape, jnp.int32)
    chosen = jnp.zeros(shape, jnp.int32)
    for s in range(steps - 1, -1, -1):
        here_now = real & (key_step == s)
        live = live | jnp.where(here_now & (cur == key_beam) & (step >= s), 1, 0)
        chosen = chosen | jnp.where(here_now & (end == key_beam) & (step == s), 1, 0)
        cur = jnp.where(step >= s, lookup(parents_ref, s, cur, beams), cur)
        end = jnp.where(step < s, lookup(parents_ref, s, end, beams), end)
    fresh_ref[...] = jnp.where(live > 0, 0.0, FILL)
    final_ref[...] = jnp.where(chosen > 0, 1.0, 0.0).astype(BF16)
    own_keys = here * tail
    holder = jnp.where(lane < own_keys, seq, other)
    own_beam = holder * here + lane % own_keys // tail
    extra_ref[...] = jnp.where((lane < 2 * own_keys) & (cur == own_beam), 0.0, FILL)


def split_heads(q_ref, rows):
    low = lanes((3 * rows, 128)) < HEAD
    q = q_ref[...].reshape(3 * rows, 128).astype(F32)
    both = [jnp.where(low, q, 0.0), jnp.where(low, 0.0, q)]
    return jnp.concatenate(both, axis=0).astype(BF16)


def pack_partial(o, total, lse, rows, store):
    lane = lanes((rows, 128))
    low = lane < HEAD
    stats = jnp.zeros((rows, 128), F32)
    for i in range(6):
        rest = lse[i]
        for piece in range(3):
            part = rest.astype(BF16).astype(F32)
            rest = rest - part
            stats = jnp.where(lane == 3 * i + piece, part, stats)
    for j in range(3):
        even = o[j * rows : (j + 1) * rows, :] / total[j]
        odd = o[(3 + j) * rows : (4 + j) * rows, :] / total[3 + j]
        store(j, jnp.where(low, even, odd).astype(BF16))
    store(3, stats.astype(BF16))


def fresh_kernel(q_ref, kv_ref, other_ref, bias_ref, final_ref, out_ref, pick_ref):
    rows = kv_ref.shape[1]
    q = split_heads(q_ref.at[0], rows)
    fill = jnp.zeros((128 - 2 * rows, 128), BF16)
    k = jnp.concatenate([kv_ref[0], other_ref[0], fill], axis=0)
    v = jnp.concatenate([kv_ref[1], other_ref[1], fill], axis=0)
    s = dot_t(q, k)
    probs, total, lse = [], [], []
    for i in range(6):
        piece = s[i * rows : (i + 1) * rows, :] + bias_ref[...]
        top = jnp.max(piece, axis=-1, keepdims=True)
        e = jnp.exp(piece - top)
        total.append(jnp.sum(e, axis=-1, keepdims=True))
        lse.append(top + jnp.log(total[i]))
        probs.append(e.astype(BF16))
    o = dot(jnp.concatenate(probs, axis=0), v)

    def store(j, tile):
        out_ref[:, j * 128 : (j + 1) * 128] = tile

    pack_partial(o, total, lse, rows, store)
    pick_k = dot(final_ref[...], k).astype(BF16)
    pick_v = dot(final_ref[...], v).astype(BF16)
    each = pick_ref.shape[1]
    for d in range(pick_ref.shape[0]):
        pick_ref[d, :, 0:128] = pick_k[d * each : (d + 1) * each, :]
        pick_ref[d, :, 128:256] = pick_v[d * each : (d + 1) * each, :]
        pick_ref[d, :, 256:512] = jnp.zeros((each, 256), BF16)


def attend_kernel(
    bias_ref,
    extra_ref,
    q_ref,
    own_ref,
    other_own_ref,
    pick_ref,
    *refs,
):
    other_k_ref, sources, out_ref, held = refs[0], refs[1:4], refs[4], refs[5:8]
    score_refs, prob_refs, top_ref, sem = refs[8:10], refs[10:12], refs[12], refs[13]
    k_ref, v_ref, other_v_ref = held
    rows = extra_ref.shape[0]
    half = k_ref.shape[0]
    keys = 2 * half
    own_keys = own_ref.shape[1] * own_ref.shape[2]
    pairs = q_ref.shape[0]
    chunk = 512
    chunks = keys // chunk
    fill = jnp.zeros((128 - 2 * own_keys, 128), BF16)

    def lane_span(pair):
        return slice(pair * 128, (pair + 1) * 128)

    copies = {}
    for pair in range(pairs):
        for i in range(3):
            copies[pair, i] = pltpu.make_async_copy(
                sources[i].at[:, lane_span(pair)], held[i].at[:, lane_span(pair)], sem.at[pair, i]
            )

    def needed(turn):
        keys_of = [copies[turn, 0]] if turn < pairs else []
        return keys_of + [copies[turn - 1, i] for i in (1, 2) if 1 <= turn <= pairs]

    for copy in needed(0) + needed(1):
        copy.start()

    def extra(pair, i):
        both = [r[i, :, :, lane_span(pair)].reshape(own_keys, 128) for r in (own_ref, other_own_ref)]
        return jnp.concatenate([*both, fill], axis=0)

    def fold(x):
        tiles = [x[:, at : at + 128] for at in range(0, x.shape[1], 128)]
        return functools.reduce(jnp.maximum, tiles)

    queries = {}

    def score(pair, i):
        s_ref = score_refs[pair % 2]
        if i == 0:
            queries[pair] = split_heads(q_ref.at[pair], rows)
            s = dot_t(queries[pair], extra(pair, 0))
            s = s + jnp.concatenate([extra_ref[...]] * 6, axis=0)
            s_ref[:, keys:] = s
            top = s
        else:
            top = top_ref[...]
        at = i * chunk
        source, start = (k_ref, at) if at < half else (other_k_ref, at - half)
        s = dot_t(queries[pair], source[start : start + chunk, lane_span(pair)])
        s = s + bias_ref[0:1, at : at + chunk]
        s_ref[:, at : at + chunk] = s
        top_ref[...] = jnp.maximum(top, fold(s))

    tops, totals = {}, {}

    def soften(pair, i):
        s_ref, p_ref = score_refs[pair % 2], prob_refs[pair % 2]
        span = slice(i * rows, (i + 1) * rows)
        top = tops[pair][span, :]
        total = jnp.zeros((rows, 128), F32)
        for at in range(0, keys + 128, 128):
            e = jnp.exp(s_ref[span, at : at + 128] - top)
            total = total + e
            p_ref[span, at : at + 128] = e.astype(BF16)
        totals[pair, i] = jnp.sum(total, axis=-1, keepdims=True)

    summed = {}

    def weigh(pair, part):
        p_ref = prob_refs[pair % 2]
        if part == 0:
            summed[pair] = dot(p_ref[:, 0:half], v_ref[:, lane_span(pair)])
            return
        o = summed[pair] + dot(p_ref[:, half:keys], other_v_ref[:, lane_span(pair)])
        o = o + dot(p_ref[:, keys:], extra(pair, 1))
        total = [totals[pair, i] for i in range(6)]
        lse = [tops[pair][i * rows : (i + 1) * rows, :] + jnp.log(total[i]) for i in range(6)]

        def store(j, tile):
            out_ref[pair, 0:rows, lane_span(j)] = tile

        pack_partial(o, total, lse, rows, store)
        out_ref[pair, rows:, :] = pick_ref[pair]

    for turn in range(pairs + 2):
        for copy in needed(turn):
            copy.wait()
        for copy in needed(turn + 2):
            copy.start()
        for i in range(chunks):
            if turn < pairs:
                score(turn, i)
            if 0 <= turn - 1 < pairs and i < 6:
                soften(turn - 1, i)
            if turn >= 2 and i in (3, 6):
                weigh(turn - 2, 0 if i == 3 else 1)
        if turn < pairs:
            tops[turn] = jnp.max(top_ref[...], axis=-1, keepdims=True)


def join_kernel(part_ref, fresh_ref, seq_ref, w_hbm, other_w_hbm, out_ref, w_ref, other_w_ref, sem):
    copies = [
        pltpu.make_async_copy(w_hbm, w_ref, sem.at[0]),
        pltpu.make_async_copy(other_w_hbm, other_w_ref, sem.at[1]),
    ]
    for copy in copies:
        copy.start()
    sources, rows = part_ref.shape[0], fresh_ref.shape[0]
    core = seq_ref[0] % 2
    low = lanes((rows, 128)) < HEAD

    def tile(s, j):
        span = slice(j * 128, (j + 1) * 128)
        source = fresh_ref[:, span] if s == sources else part_ref[s, 0:rows, span]
        return source.astype(F32)

    stats = [tile(s, 3) for s in range(sources + 1)]
    lse = [x + pltpu.roll(x, 127, 1) + pltpu.roll(x, 126, 1) for x in stats]
    top = functools.reduce(jnp.maximum, lse)
    weight = [jnp.exp(x - top) for x in lse]
    inverse = 1.0 / functools.reduce(jnp.add, weight)
    heads = []
    for j in range(3):
        total = jnp.zeros((rows, 128), F32)
        for s in range(sources + 1):
            w = weight[s] * inverse
            even, odd = w[:, 3 * j : 3 * j + 1], w[:, 9 + 3 * j : 10 + 3 * j]
            total = total + tile(s, j) * jnp.where(low, even, odd)
        heads.append(jnp.where(core == 0, total, swap(total)).astype(BF16))
    for copy in copies:
        copy.wait()
    out = jnp.zeros((rows, w_ref.shape[1]), F32)
    for j, total in enumerate(heads):
        span = slice(j * HEAD, (j + 1) * HEAD)
        out = out + dot(total, jnp.concatenate([w_ref[span, :], other_w_ref[span, :]], axis=0))
    out = out.astype(BF16)
    each = rows // sources
    for s in range(sources):
        out_ref[s] = out[s * each : (s + 1) * each, :]


def route_kernel(capacity, order_ref, route_ref, gate_ref, place_ref, mix_ref):
    beams, steps = route_ref.shape[0], route_ref.shape[1]
    rows = beams * steps
    slots = place_ref.shape[0]
    slot = lanes((rows, slots))
    routes = jnp.concatenate([route_ref[b] for b in range(beams)], axis=0)
    gates = jnp.concatenate([gate_ref[b] for b in range(beams)], axis=0)
    named = jnp.zeros((rows, slots), F32)
    gate = jnp.zeros((rows, slots), F32)
    for j in range(routes.shape[1]):
        hit = routes[:, j : j + 1] == slot // capacity
        named = jnp.where(hit, 1.0, named)
        gate = jnp.where(hit, gates[:, j : j + 1], gate)
    earlier = jnp.where(
        lanes((rows, rows)) < lax.broadcasted_iota(jnp.int32, (rows, rows), 0), 1.0, 0.0
    )
    rank = dot(earlier.astype(BF16), named.astype(BF16))
    placed = (named > 0.0) & (rank == (slot % capacity).astype(F32))
    mix_ref[...] = jnp.where(placed, gate, 0.0)
    place_ref[...] = jnp.where(placed, 1.0, 0.0).T.astype(BF16)


def dispatch_kernel(x_hbm, sums_ref, gain_hbm, place_ref, hidden_ref, out_ref, x_ref, gain_ref, sem):
    copies = [
        pltpu.make_async_copy(x_hbm, x_ref, sem.at[0]),
        pltpu.make_async_copy(gain_hbm, gain_ref, sem.at[1]),
    ]
    for copy in copies:
        copy.start()
    beams = x_ref.shape[0]
    total = sums_ref[0].astype(F32)
    for s in range(1, sums_ref.shape[0]):
        total = total + sums_ref[s].astype(F32)
    for copy in copies:
        copy.wait()
    inputs = jnp.concatenate([x_ref[b].astype(F32) for b in range(beams)], axis=0)
    hidden = inputs + total
    hidden_ref[...] = hidden
    expert_in = norm(hidden, gain_ref[...].reshape(1, -1)).astype(BF16)
    buffer = dot(place_ref[...], expert_in)
    experts, capacity = out_ref.shape[0], out_ref.shape[1]
    for e in range(experts):
        out_ref[e] = buffer[e * capacity : (e + 1) * capacity, :].astype(BF16)


def expert_kernel(x_ref, w_in_hbm, w_out_ref, out_ref, w_in_ref, rows_ref, sem):
    depth = w_in_ref.shape[1] // 3
    spans = [slice(i * depth, (i + 1) * depth) for i in range(3)]
    copies = [
        pltpu.make_async_copy(w_in_hbm.at[:, span], w_in_ref.at[:, span], sem.at[i])
        for i, span in enumerate(spans)
    ]
    for copy in copies:
        copy.start()
    sources, capacity = x_ref.shape[0], x_ref.shape[1]
    for s in range(sources):
        rows_ref[s * capacity : (s + 1) * capacity, :] = x_ref[s].astype(F32)
    x = rows_ref[...].astype(BF16)
    projected = jnp.zeros((sources * capacity, w_in_ref.shape[2]), F32)
    for copy, span in zip(copies, spans):
        copy.wait()
        projected = projected + dot(x[:, span], w_in_ref[0, span, :])
    half = projected.shape[1] // 2
    g, u = projected[:, 0:half], projected[:, half:]
    act = (g * jax.nn.sigmoid(g) * u).astype(BF16)
    out = dot(act, w_out_ref[0])
    for s in range(sources):
        out_ref[s] = out[s * capacity : (s + 1) * capacity, :].astype(BF16)


def mix_kernel(hidden_ref, mix_ref, back_ref, out_ref, rows_ref):
    experts, capacity = back_ref.shape[0], back_ref.shape[1]
    for e in range(experts):
        rows_ref[e * capacity : (e + 1) * capacity, :] = back_ref[e].astype(F32)
    returned = rows_ref[...].astype(BF16)
    rest = mix_ref[...]
    total = hidden_ref[...]
    for _ in range(3):
        part = rest.astype(BF16)
        rest = rest - part.astype(F32)
        total = total + dot(part, returned)
    steps = out_ref.shape[1]
    for b in range(out_ref.shape[0]):
        out_ref[b] = total[b * steps : (b + 1) * steps, :].astype(BF16)


def final_kernel(seq_ref, parents_ref, part_ref, *refs):
    own_refs, (k_ref, v_ref) = refs[:-2], refs[-2:]
    steps = parents_ref.shape[0]
    here, tail = own_refs[0].shape[1], own_refs[0].shape[2]
    start = part_ref.shape[1] - here * steps
    seq = seq_ref[0]
    for i in range(here):
        beam = seq * here + i
        for s in range(steps - 1, -1, -1):
            beam = parents_ref[s, beam]
        apart = lax.bitwise_xor(beam // here, seq)
        for j, own_ref in enumerate(own_refs):

            @pl.when(apart == j)
            def _():
                k_ref[0:tail, i, :] = own_ref[0, beam % here]
                v_ref[0:tail, i, :] = own_ref[1, beam % here]

        span = slice(start + i * steps, start + (i + 1) * steps)
        for p in range(part_ref.shape[0]):
            k_ref[tail:, i, p * 128 : (p + 1) * 128] = part_ref[p, span, 0:128]
            v_ref[tail:, i, p * 128 : (p + 1) * 128] = part_ref[p, span, 128:256]


def rotary_tables(rows, steps, start):
    half = HEAD // 2
    frequency = ROPE_BASE ** (-(np.arange(half, dtype=np.float64) * 2.0 / HEAD))
    angles = (np.arange(rows) % steps + start)[:, None] * frequency[None, :]
    cosine = np.tile(np.cos(angles), (1, 8)).astype(np.float32)
    sine = np.sin(angles)
    sine = np.tile(np.concatenate([-sine, sine], axis=1), (1, 4)).astype(np.float32)
    return cosine, sine


def block(shape):
    return pl.BlockSpec(shape, lambda i: (0,) * len(shape))


def call(kernel, outs, *args, ins=(), scratch=(), mib=32):
    specs = list(ins) + [block(a.shape) for a in args[len(ins) :]]
    return pl.pallas_call(
        kernel,
        grid=(1,),
        out_shape=outs,
        in_specs=specs,
        out_specs=jax.tree.map(lambda o: block(o.shape), outs),
        scratch_shapes=list(scratch),
        compiler_params=params(mib),
        cost_estimate=pl.CostEstimate(
            flops=1 << 20, bytes_accessed=1 << 20, transcendentals=0
        ),
    )(*args)


def shaped(shape, dtype=BF16):
    return jax.ShapeDtypeStruct(shape, dtype)


def local(
    inputs,
    parents,
    block_len,
    prompt_key_cache,
    prompt_value_cache,
    generated_key_cache,
    generated_value_cache,
    gain_attn,
    gain_moe,
    w_query,
    key_projection_weight,
    value_projection_weight,
    w_output,
    w_in,
    w_out,
    routes,
    gate_weights,
):
    def stay(a):
        return pltpu.with_memory_space_constraint(a, pltpu.MemorySpace.HBM)

    n_seq = lax.axis_size("seq")
    n_req = lax.axis_size("req")
    n_chips = n_seq // 2
    seq = lax.axis_index("seq").astype(jnp.int32).reshape(1)
    here, steps, width = inputs.shape[1:]
    local_rows = here * steps
    rows = local_rows * n_chips
    keys, kv_width = prompt_key_cache.shape[1:]
    tail = generated_key_cache.shape[2]
    capacity = 4
    x = stay(inputs[0])
    anywhere = pl.BlockSpec(memory_space=pl.ANY)
    same_core = [[2 * z + core for z in range(n_chips)] for core in range(2)]

    def exchange(a, axis):
        return lax.all_to_all(a, axis, split_axis=0, concat_axis=0, tiled=True)

    def exchange_chips(a):
        return lax.all_to_all(
            a, "seq", split_axis=0, concat_axis=0, tiled=True, axis_index_groups=same_core
        )

    def apart(a, distance):
        return lax.ppermute(a, "seq", [(i, i ^ distance) for i in range(n_seq)])

    def of_other_core(a):
        return apart(a, 1)

    normed = call(norm_kernel, shaped((n_chips, local_rows, width)), x, stay(gain_attn))
    weights = [w_query.T, key_projection_weight.T, value_projection_weight.T]
    prompt = [prompt_key_cache[0], prompt_value_cache[0]]
    normed, *traded = lax.optimization_barrier((normed, *weights, *prompt, w_output))
    normed_all = exchange_chips(normed)
    traded = [of_other_core(a) for a in traded]
    other_weights, other_prompt, other_w_output = traded[:3], traded[3:5], traded[5]
    own = call(
        pack_kernel,
        shaped((2, here, tail, kv_width)),
        normed,
        stay(generated_key_cache[0]),
        stay(generated_value_cache[0]),
        ins=[anywhere],
    )
    other_own = apart(own, 1)
    bias, extra, fresh_bias, final = call(
        functools.partial(mask_kernel, tail, here),
        (
            shaped((8, 2 * keys), F32),
            shaped((rows, 128), F32),
            shaped((rows, 128), F32),
            shaped((rows, 128)),
        ),
        normed,
        seq,
        parents[0],
        block_len,
        apart(block_len, 1),
        ins=[anywhere, scalars(), scalars(), scalars(), scalars()],
    )
    cosine, sine = map(jnp.asarray, rotary_tables(rows, steps, keys * n_seq + tail))
    q, kv = call(
        project_kernel,
        (shaped((n_chips, 3 * rows, 128)), shaped((2, rows, 128))),
        normed_all,
        seq,
        *[stay(w) for w in weights],
        other_weights[0],
        *map(stay, other_weights[1:]),
        stay(cosine),
        stay(sine),
        ins=[block(normed_all.shape), scalars()],
    )
    q_all = exchange_chips(q)
    fresh, pick = call(
        fresh_kernel,
        (shaped((rows, 512)), shaped((n_chips, local_rows, 512))),
        q,
        kv,
        apart(kv, 1),
        fresh_bias,
        final,
    )

    resident = pl.BlockSpec(memory_space=pltpu.VMEM)
    operands = (bias, extra, q_all, own, other_own, pick, other_prompt[0])
    partial_shape = shaped((n_chips, rows + local_rows, 512))
    partial = pl.pallas_call(
        attend_kernel,
        grid=(1,),
        out_shape=partial_shape,
        in_specs=[resident] * len(operands) + [anywhere] * 3,
        out_specs=block(partial_shape.shape),
        scratch_shapes=[pltpu.VMEM((keys, kv_width), BF16)] * 3
        + [
            pltpu.VMEM((6 * rows, 2 * keys + 128), F32),
            pltpu.VMEM((6 * rows, 2 * keys + 128), F32),
            pltpu.VMEM((6 * rows, 2 * keys + 128), BF16),
            pltpu.VMEM((6 * rows, 2 * keys + 128), BF16),
            pltpu.VMEM((6 * rows, 128), F32),
            pltpu.SemaphoreType.DMA((kv_width // 128, 3)),
        ],
        compiler_params=params(32),
        cost_estimate=pl.CostEstimate(
            flops=4 * 24 * rows * 2 * keys * HEAD,
            bytes_accessed=8 * keys * kv_width,
            transcendentals=24 * rows * 2 * keys,
        ),
    )(*operands, *map(stay, prompt), other_prompt[1])
    parts = exchange_chips(partial)
    sums = call(
        join_kernel,
        shaped((n_chips, local_rows, width)),
        parts,
        fresh,
        seq,
        stay(w_output),
        other_w_output,
        ins=[resident, resident, scalars(), anywhere, anywhere],
        scratch=[pltpu.VMEM(w_output.shape, BF16)] * 2 + [pltpu.SemaphoreType.DMA((2,))],
    )
    slots = n_req * capacity
    place, mix = call(
        functools.partial(route_kernel, capacity),
        (shaped((slots, local_rows)), shaped((local_rows, slots), F32)),
        sums,
        stay(routes[0]),
        stay(gate_weights[0]),
        ins=[anywhere],
    )
    sums = exchange_chips(sums)
    hidden, buffer = call(
        dispatch_kernel,
        (shaped((local_rows, width), F32), shaped((n_req, capacity, width))),
        x,
        sums,
        stay(gain_moe),
        place,
        ins=[anywhere, resident, anywhere, resident],
        scratch=[
            pltpu.VMEM(x.shape, BF16),
            pltpu.VMEM((width,), F32),
            pltpu.SemaphoreType.DMA((2,)),
        ],
    )
    own, buffer = lax.optimization_barrier((own, buffer))
    even = [own] + [apart(own, k) for k in range(2, n_seq, 2)]
    buffer = exchange(buffer, "req")
    back = call(
        expert_kernel,
        shaped(buffer.shape),
        buffer,
        stay(w_in),
        w_out,
        ins=[resident, anywhere, resident],
        scratch=[
            pltpu.VMEM(w_in.shape, BF16),
            pltpu.VMEM((slots, width), F32),
            pltpu.SemaphoreType.DMA((3,)),
        ],
    )
    back, *even = lax.optimization_barrier((back, *even))
    odd = [other_own] + [apart(a, 1) for a in even[1:]]
    owns = [a for pair in zip(even, odd) for a in pair]
    back = exchange(back, "req")
    mixed = call(
        mix_kernel,
        shaped((here, steps, width)),
        hidden,
        mix,
        back,
        ins=[resident] * 3,
        scratch=[pltpu.VMEM((slots, width), F32)],
    )
    final_k, final_v = call(
        final_kernel,
        (shaped((tail + steps, here, kv_width)),) * 2,
        seq,
        parents[0],
        parts,
        *owns,
        ins=[scalars(), scalars()],
    )
    return (
        mixed[None],
        final_k.transpose(1, 0, 2)[None],
        final_v.transpose(1, 0, 2)[None],
    )


def solution(mesh):
    placed = (
        P("req", "seq", None, None),
        P("req", None, None),
        P("req", "seq"),
        P("req", "seq", None),
        P("req", "seq", None),
        P("req", "seq", None, None),
        P("req", "seq", None, None),
        P(),
        P(),
        P(None, "seq"),
        P(None, "seq"),
        P(None, "seq"),
        P("seq", None),
        P("req", None, None),
        P("req", None, None),
        P("req", "seq", None, None),
        P("req", "seq", None, None),
    )
    return jax.shard_map(
        local,
        mesh=mesh,
        in_specs=placed,
        out_specs=(P("req", "seq", None, None),) * 3,
        check_vma=False,
    )
```

```python
import functools

import jax
import jax.numpy as jnp
import numpy as np
from jax import lax
from jax.experimental import pallas as pl
from jax.experimental.pallas import tpu as pltpu
from jax.sharding import PartitionSpec as P

HEAD = 64
BLK = 128
EPSILON = 1e-05
ROPE_BASE = 10000.0
FILL = -(2.0**100)
SCALE = 0.125
BF16 = jnp.bfloat16
F32 = jnp.float32


def scalars():
    return pl.BlockSpec(memory_space=pltpu.SMEM)


def params(mib):
    return pltpu.CompilerParams(vmem_limit_bytes=mib << 20)


def dot(a, b):
    return jnp.dot(a, b, preferred_element_type=F32)


def dot_t(a, b):
    return lax.dot_general(a, b, (((1,), (1,)), ((), ())), preferred_element_type=F32)


def lanes(shape):
    return lax.broadcasted_iota(jnp.int32, shape, len(shape) - 1)


def norm(x, gain):
    mean_sq = jnp.mean(x * x, axis=-1, keepdims=True)
    return x * lax.rsqrt(mean_sq + EPSILON) * gain


def norm_kernel(x_ref, gain_ref, out_ref):
    beams, steps = x_ref.shape[0], x_ref.shape[1]
    gain = gain_ref[...].reshape(1, -1)
    rows = [norm(x_ref[b].astype(F32), gain) for b in range(beams)]
    rows = jnp.concatenate(rows, axis=0).astype(BF16)
    for d in range(out_ref.shape[0]):
        out_ref[d] = rows


def pack_kernel(order_ref, own_k_ref, own_v_ref, out_ref):
    out_ref[0] = own_k_ref[...]
    out_ref[1] = own_v_ref[...]


def stage_kernel(order_ref, source, out_ref, sem):
    copy = pltpu.make_async_copy(source.at[:, 0 : out_ref.shape[1]], out_ref, sem)
    copy.start()
    copy.wait()


def swap(x):
    return pltpu.roll(x, HEAD, 1)


def even_odd(own, other, core):
    return jnp.where(core == 0, own, other), jnp.where(core == 0, other, own)


def project_kernel(
    x_ref,
    seq_ref,
    wq_ref,
    wk_ref,
    wv_ref,
    other_wq_ref,
    other_wk_ref,
    other_wv_ref,
    cos_ref,
    sin_ref,
    q_ref,
    kv_ref,
):
    core = seq_ref[0] % 2
    rows = x_ref.shape[0] * x_ref.shape[1]
    x = x_ref[...].reshape(rows, x_ref.shape[2])
    half = HEAD // 2

    def turned(wq, wk):
        y = jnp.concatenate([dot_t(x, wq) * SCALE, dot_t(x, wk)], axis=1)
        first = lanes(y.shape) % HEAD < half
        width = y.shape[1]
        turn = jnp.where(first, pltpu.roll(y, width - half, 1), pltpu.roll(y, half, 1))
        return y * cos_ref[...] + turn * sin_ref[...]

    y = turned(wq_ref[...], wk_ref[...])
    z = turned(other_wq_ref[...], other_wk_ref[...])
    even, odd = even_odd(y, z, core)
    v_even, v_odd = even_odd(dot_t(x, wv_ref[...]), dot_t(x, other_wv_ref[...]), core)
    low = lanes((rows, 128)) < HEAD
    e0, e1, o0, o1 = even[:, 0:128], even[:, 128:256], odd[:, 0:128], odd[:, 128:256]
    tiles = [
        jnp.where(low, e0, swap(o0)),
        jnp.where(low, swap(e0), o0),
        jnp.where(low, e1, swap(o1)),
    ]
    q = jnp.concatenate(tiles, axis=0).astype(BF16)
    for d in range(q_ref.shape[0]):
        q_ref[d] = q
    kv_ref[0] = jnp.where(low, swap(e1), o1).astype(BF16)
    kv_ref[1] = jnp.concatenate([v_even, v_odd], axis=1).astype(BF16)


def lookup(parents_ref, step, cur, beams):
    found = jnp.zeros(cur.shape, jnp.int32)
    for b in range(beams):
        found = jnp.where(cur == b, parents_ref[step, b], found)
    return found


def mask_kernel(
    tail,
    here,
    order_ref,
    seq_ref,
    parents_ref,
    len_ref,
    other_len_ref,
    bias_ref,
    extra_ref,
    fresh_ref,
    final_ref,
):
    steps, beams = parents_ref.shape
    seq = seq_ref[0]
    core = seq % 2
    other = seq + 1 - 2 * core
    shape = extra_ref.shape
    rows = shape[0]
    lane = lanes(shape)
    spot = lanes((bias_ref.shape[0], BLK))
    half = bias_ref.shape[1] // 2
    for source, start in ((len_ref, 0), (other_len_ref, half)):
        for j in range(half // BLK):
            at = start + j * BLK
            bias_ref[:, at : at + BLK] = jnp.where(spot < source[0, j], 0.0, FILL)
    row = lax.broadcasted_iota(jnp.int32, shape, 0)

    def beam_of(place, parity):
        return (place // (here * steps)) * 2 * here + parity * here + place // steps % here

    step = row % steps
    key = lane % rows
    key_beam = beam_of(key, jnp.where(lane < rows, core, 1 - core))
    key_step = key % steps
    real = lane < 2 * rows
    cur = beam_of(row, core)
    end = cur
    live = jnp.zeros(shape, jnp.int32)
    chosen = jnp.zeros(shape, jnp.int32)
    for s in range(steps - 1, -1, -1):
        here_now = real & (key_step == s)
        live = live | jnp.where(here_now & (cur == key_beam) & (step >= s), 1, 0)
        chosen = chosen | jnp.where(here_now & (end == key_beam) & (step == s), 1, 0)
        cur = jnp.where(step >= s, lookup(parents_ref, s, cur, beams), cur)
        end = jnp.where(step < s, lookup(parents_ref, s, end, beams), end)
    fresh_ref[...] = jnp.where(live > 0, 0.0, FILL)
    final_ref[...] = jnp.where(chosen > 0, 1.0, 0.0).astype(BF16)
    own_keys = here * tail
    holder = jnp.where(lane < own_keys, seq, other)
    own_beam = holder * here + lane % own_keys // tail
    extra_ref[...] = jnp.where((lane < 2 * own_keys) & (cur == own_beam), 0.0, FILL)


def split_heads(q_ref, rows):
    low = lanes((3 * rows, 128)) < HEAD
    q = q_ref[...].reshape(3 * rows, 128).astype(F32)
    both = [jnp.where(low, q, 0.0), jnp.where(low, 0.0, q)]
    return jnp.concatenate(both, axis=0).astype(BF16)


def pack_partial(o, total, lse, rows, store):
    lane = lanes((rows, 128))
    low = lane < HEAD
    stats = jnp.zeros((rows, 128), F32)
    for i in range(6):
        rest = lse[i]
        for piece in range(3):
            part = rest.astype(BF16).astype(F32)
            rest = rest - part
            stats = jnp.where(lane == 3 * i + piece, part, stats)
    for j in range(3):
        even = o[j * rows : (j + 1) * rows, :] / total[j]
        odd = o[(3 + j) * rows : (4 + j) * rows, :] / total[3 + j]
        store(j, jnp.where(low, even, odd).astype(BF16))
    store(3, stats.astype(BF16))


def fresh_kernel(q_ref, kv_ref, other_ref, bias_ref, final_ref, out_ref, pick_ref):
    rows = kv_ref.shape[1]
    q = split_heads(q_ref.at[0], rows)
    fill = jnp.zeros((128 - 2 * rows, 128), BF16)
    k = jnp.concatenate([kv_ref[0], other_ref[0], fill], axis=0)
    v = jnp.concatenate([kv_ref[1], other_ref[1], fill], axis=0)
    s = dot_t(q, k)
    probs, total, lse = [], [], []
    for i in range(6):
        piece = s[i * rows : (i + 1) * rows, :] + bias_ref[...]
        top = jnp.max(piece, axis=-1, keepdims=True)
        e = jnp.exp(piece - top)
        total.append(jnp.sum(e, axis=-1, keepdims=True))
        lse.append(top + jnp.log(total[i]))
        probs.append(e.astype(BF16))
    o = dot(jnp.concatenate(probs, axis=0), v)

    def store(j, tile):
        out_ref[:, j * 128 : (j + 1) * 128] = tile

    pack_partial(o, total, lse, rows, store)
    pick_k = dot(final_ref[...], k).astype(BF16)
    pick_v = dot(final_ref[...], v).astype(BF16)
    each = pick_ref.shape[1]
    for d in range(pick_ref.shape[0]):
        pick_ref[d, :, 0:128] = pick_k[d * each : (d + 1) * each, :]
        pick_ref[d, :, 128:256] = pick_v[d * each : (d + 1) * each, :]
        pick_ref[d, :, 256:512] = jnp.zeros((each, 256), BF16)


def attend_kernel(
    bias_ref,
    extra_ref,
    q_ref,
    own_ref,
    other_own_ref,
    pick_ref,
    *refs,
):
    other_k_ref, first_k_ref, sources = refs[0], refs[1], refs[2:5]
    out_ref, held = refs[5], refs[6:9]
    score_refs, prob_refs, top_ref, sem = refs[9:11], refs[11:13], refs[13], refs[14]
    k_ref, v_ref, other_v_ref = held
    rows = extra_ref.shape[0]
    half = k_ref.shape[0]
    keys = 2 * half
    own_keys = own_ref.shape[1] * own_ref.shape[2]
    pairs = q_ref.shape[0]
    chunk = 512
    chunks = keys // chunk
    fill = jnp.zeros((128 - 2 * own_keys, 128), BF16)

    def lane_span(pair):
        return slice(pair * 128, (pair + 1) * 128)

    copies = {}
    for pair in range(pairs):
        for i in range(3):
            copies[pair, i] = pltpu.make_async_copy(
                sources[i].at[:, lane_span(pair)], held[i].at[:, lane_span(pair)], sem.at[pair, i]
            )

    staged = first_k_ref.shape[1] // 128

    def needed(turn):
        keys_of = [copies[turn, 0]] if staged <= turn < pairs else []
        return keys_of + [copies[turn - 1, i] for i in (1, 2) if 1 <= turn <= pairs]

    for copy in needed(0) + needed(1):
        copy.start()

    def extra(pair, i):
        both = [r[i, :, :, lane_span(pair)].reshape(own_keys, 128) for r in (own_ref, other_own_ref)]
        return jnp.concatenate([*both, fill], axis=0)

    def fold(x):
        tiles = [x[:, at : at + 128] for at in range(0, x.shape[1], 128)]
        return functools.reduce(jnp.maximum, tiles)

    queries = {}

    def score(pair, i):
        s_ref = score_refs[pair % 2]
        if i == 0:
            queries[pair] = split_heads(q_ref.at[pair], rows)
            s = dot_t(queries[pair], extra(pair, 0))
            s = s + jnp.concatenate([extra_ref[...]] * 6, axis=0)
            s_ref[:, keys:] = s
            top = s
        else:
            top = top_ref[...]
        at = i * chunk
        own_k_ref = first_k_ref if pair < staged else k_ref
        source, start = (own_k_ref, at) if at < half else (other_k_ref, at - half)
        s = dot_t(queries[pair], source[start : start + chunk, lane_span(pair)])
        s = s + bias_ref[0:1, at : at + chunk]
        s_ref[:, at : at + chunk] = s
        top_ref[...] = jnp.maximum(top, fold(s))

    tops, totals = {}, {}

    def soften(pair, i):
        s_ref, p_ref = score_refs[pair % 2], prob_refs[pair % 2]
        span = slice(i * rows, (i + 1) * rows)
        top = tops[pair][span, :]
        total = jnp.zeros((rows, 128), F32)
        for at in range(0, keys + 128, 128):
            e = jnp.exp(s_ref[span, at : at + 128] - top)
            total = total + e
            p_ref[span, at : at + 128] = e.astype(BF16)
        totals[pair, i] = jnp.sum(total, axis=-1, keepdims=True)

    summed = {}

    def weigh(pair, part):
        p_ref = prob_refs[pair % 2]
        if part == 0:
            summed[pair] = dot(p_ref[:, 0:half], v_ref[:, lane_span(pair)])
            return
        o = summed[pair] + dot(p_ref[:, half:keys], other_v_ref[:, lane_span(pair)])
        o = o + dot(p_ref[:, keys:], extra(pair, 1))
        total = [totals[pair, i] for i in range(6)]
        lse = [tops[pair][i * rows : (i + 1) * rows, :] + jnp.log(total[i]) for i in range(6)]

        def store(j, tile):
            out_ref[pair, 0:rows, lane_span(j)] = tile

        pack_partial(o, total, lse, rows, store)
        out_ref[pair, rows:, :] = pick_ref[pair]

    for turn in range(pairs + 2):
        for copy in needed(turn):
            copy.wait()
        for copy in needed(turn + 2):
            copy.start()
        for i in range(chunks):
            if turn < pairs:
                score(turn, i)
            if 0 <= turn - 1 < pairs and i < 6:
                soften(turn - 1, i)
            if turn >= 2 and i in (3, 6):
                weigh(turn - 2, 0 if i == 3 else 1)
        if turn < pairs:
            tops[turn] = jnp.max(top_ref[...], axis=-1, keepdims=True)


def join_kernel(part_ref, fresh_ref, seq_ref, w_hbm, other_w_hbm, out_ref, w_ref, other_w_ref, sem):
    copies = [
        pltpu.make_async_copy(w_hbm, w_ref, sem.at[0]),
        pltpu.make_async_copy(other_w_hbm, other_w_ref, sem.at[1]),
    ]
    for copy in copies:
        copy.start()
    sources, rows = part_ref.shape[0], fresh_ref.shape[0]
    core = seq_ref[0] % 2
    low = lanes((rows, 128)) < HEAD

    def tile(s, j):
        span = slice(j * 128, (j + 1) * 128)
        source = fresh_ref[:, span] if s == sources else part_ref[s, 0:rows, span]
        return source.astype(F32)

    stats = [tile(s, 3) for s in range(sources + 1)]
    lse = [x + pltpu.roll(x, 127, 1) + pltpu.roll(x, 126, 1) for x in stats]
    top = functools.reduce(jnp.maximum, lse)
    weight = [jnp.exp(x - top) for x in lse]
    inverse = 1.0 / functools.reduce(jnp.add, weight)
    heads = []
    for j in range(3):
        total = jnp.zeros((rows, 128), F32)
        for s in range(sources + 1):
            w = weight[s] * inverse
            even, odd = w[:, 3 * j : 3 * j + 1], w[:, 9 + 3 * j : 10 + 3 * j]
            total = total + tile(s, j) * jnp.where(low, even, odd)
        heads.append(jnp.where(core == 0, total, swap(total)).astype(BF16))
    for copy in copies:
        copy.wait()
    out = jnp.zeros((rows, w_ref.shape[1]), F32)
    for j, total in enumerate(heads):
        span = slice(j * HEAD, (j + 1) * HEAD)
        out = out + dot(total, jnp.concatenate([w_ref[span, :], other_w_ref[span, :]], axis=0))
    out = out.astype(BF16)
    each = rows // sources
    for s in range(sources):
        out_ref[s] = out[s * each : (s + 1) * each, :]


def route_kernel(capacity, order_ref, route_ref, gate_ref, place_ref, mix_ref):
    beams, steps = route_ref.shape[0], route_ref.shape[1]
    rows = beams * steps
    slots = place_ref.shape[0]
    slot = lanes((rows, slots))
    routes = jnp.concatenate([route_ref[b] for b in range(beams)], axis=0)
    gates = jnp.concatenate([gate_ref[b] for b in range(beams)], axis=0)
    named = jnp.zeros((rows, slots), F32)
    gate = jnp.zeros((rows, slots), F32)
    for j in range(routes.shape[1]):
        hit = routes[:, j : j + 1] == slot // capacity
        named = jnp.where(hit, 1.0, named)
        gate = jnp.where(hit, gates[:, j : j + 1], gate)
    earlier = jnp.where(
        lanes((rows, rows)) < lax.broadcasted_iota(jnp.int32, (rows, rows), 0), 1.0, 0.0
    )
    rank = dot(earlier.astype(BF16), named.astype(BF16))
    placed = (named > 0.0) & (rank == (slot % capacity).astype(F32))
    mix_ref[...] = jnp.where(placed, gate, 0.0)
    place_ref[...] = jnp.where(placed, 1.0, 0.0).T.astype(BF16)


def dispatch_kernel(x_hbm, sums_ref, gain_hbm, place_ref, hidden_ref, out_ref, x_ref, gain_ref, sem):
    copies = [
        pltpu.make_async_copy(x_hbm, x_ref, sem.at[0]),
        pltpu.make_async_copy(gain_hbm, gain_ref, sem.at[1]),
    ]
    for copy in copies:
        copy.start()
    beams = x_ref.shape[0]
    total = sums_ref[0].astype(F32)
    for s in range(1, sums_ref.shape[0]):
        total = total + sums_ref[s].astype(F32)
    for copy in copies:
        copy.wait()
    inputs = jnp.concatenate([x_ref[b].astype(F32) for b in range(beams)], axis=0)
    hidden = inputs + total
    hidden_ref[...] = hidden
    expert_in = norm(hidden, gain_ref[...].reshape(1, -1)).astype(BF16)
    buffer = dot(place_ref[...], expert_in)
    experts, capacity = out_ref.shape[0], out_ref.shape[1]
    for e in range(experts):
        out_ref[e] = buffer[e * capacity : (e + 1) * capacity, :].astype(BF16)


def expert_kernel(x_ref, w_in_hbm, w_out_ref, out_ref, w_in_ref, rows_ref, sem):
    depth = w_in_ref.shape[1] // 3
    spans = [slice(i * depth, (i + 1) * depth) for i in range(3)]
    copies = [
        pltpu.make_async_copy(w_in_hbm.at[:, span], w_in_ref.at[:, span], sem.at[i])
        for i, span in enumerate(spans)
    ]
    for copy in copies:
        copy.start()
    sources, capacity = x_ref.shape[0], x_ref.shape[1]
    for s in range(sources):
        rows_ref[s * capacity : (s + 1) * capacity, :] = x_ref[s].astype(F32)
    x = rows_ref[...].astype(BF16)
    projected = jnp.zeros((sources * capacity, w_in_ref.shape[2]), F32)
    for copy, span in zip(copies, spans):
        copy.wait()
        projected = projected + dot(x[:, span], w_in_ref[0, span, :])
    half = projected.shape[1] // 2
    g, u = projected[:, 0:half], projected[:, half:]
    act = (g * jax.nn.sigmoid(g) * u).astype(BF16)
    out = dot(act, w_out_ref[0])
    for s in range(sources):
        out_ref[s] = out[s * capacity : (s + 1) * capacity, :].astype(BF16)


def mix_kernel(hidden_ref, mix_ref, back_ref, out_ref, rows_ref):
    experts, capacity = back_ref.shape[0], back_ref.shape[1]
    for e in range(experts):
        rows_ref[e * capacity : (e + 1) * capacity, :] = back_ref[e].astype(F32)
    returned = rows_ref[...].astype(BF16)
    rest = mix_ref[...]
    total = hidden_ref[...]
    for _ in range(3):
        part = rest.astype(BF16)
        rest = rest - part.astype(F32)
        total = total + dot(part, returned)
    steps = out_ref.shape[1]
    for b in range(out_ref.shape[0]):
        out_ref[b] = total[b * steps : (b + 1) * steps, :].astype(BF16)


def final_kernel(seq_ref, parents_ref, part_ref, *refs):
    own_refs, (k_ref, v_ref) = refs[:-2], refs[-2:]
    steps = parents_ref.shape[0]
    here, tail = own_refs[0].shape[1], own_refs[0].shape[2]
    start = part_ref.shape[1] - here * steps
    seq = seq_ref[0]
    for i in range(here):
        beam = seq * here + i
        for s in range(steps - 1, -1, -1):
            beam = parents_ref[s, beam]
        apart = lax.bitwise_xor(beam // here, seq)
        for j, own_ref in enumerate(own_refs):

            @pl.when(apart == j)
            def _():
                k_ref[0:tail, i, :] = own_ref[0, beam % here]
                v_ref[0:tail, i, :] = own_ref[1, beam % here]

        span = slice(start + i * steps, start + (i + 1) * steps)
        for p in range(part_ref.shape[0]):
            k_ref[tail:, i, p * 128 : (p + 1) * 128] = part_ref[p, span, 0:128]
            v_ref[tail:, i, p * 128 : (p + 1) * 128] = part_ref[p, span, 128:256]


def rotary_tables(rows, steps, start):
    half = HEAD // 2
    frequency = ROPE_BASE ** (-(np.arange(half, dtype=np.float64) * 2.0 / HEAD))
    angles = (np.arange(rows) % steps + start)[:, None] * frequency[None, :]
    cosine = np.tile(np.cos(angles), (1, 8)).astype(np.float32)
    sine = np.sin(angles)
    sine = np.tile(np.concatenate([-sine, sine], axis=1), (1, 4)).astype(np.float32)
    return cosine, sine


def block(shape):
    return pl.BlockSpec(shape, lambda i: (0,) * len(shape))


def call(kernel, outs, *args, ins=(), scratch=(), mib=32):
    specs = list(ins) + [block(a.shape) for a in args[len(ins) :]]
    return pl.pallas_call(
        kernel,
        grid=(1,),
        out_shape=outs,
        in_specs=specs,
        out_specs=jax.tree.map(lambda o: block(o.shape), outs),
        scratch_shapes=list(scratch),
        compiler_params=params(mib),
        cost_estimate=pl.CostEstimate(
            flops=1 << 20, bytes_accessed=1 << 20, transcendentals=0
        ),
    )(*args)


def shaped(shape, dtype=BF16):
    return jax.ShapeDtypeStruct(shape, dtype)


def local(
    inputs,
    parents,
    block_len,
    prompt_key_cache,
    prompt_value_cache,
    generated_key_cache,
    generated_value_cache,
    gain_attn,
    gain_moe,
    w_query,
    key_projection_weight,
    value_projection_weight,
    w_output,
    w_in,
    w_out,
    routes,
    gate_weights,
):
    def stay(a):
        return pltpu.with_memory_space_constraint(a, pltpu.MemorySpace.HBM)

    n_seq = lax.axis_size("seq")
    n_req = lax.axis_size("req")
    n_chips = n_seq // 2
    seq = lax.axis_index("seq").astype(jnp.int32).reshape(1)
    here, steps, width = inputs.shape[1:]
    local_rows = here * steps
    rows = local_rows * n_chips
    keys, kv_width = prompt_key_cache.shape[1:]
    tail = generated_key_cache.shape[2]
    capacity = 4
    x = stay(inputs[0])
    anywhere = pl.BlockSpec(memory_space=pl.ANY)
    same_core = [[2 * z + core for z in range(n_chips)] for core in range(2)]

    def exchange(a, axis):
        return lax.all_to_all(a, axis, split_axis=0, concat_axis=0, tiled=True)

    def exchange_chips(a):
        return lax.all_to_all(
            a, "seq", split_axis=0, concat_axis=0, tiled=True, axis_index_groups=same_core
        )

    def apart(a, distance):
        return lax.ppermute(a, "seq", [(i, i ^ distance) for i in range(n_seq)])

    def of_other_core(a):
        return apart(a, 1)

    normed = call(norm_kernel, shaped((n_chips, local_rows, width)), x, stay(gain_attn))
    weights = [w_query.T, key_projection_weight.T, value_projection_weight.T]
    prompt = [prompt_key_cache[0], prompt_value_cache[0]]
    normed, *traded = lax.optimization_barrier((normed, *weights, *prompt, w_output))
    normed_all = exchange_chips(normed)
    traded = [of_other_core(a) for a in traded]
    other_weights, other_prompt, other_w_output = traded[:3], traded[3:5], traded[5]
    own = call(
        pack_kernel,
        shaped((2, here, tail, kv_width)),
        normed,
        stay(generated_key_cache[0]),
        stay(generated_value_cache[0]),
        ins=[anywhere],
    )
    other_own = apart(own, 1)
    bias, extra, fresh_bias, final = call(
        functools.partial(mask_kernel, tail, here),
        (
            shaped((8, 2 * keys), F32),
            shaped((rows, 128), F32),
            shaped((rows, 128), F32),
            shaped((rows, 128)),
        ),
        normed,
        seq,
        parents[0],
        block_len,
        apart(block_len, 1),
        ins=[anywhere, scalars(), scalars(), scalars(), scalars()],
    )
    cosine, sine = map(jnp.asarray, rotary_tables(rows, steps, keys * n_seq + tail))
    q, kv = call(
        project_kernel,
        (shaped((n_chips, 3 * rows, 128)), shaped((2, rows, 128))),
        normed_all,
        seq,
        *[stay(w) for w in weights],
        *other_weights,
        stay(cosine),
        stay(sine),
        ins=[block(normed_all.shape), scalars()],
    )
    q_all = exchange_chips(q)
    fresh, pick = call(
        fresh_kernel,
        (shaped((rows, 512)), shaped((n_chips, local_rows, 512))),
        q,
        kv,
        apart(kv, 1),
        fresh_bias,
        final,
    )

    resident = pl.BlockSpec(memory_space=pltpu.VMEM)
    first_k = pl.pallas_call(
        stage_kernel,
        out_shape=shaped((keys, 128)),
        in_specs=[anywhere] * 2,
        out_specs=resident,
        scratch_shapes=[pltpu.SemaphoreType.DMA],
        compiler_params=params(4),
    )(q, stay(prompt[0]))
    operands = (bias, extra, q_all, own, other_own, pick, other_prompt[0], first_k)
    partial_shape = shaped((n_chips, rows + local_rows, 512))
    partial = pl.pallas_call(
        attend_kernel,
        grid=(1,),
        out_shape=partial_shape,
        in_specs=[resident] * len(operands) + [anywhere] * 3,
        out_specs=block(partial_shape.shape),
        scratch_shapes=[pltpu.VMEM((keys, kv_width), BF16)] * 3
        + [
            pltpu.VMEM((6 * rows, 2 * keys + 128), F32),
            pltpu.VMEM((6 * rows, 2 * keys + 128), F32),
            pltpu.VMEM((6 * rows, 2 * keys + 128), BF16),
            pltpu.VMEM((6 * rows, 2 * keys + 128), BF16),
            pltpu.VMEM((6 * rows, 128), F32),
            pltpu.SemaphoreType.DMA((kv_width // 128, 3)),
        ],
        compiler_params=params(32),
        cost_estimate=pl.CostEstimate(
            flops=4 * 24 * rows * 2 * keys * HEAD,
            bytes_accessed=8 * keys * kv_width,
            transcendentals=24 * rows * 2 * keys,
        ),
    )(*operands, *map(stay, prompt), other_prompt[1])
    parts = exchange_chips(partial)
    sums = call(
        join_kernel,
        shaped((n_chips, local_rows, width)),
        parts,
        fresh,
        seq,
        stay(w_output),
        other_w_output,
        ins=[resident, resident, scalars(), anywhere, anywhere],
        scratch=[pltpu.VMEM(w_output.shape, BF16)] * 2 + [pltpu.SemaphoreType.DMA((2,))],
    )
    slots = n_req * capacity
    place, mix = call(
        functools.partial(route_kernel, capacity),
        (shaped((slots, local_rows)), shaped((local_rows, slots), F32)),
        sums,
        stay(routes[0]),
        stay(gate_weights[0]),
        ins=[anywhere],
    )
    sums = exchange_chips(sums)
    hidden, buffer = call(
        dispatch_kernel,
        (shaped((local_rows, width), F32), shaped((n_req, capacity, width))),
        x,
        sums,
        stay(gain_moe),
        place,
        ins=[anywhere, resident, anywhere, resident],
        scratch=[
            pltpu.VMEM(x.shape, BF16),
            pltpu.VMEM((width,), F32),
            pltpu.SemaphoreType.DMA((2,)),
        ],
    )
    own, buffer = lax.optimization_barrier((own, buffer))
    even = [own] + [apart(own, k) for k in range(2, n_seq, 2)]
    buffer = exchange(buffer, "req")
    back = call(
        expert_kernel,
        shaped(buffer.shape),
        buffer,
        stay(w_in),
        w_out,
        ins=[resident, anywhere, resident],
        scratch=[
            pltpu.VMEM(w_in.shape, BF16),
            pltpu.VMEM((slots, width), F32),
            pltpu.SemaphoreType.DMA((3,)),
        ],
    )
    back, *even = lax.optimization_barrier((back, *even))
    odd = [other_own] + [apart(a, 1) for a in even[1:]]
    owns = [a for pair in zip(even, odd) for a in pair]
    back = exchange(back, "req")
    mixed = call(
        mix_kernel,
        shaped((here, steps, width)),
        hidden,
        mix,
        back,
        ins=[resident] * 3,
        scratch=[pltpu.VMEM((slots, width), F32)],
    )
    final_k, final_v = call(
        final_kernel,
        (shaped((tail + steps, here, kv_width)),) * 2,
        seq,
        parents[0],
        parts,
        *owns,
        ins=[scalars(), scalars()],
    )
    return (
        mixed[None],
        final_k.transpose(1, 0, 2)[None],
        final_v.transpose(1, 0, 2)[None],
    )


def solution(mesh):
    placed = (
        P("req", "seq", None, None),
        P("req", None, None),
        P("req", "seq"),
        P("req", "seq", None),
        P("req", "seq", None),
        P("req", "seq", None, None),
        P("req", "seq", None, None),
        P(),
        P(),
        P(None, "seq"),
        P(None, "seq"),
        P(None, "seq"),
        P("seq", None),
        P("req", None, None),
        P("req", None, None),
        P("req", "seq", None, None),
        P("req", "seq", None, None),
    )
    return jax.shard_map(
        local,
        mesh=mesh,
        in_specs=placed,
        out_specs=(P("req", "seq", None, None),) * 3,
        check_vma=False,
    )
```

```python
import functools

import jax
import jax.numpy as jnp
import numpy as np
from jax import lax
from jax.experimental import pallas as pl
from jax.experimental.pallas import tpu as pltpu
from jax.sharding import PartitionSpec as P

HEAD = 64
BLK = 128
EPSILON = 1e-05
ROPE_BASE = 10000.0
FILL = -(2.0**100)
SCALE = 0.125
BF16 = jnp.bfloat16
F32 = jnp.float32


def scalars():
    return pl.BlockSpec(memory_space=pltpu.SMEM)


def params(mib):
    return pltpu.CompilerParams(vmem_limit_bytes=mib << 20)


def dot(a, b):
    return jnp.dot(a, b, preferred_element_type=F32)


def dot_t(a, b):
    return lax.dot_general(a, b, (((1,), (1,)), ((), ())), preferred_element_type=F32)


def lanes(shape):
    return lax.broadcasted_iota(jnp.int32, shape, len(shape) - 1)


def norm(x, gain):
    mean_sq = jnp.mean(x * x, axis=-1, keepdims=True)
    return x * lax.rsqrt(mean_sq + EPSILON) * gain


def norm_kernel(x_ref, gain_ref, out_ref):
    beams, steps = x_ref.shape[0], x_ref.shape[1]
    gain = gain_ref[...].reshape(1, -1)
    rows = [norm(x_ref[b].astype(F32), gain) for b in range(beams)]
    rows = jnp.concatenate(rows, axis=0).astype(BF16)
    for d in range(out_ref.shape[0]):
        out_ref[d] = rows


def pack_kernel(order_ref, own_k_ref, own_v_ref, out_ref):
    out_ref[0] = own_k_ref[...]
    out_ref[1] = own_v_ref[...]


def swap(x):
    return pltpu.roll(x, HEAD, 1)


def even_odd(own, other, core):
    return jnp.where(core == 0, own, other), jnp.where(core == 0, other, own)


def project_kernel(
    x_ref,
    seq_ref,
    wq_ref,
    wk_ref,
    wv_ref,
    other_wq_ref,
    other_wk_ref,
    other_wv_ref,
    cos_ref,
    sin_ref,
    q_ref,
    kv_ref,
):
    core = seq_ref[0] % 2
    rows = x_ref.shape[0] * x_ref.shape[1]
    x = x_ref[...].reshape(rows, x_ref.shape[2])
    half = HEAD // 2

    def turned(wq, wk):
        y = jnp.concatenate([dot_t(x, wq) * SCALE, dot_t(x, wk)], axis=1)
        first = lanes(y.shape) % HEAD < half
        width = y.shape[1]
        turn = jnp.where(first, pltpu.roll(y, width - half, 1), pltpu.roll(y, half, 1))
        return y * cos_ref[...] + turn * sin_ref[...]

    y = turned(wq_ref[...], wk_ref[...])
    z = turned(other_wq_ref[...], other_wk_ref[...])
    even, odd = even_odd(y, z, core)
    v_even, v_odd = even_odd(dot_t(x, wv_ref[...]), dot_t(x, other_wv_ref[...]), core)
    low = lanes((rows, 128)) < HEAD
    e0, e1, o0, o1 = even[:, 0:128], even[:, 128:256], odd[:, 0:128], odd[:, 128:256]
    tiles = [
        jnp.where(low, e0, swap(o0)),
        jnp.where(low, swap(e0), o0),
        jnp.where(low, e1, swap(o1)),
    ]
    q = jnp.concatenate(tiles, axis=0).astype(BF16)
    for d in range(q_ref.shape[0]):
        q_ref[d] = q
    kv_ref[0] = jnp.where(low, swap(e1), o1).astype(BF16)
    kv_ref[1] = jnp.concatenate([v_even, v_odd], axis=1).astype(BF16)


def lookup(parents_ref, step, cur, beams):
    found = jnp.zeros(cur.shape, jnp.int32)
    for b in range(beams):
        found = jnp.where(cur == b, parents_ref[step, b], found)
    return found


def mask_kernel(
    tail,
    here,
    order_ref,
    seq_ref,
    parents_ref,
    len_ref,
    other_len_ref,
    bias_ref,
    extra_ref,
    fresh_ref,
    final_ref,
):
    steps, beams = parents_ref.shape
    seq = seq_ref[0]
    core = seq % 2
    other = seq + 1 - 2 * core
    shape = extra_ref.shape
    rows = shape[0]
    lane = lanes(shape)
    spot = lanes((bias_ref.shape[0], BLK))
    half = bias_ref.shape[1] // 2
    for source, start in ((len_ref, 0), (other_len_ref, half)):
        for j in range(half // BLK):
            at = start + j * BLK
            bias_ref[:, at : at + BLK] = jnp.where(spot < source[0, j], 0.0, FILL)
    row = lax.broadcasted_iota(jnp.int32, shape, 0)

    def beam_of(place, parity):
        return (place // (here * steps)) * 2 * here + parity * here + place // steps % here

    step = row % steps
    key = lane % rows
    key_beam = beam_of(key, jnp.where(lane < rows, core, 1 - core))
    key_step = key % steps
    real = lane < 2 * rows
    cur = beam_of(row, core)
    end = cur
    live = jnp.zeros(shape, jnp.int32)
    chosen = jnp.zeros(shape, jnp.int32)
    for s in range(steps - 1, -1, -1):
        here_now = real & (key_step == s)
        live = live | jnp.where(here_now & (cur == key_beam) & (step >= s), 1, 0)
        chosen = chosen | jnp.where(here_now & (end == key_beam) & (step == s), 1, 0)
        cur = jnp.where(step >= s, lookup(parents_ref, s, cur, beams), cur)
        end = jnp.where(step < s, lookup(parents_ref, s, end, beams), end)
    fresh_ref[...] = jnp.where(live > 0, 0.0, FILL)
    final_ref[...] = jnp.where(chosen > 0, 1.0, 0.0).astype(BF16)
    own_keys = here * tail
    holder = jnp.where(lane < own_keys, seq, other)
    own_beam = holder * here + lane % own_keys // tail
    extra_ref[...] = jnp.where((lane < 2 * own_keys) & (cur == own_beam), 0.0, FILL)


def split_heads(q_ref, rows):
    low = lanes((3 * rows, 128)) < HEAD
    q = q_ref[...].reshape(3 * rows, 128).astype(F32)
    both = [jnp.where(low, q, 0.0), jnp.where(low, 0.0, q)]
    return jnp.concatenate(both, axis=0).astype(BF16)


def pack_partial(o, total, lse, rows, store):
    lane = lanes((rows, 128))
    low = lane < HEAD
    stats = jnp.zeros((rows, 128), F32)
    for i in range(6):
        rest = lse[i]
        for piece in range(3):
            part = rest.astype(BF16).astype(F32)
            rest = rest - part
            stats = jnp.where(lane == 3 * i + piece, part, stats)
    for j in range(3):
        even = o[j * rows : (j + 1) * rows, :] / total[j]
        odd = o[(3 + j) * rows : (4 + j) * rows, :] / total[3 + j]
        store(j, jnp.where(low, even, odd).astype(BF16))
    store(3, stats.astype(BF16))


def fresh_kernel(q_ref, kv_ref, other_ref, bias_ref, final_ref, out_ref, pick_ref):
    rows = kv_ref.shape[1]
    q = split_heads(q_ref.at[0], rows)
    fill = jnp.zeros((128 - 2 * rows, 128), BF16)
    k = jnp.concatenate([kv_ref[0], other_ref[0], fill], axis=0)
    v = jnp.concatenate([kv_ref[1], other_ref[1], fill], axis=0)
    s = dot_t(q, k)
    probs, total, lse = [], [], []
    for i in range(6):
        piece = s[i * rows : (i + 1) * rows, :] + bias_ref[...]
        top = jnp.max(piece, axis=-1, keepdims=True)
        e = jnp.exp(piece - top)
        total.append(jnp.sum(e, axis=-1, keepdims=True))
        lse.append(top + jnp.log(total[i]))
        probs.append(e.astype(BF16))
    o = dot(jnp.concatenate(probs, axis=0), v)

    def store(j, tile):
        out_ref[:, j * 128 : (j + 1) * 128] = tile

    pack_partial(o, total, lse, rows, store)
    pick_k = dot(final_ref[...], k).astype(BF16)
    pick_v = dot(final_ref[...], v).astype(BF16)
    each = pick_ref.shape[1]
    for d in range(pick_ref.shape[0]):
        pick_ref[d, :, 0:128] = pick_k[d * each : (d + 1) * each, :]
        pick_ref[d, :, 128:256] = pick_v[d * each : (d + 1) * each, :]
        pick_ref[d, :, 256:512] = jnp.zeros((each, 256), BF16)


def attend_kernel(
    bias_ref,
    extra_ref,
    q_ref,
    own_ref,
    other_own_ref,
    pick_ref,
    *refs,
):
    other_k_ref, sources, out_ref, held = refs[0], refs[1:4], refs[4], refs[5:8]
    score_refs, prob_refs, top_ref, sem = refs[8:10], refs[10:12], refs[12], refs[13]
    k_ref, v_ref, other_v_ref = held
    rows = extra_ref.shape[0]
    half = k_ref.shape[0]
    keys = 2 * half
    own_keys = own_ref.shape[1] * own_ref.shape[2]
    pairs = q_ref.shape[0]
    chunk = 1024
    chunks = keys // chunk
    fill = jnp.zeros((128 - 2 * own_keys, 128), BF16)

    def lane_span(pair):
        return slice(pair * 128, (pair + 1) * 128)

    copies = {}
    for pair in range(pairs):
        for i in range(3):
            copies[pair, i] = pltpu.make_async_copy(
                sources[i].at[:, lane_span(pair)], held[i].at[:, lane_span(pair)], sem.at[pair, i]
            )

    def needed(turn):
        keys_of = [copies[turn, 0]] if turn < pairs else []
        return keys_of + [copies[turn - 1, i] for i in (1, 2) if 1 <= turn <= pairs]

    for copy in needed(0) + needed(1):
        copy.start()

    def extra(pair, i):
        both = [r[i, :, :, lane_span(pair)].reshape(own_keys, 128) for r in (own_ref, other_own_ref)]
        return jnp.concatenate([*both, fill], axis=0)

    def fold(x):
        tiles = [x[:, at : at + 128] for at in range(0, x.shape[1], 128)]
        return functools.reduce(jnp.maximum, tiles)

    queries = {}

    def score(pair, i):
        s_ref = score_refs[pair % 2]
        if i == 0:
            queries[pair] = split_heads(q_ref.at[pair], rows)
            s = dot_t(queries[pair], extra(pair, 0))
            s = s + jnp.concatenate([extra_ref[...]] * 6, axis=0)
            s_ref[:, keys:] = s
            top = s
        else:
            top = top_ref[...]
        at = i * chunk
        source, start = (k_ref, at) if at < half else (other_k_ref, at - half)
        s = dot_t(queries[pair], source[start : start + chunk, lane_span(pair)])
        s = s + bias_ref[0:1, at : at + chunk]
        s_ref[:, at : at + chunk] = s
        top_ref[...] = jnp.maximum(top, fold(s))

    tops, totals = {}, {}

    def soften(pair, i):
        s_ref, p_ref = score_refs[pair % 2], prob_refs[pair % 2]
        span = slice(i * rows, (i + 1) * rows)
        top = tops[pair][span, :]
        total = jnp.zeros((rows, 128), F32)
        for at in range(0, keys + 128, 128):
            e = jnp.exp(s_ref[span, at : at + 128] - top)
            total = total + e
            p_ref[span, at : at + 128] = e.astype(BF16)
        totals[pair, i] = jnp.sum(total, axis=-1, keepdims=True)

    summed = {}

    def weigh(pair, part):
        p_ref = prob_refs[pair % 2]
        if part == 0:
            summed[pair] = dot(p_ref[:, 0:half], v_ref[:, lane_span(pair)])
            return
        o = summed[pair] + dot(p_ref[:, half:keys], other_v_ref[:, lane_span(pair)])
        o = o + dot(p_ref[:, keys:], extra(pair, 1))
        total = [totals[pair, i] for i in range(6)]
        lse = [tops[pair][i * rows : (i + 1) * rows, :] + jnp.log(total[i]) for i in range(6)]

        def store(j, tile):
            out_ref[pair, 0:rows, lane_span(j)] = tile

        pack_partial(o, total, lse, rows, store)
        out_ref[pair, rows:, :] = pick_ref[pair]

    for turn in range(pairs + 2):
        for copy in needed(turn):
            copy.wait()
        for copy in needed(turn + 2):
            copy.start()
        for i in range(chunks):
            if turn < pairs:
                score(turn, i)
            if 0 <= turn - 1 < pairs:
                for part in range(i * 6 // chunks, (i + 1) * 6 // chunks):
                    soften(turn - 1, part)
            if turn >= 2 and i in (1, 3):
                weigh(turn - 2, i // 2)
        if turn < pairs:
            tops[turn] = jnp.max(top_ref[...], axis=-1, keepdims=True)


def join_kernel(part_ref, fresh_ref, seq_ref, w_hbm, other_w_hbm, out_ref, w_ref, other_w_ref, sem):
    copies = [
        pltpu.make_async_copy(w_hbm, w_ref, sem.at[0]),
        pltpu.make_async_copy(other_w_hbm, other_w_ref, sem.at[1]),
    ]
    for copy in copies:
        copy.start()
    sources, rows = part_ref.shape[0], fresh_ref.shape[0]
    core = seq_ref[0] % 2
    low = lanes((rows, 128)) < HEAD

    def tile(s, j):
        span = slice(j * 128, (j + 1) * 128)
        source = fresh_ref[:, span] if s == sources else part_ref[s, 0:rows, span]
        return source.astype(F32)

    stats = [tile(s, 3) for s in range(sources + 1)]
    lse = [x + pltpu.roll(x, 127, 1) + pltpu.roll(x, 126, 1) for x in stats]
    top = functools.reduce(jnp.maximum, lse)
    weight = [jnp.exp(x - top) for x in lse]
    inverse = 1.0 / functools.reduce(jnp.add, weight)
    heads = []
    for j in range(3):
        total = jnp.zeros((rows, 128), F32)
        for s in range(sources + 1):
            w = weight[s] * inverse
            even, odd = w[:, 3 * j : 3 * j + 1], w[:, 9 + 3 * j : 10 + 3 * j]
            total = total + tile(s, j) * jnp.where(low, even, odd)
        heads.append(jnp.where(core == 0, total, swap(total)).astype(BF16))
    for copy in copies:
        copy.wait()
    out = jnp.zeros((rows, w_ref.shape[1]), F32)
    for j, total in enumerate(heads):
        span = slice(j * HEAD, (j + 1) * HEAD)
        out = out + dot(total, jnp.concatenate([w_ref[span, :], other_w_ref[span, :]], axis=0))
    out = out.astype(BF16)
    each = rows // sources
    for s in range(sources):
        out_ref[s] = out[s * each : (s + 1) * each, :]


def route_kernel(capacity, order_ref, route_ref, gate_ref, place_ref, mix_ref):
    beams, steps = route_ref.shape[0], route_ref.shape[1]
    rows = beams * steps
    slots = place_ref.shape[0]
    slot = lanes((rows, slots))
    routes = jnp.concatenate([route_ref[b] for b in range(beams)], axis=0)
    gates = jnp.concatenate([gate_ref[b] for b in range(beams)], axis=0)
    named = jnp.zeros((rows, slots), F32)
    gate = jnp.zeros((rows, slots), F32)
    for j in range(routes.shape[1]):
        hit = routes[:, j : j + 1] == slot // capacity
        named = jnp.where(hit, 1.0, named)
        gate = jnp.where(hit, gates[:, j : j + 1], gate)
    earlier = jnp.where(
        lanes((rows, rows)) < lax.broadcasted_iota(jnp.int32, (rows, rows), 0), 1.0, 0.0
    )
    rank = dot(earlier.astype(BF16), named.astype(BF16))
    placed = (named > 0.0) & (rank == (slot % capacity).astype(F32))
    mix_ref[...] = jnp.where(placed, gate, 0.0)
    place_ref[...] = jnp.where(placed, 1.0, 0.0).T.astype(BF16)


def dispatch_kernel(x_hbm, sums_ref, gain_hbm, place_ref, hidden_ref, out_ref, x_ref, gain_ref, sem):
    copies = [
        pltpu.make_async_copy(x_hbm, x_ref, sem.at[0]),
        pltpu.make_async_copy(gain_hbm, gain_ref, sem.at[1]),
    ]
    for copy in copies:
        copy.start()
    beams = x_ref.shape[0]
    total = sums_ref[0].astype(F32)
    for s in range(1, sums_ref.shape[0]):
        total = total + sums_ref[s].astype(F32)
    for copy in copies:
        copy.wait()
    inputs = jnp.concatenate([x_ref[b].astype(F32) for b in range(beams)], axis=0)
    hidden = inputs + total
    hidden_ref[...] = hidden
    expert_in = norm(hidden, gain_ref[...].reshape(1, -1)).astype(BF16)
    buffer = dot(place_ref[...], expert_in)
    experts, capacity = out_ref.shape[0], out_ref.shape[1]
    for e in range(experts):
        out_ref[e] = buffer[e * capacity : (e + 1) * capacity, :].astype(BF16)


def expert_kernel(x_ref, w_in_hbm, w_out_ref, out_ref, w_in_ref, rows_ref, sem):
    depth = w_in_ref.shape[1] // 3
    spans = [slice(i * depth, (i + 1) * depth) for i in range(3)]
    copies = [
        pltpu.make_async_copy(w_in_hbm.at[:, span], w_in_ref.at[:, span], sem.at[i])
        for i, span in enumerate(spans)
    ]
    for copy in copies:
        copy.start()
    sources, capacity = x_ref.shape[0], x_ref.shape[1]
    for s in range(sources):
        rows_ref[s * capacity : (s + 1) * capacity, :] = x_ref[s].astype(F32)
    x = rows_ref[...].astype(BF16)
    projected = jnp.zeros((sources * capacity, w_in_ref.shape[2]), F32)
    for copy, span in zip(copies, spans):
        copy.wait()
        projected = projected + dot(x[:, span], w_in_ref[0, span, :])
    half = projected.shape[1] // 2
    g, u = projected[:, 0:half], projected[:, half:]
    act = (g * jax.nn.sigmoid(g) * u).astype(BF16)
    out = dot(act, w_out_ref[0])
    for s in range(sources):
        out_ref[s] = out[s * capacity : (s + 1) * capacity, :].astype(BF16)


def mix_kernel(hidden_ref, mix_ref, back_ref, out_ref, rows_ref):
    experts, capacity = back_ref.shape[0], back_ref.shape[1]
    for e in range(experts):
        rows_ref[e * capacity : (e + 1) * capacity, :] = back_ref[e].astype(F32)
    returned = rows_ref[...].astype(BF16)
    rest = mix_ref[...]
    total = hidden_ref[...]
    for _ in range(3):
        part = rest.astype(BF16)
        rest = rest - part.astype(F32)
        total = total + dot(part, returned)
    steps = out_ref.shape[1]
    for b in range(out_ref.shape[0]):
        out_ref[b] = total[b * steps : (b + 1) * steps, :].astype(BF16)


def final_kernel(seq_ref, parents_ref, part_ref, *refs):
    own_refs, (k_ref, v_ref) = refs[:-2], refs[-2:]
    steps = parents_ref.shape[0]
    here, tail = own_refs[0].shape[1], own_refs[0].shape[2]
    start = part_ref.shape[1] - here * steps
    seq = seq_ref[0]
    for i in range(here):
        beam = seq * here + i
        for s in range(steps - 1, -1, -1):
            beam = parents_ref[s, beam]
        apart = lax.bitwise_xor(beam // here, seq)
        for j, own_ref in enumerate(own_refs):

            @pl.when(apart == j)
            def _():
                k_ref[0:tail, i, :] = own_ref[0, beam % here]
                v_ref[0:tail, i, :] = own_ref[1, beam % here]

        span = slice(start + i * steps, start + (i + 1) * steps)
        for p in range(part_ref.shape[0]):
            k_ref[tail:, i, p * 128 : (p + 1) * 128] = part_ref[p, span, 0:128]
            v_ref[tail:, i, p * 128 : (p + 1) * 128] = part_ref[p, span, 128:256]


def rotary_tables(rows, steps, start):
    half = HEAD // 2
    frequency = ROPE_BASE ** (-(np.arange(half, dtype=np.float64) * 2.0 / HEAD))
    angles = (np.arange(rows) % steps + start)[:, None] * frequency[None, :]
    cosine = np.tile(np.cos(angles), (1, 8)).astype(np.float32)
    sine = np.sin(angles)
    sine = np.tile(np.concatenate([-sine, sine], axis=1), (1, 4)).astype(np.float32)
    return cosine, sine


def block(shape):
    return pl.BlockSpec(shape, lambda i: (0,) * len(shape))


def call(kernel, outs, *args, ins=(), scratch=(), mib=32):
    specs = list(ins) + [block(a.shape) for a in args[len(ins) :]]
    return pl.pallas_call(
        kernel,
        grid=(1,),
        out_shape=outs,
        in_specs=specs,
        out_specs=jax.tree.map(lambda o: block(o.shape), outs),
        scratch_shapes=list(scratch),
        compiler_params=params(mib),
        cost_estimate=pl.CostEstimate(
            flops=1 << 20, bytes_accessed=1 << 20, transcendentals=0
        ),
    )(*args)


def shaped(shape, dtype=BF16):
    return jax.ShapeDtypeStruct(shape, dtype)


def local(
    inputs,
    parents,
    block_len,
    prompt_key_cache,
    prompt_value_cache,
    generated_key_cache,
    generated_value_cache,
    gain_attn,
    gain_moe,
    w_query,
    key_projection_weight,
    value_projection_weight,
    w_output,
    w_in,
    w_out,
    routes,
    gate_weights,
):
    def stay(a):
        return pltpu.with_memory_space_constraint(a, pltpu.MemorySpace.HBM)

    n_seq = lax.axis_size("seq")
    n_req = lax.axis_size("req")
    n_chips = n_seq // 2
    seq = lax.axis_index("seq").astype(jnp.int32).reshape(1)
    here, steps, width = inputs.shape[1:]
    local_rows = here * steps
    rows = local_rows * n_chips
    keys, kv_width = prompt_key_cache.shape[1:]
    tail = generated_key_cache.shape[2]
    capacity = 4
    x = stay(inputs[0])
    anywhere = pl.BlockSpec(memory_space=pl.ANY)
    same_core = [[2 * z + core for z in range(n_chips)] for core in range(2)]

    def exchange(a, axis):
        return lax.all_to_all(a, axis, split_axis=0, concat_axis=0, tiled=True)

    def exchange_chips(a):
        return lax.all_to_all(
            a, "seq", split_axis=0, concat_axis=0, tiled=True, axis_index_groups=same_core
        )

    def apart(a, distance):
        return lax.ppermute(a, "seq", [(i, i ^ distance) for i in range(n_seq)])

    def of_other_core(a):
        return apart(a, 1)

    normed = call(norm_kernel, shaped((n_chips, local_rows, width)), x, stay(gain_attn))
    weights = [w_query.T, key_projection_weight.T, value_projection_weight.T]
    prompt = [prompt_key_cache[0], prompt_value_cache[0]]
    normed, *traded = lax.optimization_barrier((normed, *weights, *prompt, w_output))
    normed_all = exchange_chips(normed)
    traded = [of_other_core(a) for a in traded]
    other_weights, other_prompt, other_w_output = traded[:3], traded[3:5], traded[5]
    own = call(
        pack_kernel,
        shaped((2, here, tail, kv_width)),
        normed,
        stay(generated_key_cache[0]),
        stay(generated_value_cache[0]),
        ins=[anywhere],
    )
    other_own = apart(own, 1)
    bias, extra, fresh_bias, final = call(
        functools.partial(mask_kernel, tail, here),
        (
            shaped((8, 2 * keys), F32),
            shaped((rows, 128), F32),
            shaped((rows, 128), F32),
            shaped((rows, 128)),
        ),
        normed,
        seq,
        parents[0],
        block_len,
        apart(block_len, 1),
        ins=[anywhere, scalars(), scalars(), scalars(), scalars()],
    )
    cosine, sine = map(jnp.asarray, rotary_tables(rows, steps, keys * n_seq + tail))
    q, kv = call(
        project_kernel,
        (shaped((n_chips, 3 * rows, 128)), shaped((2, rows, 128))),
        normed_all,
        seq,
        *[stay(w) for w in weights],
        other_weights[0],
        *map(stay, other_weights[1:]),
        stay(cosine),
        stay(sine),
        ins=[block(normed_all.shape), scalars()],
    )
    q_all = exchange_chips(q)
    fresh, pick = call(
        fresh_kernel,
        (shaped((rows, 512)), shaped((n_chips, local_rows, 512))),
        q,
        kv,
        apart(kv, 1),
        fresh_bias,
        final,
    )

    resident = pl.BlockSpec(memory_space=pltpu.VMEM)
    operands = (bias, extra, q_all, own, other_own, pick, other_prompt[0])
    partial_shape = shaped((n_chips, rows + local_rows, 512))
    partial = pl.pallas_call(
        attend_kernel,
        grid=(1,),
        out_shape=partial_shape,
        in_specs=[resident] * len(operands) + [anywhere] * 3,
        out_specs=block(partial_shape.shape),
        scratch_shapes=[pltpu.VMEM((keys, kv_width), BF16)] * 3
        + [
            pltpu.VMEM((6 * rows, 2 * keys + 128), F32),
            pltpu.VMEM((6 * rows, 2 * keys + 128), F32),
            pltpu.VMEM((6 * rows, 2 * keys + 128), BF16),
            pltpu.VMEM((6 * rows, 2 * keys + 128), BF16),
            pltpu.VMEM((6 * rows, 128), F32),
            pltpu.SemaphoreType.DMA((kv_width // 128, 3)),
        ],
        compiler_params=params(32),
        cost_estimate=pl.CostEstimate(
            flops=4 * 24 * rows * 2 * keys * HEAD,
            bytes_accessed=8 * keys * kv_width,
            transcendentals=24 * rows * 2 * keys,
        ),
    )(*operands, *map(stay, prompt), other_prompt[1])
    parts = exchange_chips(partial)
    sums = call(
        join_kernel,
        shaped((n_chips, local_rows, width)),
        parts,
        fresh,
        seq,
        stay(w_output),
        other_w_output,
        ins=[resident, resident, scalars(), anywhere, anywhere],
        scratch=[pltpu.VMEM(w_output.shape, BF16)] * 2 + [pltpu.SemaphoreType.DMA((2,))],
    )
    slots = n_req * capacity
    place, mix = call(
        functools.partial(route_kernel, capacity),
        (shaped((slots, local_rows)), shaped((local_rows, slots), F32)),
        sums,
        stay(routes[0]),
        stay(gate_weights[0]),
        ins=[anywhere],
    )
    sums_here = sums
    sums = exchange_chips(sums)
    hidden, buffer = call(
        dispatch_kernel,
        (shaped((local_rows, width), F32), shaped((n_req, capacity, width))),
        x,
        sums,
        stay(gain_moe),
        place,
        ins=[anywhere, resident, anywhere, resident],
        scratch=[
            pltpu.VMEM(x.shape, BF16),
            pltpu.VMEM((width,), F32),
            pltpu.SemaphoreType.DMA((2,)),
        ],
    )
    own, sums_here = lax.optimization_barrier((own, sums_here))
    even = [own] + [apart(own, k) for k in range(2, n_seq, 2)]
    buffer, *even = lax.optimization_barrier((buffer, *even))
    buffer = exchange(buffer, "req")
    back = call(
        expert_kernel,
        shaped(buffer.shape),
        buffer,
        stay(w_in),
        w_out,
        ins=[resident, anywhere, resident],
        scratch=[
            pltpu.VMEM(w_in.shape, BF16),
            pltpu.VMEM((slots, width), F32),
            pltpu.SemaphoreType.DMA((3,)),
        ],
    )
    odd = [other_own] + [apart(a, 1) for a in even[1:]]
    owns = [a for pair in zip(even, odd) for a in pair]
    back = exchange(back, "req")
    mixed = call(
        mix_kernel,
        shaped((here, steps, width)),
        hidden,
        mix,
        back,
        ins=[resident] * 3,
        scratch=[pltpu.VMEM((slots, width), F32)],
    )
    final_k, final_v = call(
        final_kernel,
        (shaped((tail + steps, here, kv_width)),) * 2,
        seq,
        parents[0],
        parts,
        *owns,
        ins=[scalars(), scalars()],
    )
    return (
        mixed[None],
        final_k.transpose(1, 0, 2)[None],
        final_v.transpose(1, 0, 2)[None],
    )


def solution(mesh):
    placed = (
        P("req", "seq", None, None),
        P("req", None, None),
        P("req", "seq"),
        P("req", "seq", None),
        P("req", "seq", None),
        P("req", "seq", None, None),
        P("req", "seq", None, None),
        P(),
        P(),
        P(None, "seq"),
        P(None, "seq"),
        P(None, "seq"),
        P("seq", None),
        P("req", None, None),
        P("req", None, None),
        P("req", "seq", None, None),
        P("req", "seq", None, None),
    )
    return jax.shard_map(
        local,
        mesh=mesh,
        in_specs=placed,
        out_specs=(P("req", "seq", None, None),) * 3,
        check_vma=False,
    )
```
